32 devices in a mesh: fsdp: 16 (over z, y, core), sp: 2 (over x).
Axes of the slice: x: 2, y: 2, z: 4, core: 2. Of those that a mesh axis runs over, the one named last changes fastest.
Arguments:
- latents: bfloat16 [32, 256, 768], P('fsdp', 'sp'), may hold values from -6 to 6
- condition: bfloat16 [32, 768], P('fsdp'), may hold values from -6 to 6
- cotangent: bfloat16 [32, 256, 768], P('fsdp', 'sp'), may hold values from -6 to 6
- w_ada: bfloat16 [768, 4608], P('fsdp'), may hold values from -0.21875 to 0.21875
- b_ada: bfloat16 [4608], P('fsdp'), may hold values from -3 to 3
- w_qkv: bfloat16 [768, 2304], P('fsdp'), may hold values from -0.21875 to 0.21875
- b_query: bfloat16 [768], P('fsdp'), may hold values from -3 to 3
- b_value: bfloat16 [768], P('fsdp'), may hold values from -3 to 3
- w_out: bfloat16 [768, 768], P('fsdp'), may hold values from -0.875 to 0.875
- b_out: bfloat16 [768], P('fsdp'), may hold values from -3 to 3
- w_up: bfloat16 [768, 3072], P('fsdp'), may hold values from -0.21875 to 0.21875
- b_up: bfloat16 [3072], P('fsdp'), may hold values from -3 to 3
- w_down: bfloat16 [3072, 768], P('fsdp'), may hold values from -0.109375 to 0.109375
- b_down: bfloat16 [768], P('fsdp'), may hold values from -3 to 3
Outputs:
- output: bfloat16 [32, 256, 768], P('fsdp', 'sp')
- grad_latents: float32 [32, 256, 768], P('fsdp', 'sp')
- grad_condition: float32 [32, 768], P('fsdp')
- grad_w_ada: float32 [768, 4608], P(('fsdp', 'sp'))
- grad_b_ada: float32 [4608], P(('fsdp', 'sp'))
- grad_w_qkv: float32 [768, 2304], P(('fsdp', 'sp'))
- grad_b_query: float32 [768], P(('fsdp', 'sp'))
- grad_b_value: float32 [768], P(('fsdp', 'sp'))
- grad_w_out: float32 [768, 768], P(('fsdp', 'sp'))
- grad_b_out: float32 [768], P(('fsdp', 'sp'))
- grad_w_up: float32 [768, 3072], P(('fsdp', 'sp'))
- grad_b_up: float32 [3072], P(('fsdp', 'sp'))
- grad_w_down: float32 [3072, 768], P(('fsdp', 'sp'))
- grad_b_down: float32 [768], P(('fsdp', 'sp'))
The draws below stay inside these ranges and needn't reach their ends.
All inputs are finite; a program needn't handle non-finite values.
Results may differ from the reference program's by a relative error of at most 0.015.
The reference program's roundings to bfloat16 on the way count: a program that leaves them out, or rounds other values in their place, can miss the bound.
Values may be sent and summed in bfloat16 or wider, within the bound.
A program may use at most 256 MiB of HBM per device.

```python
import math
import jax
import jax.numpy as jnp
from jax import lax

D = 768
H = 12
HD = 64
FF = 3072
S = 256
LATENTS = 32


def block_levels(stream_key, dims, cuts, smallest, high):
    level, own = 1.0, jax.random.fold_in(stream_key, 6)
    for position, shards_of in cuts:
        heights = jnp.exp(jax.random.uniform(jax.random.fold_in(own, position), (shards_of,), jnp.float32, smallest / len(cuts), high / len(cuts)))
        level = level * jnp.repeat(heights, dims[position] // shards_of).reshape([-1 if axis == position else 1 for axis in range(len(dims))])
    return level


def centred(stream_key, shape, spread, limit, shards=(), held_as=jnp.bfloat16):
    entries = spread * jax.random.normal(stream_key, shape, jnp.float32)
    if shards:
        entries = entries * block_levels(stream_key, shape, shards, -0.22, 0.18)
    return jnp.clip(entries, -limit, limit).astype(held_as)


def setup_inputs(seed: int = 0) -> dict:
    key_of = jax.random.split(jax.random.key(seed), 15)
    latents = centred(key_of[0], (LATENTS, S, D), 1.0, 6.0, ((0, 16), (1, 2)))
    condition = centred(key_of[1], (LATENTS, D), 1.0, 6.0, ((0, 16),))
    cotangent = centred(key_of[2], (LATENTS, S, D), 1.0, 6.0, ((0, 16), (1, 2)))
    w_ada = centred(key_of[3], (D, 6 * D), D ** -0.5, 0.21875, ((0, 16),))
    b_ada = centred(key_of[4], (6 * D,), 0.5, 3.0, ((0, 16),))
    w_qkv = centred(key_of[5], (D, 3 * D), D ** -0.5, 0.21875, ((0, 16),))
    b_query = centred(key_of[6], (D,), 0.5, 3.0, ((0, 16),))
    b_value = centred(key_of[7], (D,), 0.5, 3.0, ((0, 16),))
    w_out = centred(key_of[8], (D, D), (D // 16) ** -0.5, 0.875, ((0, 16),))
    b_out = centred(key_of[9], (D,), 0.5, 3.0, ((0, 16),))
    w_up = centred(key_of[10], (D, FF), D ** -0.5, 0.21875, ((0, 16),))
    b_up = centred(key_of[11], (FF,), 0.5, 3.0, ((0, 16),))
    w_down = centred(key_of[12], (FF, D), FF ** -0.5, 0.109375, ((0, 16),))
    b_down = centred(key_of[13], (D,), 0.5, 3.0, ((0, 16),))
    return dict(latents=latents, condition=condition, cotangent=cotangent, w_ada=w_ada, b_ada=b_ada, w_qkv=w_qkv, b_query=b_query, b_value=b_value, w_out=w_out, b_out=b_out, w_up=w_up, b_up=b_up, w_down=w_down, b_down=b_down)


eps = 1e-06

def normalize(values):
    centered = values - lax.optimization_barrier(jnp.mean(values, axis=-1, keepdims=True))
    inverse = lax.rsqrt(lax.optimization_barrier(jnp.mean(centered * centered, axis=-1, keepdims=True)) + eps)
    return (centered * inverse, inverse)

def norm_back(grad_in, normed, inverse):
    return inverse * (grad_in - lax.optimization_barrier(jnp.mean(grad_in, axis=-1, keepdims=True)) - normed * lax.optimization_barrier(jnp.mean(grad_in * normed, axis=-1, keepdims=True)))

def gelu_tanh(values):
    return jax.nn.gelu(values, approximate=True)

def silu_back(values, grad_out):
    return jax.vjp(jax.nn.silu, values)[1](grad_out)[0]

def gelu_back(values, grad_out):
    return jax.vjp(gelu_tanh, values)[1](grad_out)[0]

def group_pass(weights, group_data):
    w_ada, b_ada, w_qkv, b_query, b_value, w_out, b_out, w_up, b_up, w_down, b_down = weights
    latents, condition, cotangent = group_data
    batch_count = latents.shape[0]
    scale_factor = HD ** (-0.5)
    cond_float = condition.astype(jnp.float32)
    silu_cond = jax.nn.silu(cond_float)
    modulate = jnp.dot(silu_cond.astype(jnp.bfloat16), w_ada, preferred_element_type=jnp.float32) + b_ada.astype(jnp.float32)
    mod_parts = modulate.reshape(batch_count, 6, 1, D)
    shift_one, scale_one, gate_one = (mod_parts[:, 0], mod_parts[:, 1], mod_parts[:, 2])
    shift_two, scale_two, gate_two = (mod_parts[:, 3], mod_parts[:, 4], mod_parts[:, 5])
    inputs = latents.astype(jnp.float32)
    normed_one, inverse_one = normalize(inputs)
    attn_in = (normed_one * (1.0 + scale_one) + shift_one).astype(jnp.bfloat16)
    attn_flat = attn_in.reshape(-1, D)
    qkv_bias = jnp.concatenate([b_query, jnp.zeros_like(b_query), b_value]).astype(jnp.float32)
    projected = (jnp.dot(attn_flat, w_qkv, preferred_element_type=jnp.float32) + qkv_bias).astype(jnp.bfloat16)
    projected = projected.reshape(batch_count, S, 3, H, HD)
    queries = projected[:, :, 0].astype(jnp.float32)
    key_heads = projected[:, :, 1].astype(jnp.float32)
    value_heads = projected[:, :, 2].astype(jnp.float32)
    scores = jnp.einsum('bqhd,bkhd->bhqk', queries, key_heads) * scale_factor
    log_total = jnp.log(lax.optimization_barrier(jnp.sum(jnp.exp(scores), axis=-1, keepdims=True)))
    soft_float = jnp.exp(scores - log_total)
    soft_half = soft_float.astype(jnp.bfloat16)
    mixed = jnp.einsum('bhqk,bkhd->bqhd', soft_half.astype(jnp.float32), value_heads).astype(jnp.bfloat16)
    mixed_flat = mixed.reshape(-1, D)
    attn_proj = (jnp.dot(mixed_flat, w_out, preferred_element_type=jnp.float32) + b_out.astype(jnp.float32)).reshape(batch_count, S, D)
    residual = inputs + gate_one * attn_proj
    normed_two, inverse_two = normalize(residual)
    mlp_in = (normed_two * (1.0 + scale_two) + shift_two).astype(jnp.bfloat16).reshape(-1, D)
    up_value = jnp.dot(mlp_in, w_up, preferred_element_type=jnp.float32) + b_up.astype(jnp.float32)
    activated = gelu_tanh(up_value).astype(jnp.bfloat16)
    down_value = (jnp.dot(activated, w_down, preferred_element_type=jnp.float32) + b_down.astype(jnp.float32)).reshape(batch_count, S, D)
    output = (residual + gate_two * down_value).astype(jnp.bfloat16)
    grad_out = cotangent.astype(jnp.float32)
    grad_gate_two = lax.optimization_barrier(jnp.sum(grad_out * down_value, axis=1))
    grad_down = (grad_out * gate_two).astype(jnp.bfloat16).reshape(-1, D)
    gw_down = jnp.dot(activated.T, grad_down, preferred_element_type=jnp.float32)
    gb_down = lax.optimization_barrier(jnp.sum(grad_down.astype(jnp.float32), axis=0))
    grad_act = jnp.dot(grad_down, w_down.T, preferred_element_type=jnp.float32)
    grad_up = gelu_back(up_value, grad_act).astype(jnp.bfloat16)
    gw_up = jnp.dot(mlp_in.T, grad_up, preferred_element_type=jnp.float32)
    gb_up = lax.optimization_barrier(jnp.sum(grad_up.astype(jnp.float32), axis=0))
    grad_mlp = jnp.dot(grad_up, w_up.T, preferred_element_type=jnp.float32).reshape(batch_count, S, D)
    grad_scale_two = lax.optimization_barrier(jnp.sum(grad_mlp * normed_two, axis=1))
    grad_shift_two = lax.optimization_barrier(jnp.sum(grad_mlp, axis=1))
    grad_resid = grad_out + norm_back(grad_mlp * (1.0 + scale_two), normed_two, inverse_two)
    grad_gate_one = lax.optimization_barrier(jnp.sum(grad_resid * attn_proj, axis=1))
    grad_proj = (grad_resid * gate_one).astype(jnp.bfloat16).reshape(-1, D)
    gw_out = jnp.dot(mixed_flat.T, grad_proj, preferred_element_type=jnp.float32)
    gb_out = lax.optimization_barrier(jnp.sum(grad_proj.astype(jnp.float32), axis=0))
    grad_mixed = jnp.dot(grad_proj, w_out.T, preferred_element_type=jnp.float32).astype(jnp.bfloat16)
    grad_mixed = grad_mixed.reshape(batch_count, S, H, HD).astype(jnp.float32)
    grad_soft = jnp.einsum('bqhd,bkhd->bhqk', grad_mixed, value_heads)
    delta_sum = lax.optimization_barrier(jnp.sum(soft_float * grad_soft, axis=-1, keepdims=True))
    grad_scores = (soft_float * (grad_soft - delta_sum)).astype(jnp.bfloat16).astype(jnp.float32)
    grad_queries = (jnp.einsum('bhqk,bkhd->bqhd', grad_scores, key_heads) * scale_factor).astype(jnp.bfloat16)
    grad_keys = (jnp.einsum('bhqk,bqhd->bkhd', grad_scores, queries) * scale_factor).astype(jnp.bfloat16)
    grad_values = jnp.einsum('bhqk,bqhd->bkhd', soft_half.astype(jnp.float32), grad_mixed).astype(jnp.bfloat16)
    grad_qkv = jnp.stack([grad_queries, grad_keys, grad_values], axis=2).reshape(-1, 3 * D)
    gw_qkv = jnp.dot(attn_flat.T, grad_qkv, preferred_element_type=jnp.float32)
    gb_query = lax.optimization_barrier(jnp.sum(grad_queries.astype(jnp.float32), axis=(0, 1))).reshape(D)
    gb_value = lax.optimization_barrier(jnp.sum(grad_values.astype(jnp.float32), axis=(0, 1))).reshape(D)
    grad_attn_in = jnp.dot(grad_qkv, w_qkv.T, preferred_element_type=jnp.float32).reshape(batch_count, S, D)
    grad_scale_one = lax.optimization_barrier(jnp.sum(grad_attn_in * normed_one, axis=1))
    grad_shift_one = lax.optimization_barrier(jnp.sum(grad_attn_in, axis=1))
    grad_latents = grad_resid + norm_back(grad_attn_in * (1.0 + scale_one), normed_one, inverse_one)
    grad_mod = jnp.concatenate([grad_shift_one, grad_scale_one, grad_gate_one, grad_shift_two, grad_scale_two, grad_gate_two], axis=1)
    gw_ada = jnp.dot(silu_cond.T, grad_mod, precision=lax.Precision.HIGHEST)
    gb_ada = lax.optimization_barrier(jnp.sum(grad_mod, axis=0))
    grad_silu = jnp.dot(grad_mod.astype(jnp.bfloat16), w_ada.T, preferred_element_type=jnp.float32)
    grad_condition = silu_back(cond_float, grad_silu)
    grads = (gw_ada, gb_ada, gw_qkv, gb_query, gb_value, gw_out, gb_out, gw_up, gb_up, gw_down, gb_down)
    return ((output, grad_latents, grad_condition), grads)

def reference(latents, condition, cotangent, w_ada, b_ada, w_qkv, b_query, b_value, w_out, b_out, w_up, b_up, w_down, b_down):
    weights = (w_ada, b_ada, w_qkv, b_query, b_value, w_out, b_out, w_up, b_up, w_down, b_down)
    latent_total = latents.shape[0]
    group_size = math.gcd(latent_total, 16)
    group_count = latent_total // group_size
    stacked = (latents.reshape(group_count, group_size, S, D), condition.reshape(group_count, group_size, D), cotangent.reshape(group_count, group_size, S, D))

    def scan_step(running, group_data):
        outcome, grads = group_pass(weights, group_data)
        return (jax.tree.map(jnp.add, running, grads), outcome)
    zero_grads = tuple((jnp.zeros(weight.shape, jnp.float32) for weight in weights))
    grads, outcome = lax.scan(scan_step, zero_grads, stacked)
    output = outcome[0].reshape(latent_total, S, D)
    grad_latents = outcome[1].reshape(latent_total, S, D)
    grad_condition = outcome[2].reshape(latent_total, D)
    return (output, grad_latents, grad_condition, grads[0], grads[1], grads[2], grads[3], grads[4], grads[5], grads[6], grads[7], grads[8], grads[9], grads[10])
```

```python
import functools

import jax
import jax.numpy as jnp
from jax import lax
from jax.experimental import pallas as pl
from jax.experimental.pallas import tpu as pltpu
from jax.sharding import PartitionSpec as P

D = 768
H = 12
HD = 64


eps = 1e-06


def normalize(values):
    centered = values - jnp.mean(values, axis=-1, keepdims=True)
    inverse = lax.rsqrt(jnp.mean(centered * centered, axis=-1, keepdims=True) + eps)
    return (centered * inverse, inverse)


def norm_back(grad_in, normed, inverse):
    return inverse * (
        grad_in
        - jnp.mean(grad_in, axis=-1, keepdims=True)
        - normed * jnp.mean(grad_in * normed, axis=-1, keepdims=True)
    )


def gelu_tanh(values):
    return jax.nn.gelu(values, approximate=True)


def silu_back(values, grad_out):
    return jax.vjp(jax.nn.silu, values)[1](grad_out)[0]


def gelu_back(values, grad_out):
    return jax.vjp(gelu_tanh, values)[1](grad_out)[0]


LANES = 2048


def body_general(
    latents,
    condition,
    cotangent,
    w_ada,
    b_ada,
    w_qkv,
    b_query,
    b_value,
    w_out,
    b_out,
    w_up,
    b_up,
    w_down,
    b_down,
):
    f32 = jnp.float32
    bf16 = jnp.bfloat16
    fsdp_count = lax.axis_size("fsdp")
    sp_count = lax.axis_size("sp")
    owners = fsdp_count * sp_count
    fsdp_index = lax.axis_index("fsdp")
    sp_index = lax.axis_index("sp")
    owner_index = fsdp_index * sp_count + sp_index
    pair_latents = latents.shape[0]
    own_latents = pair_latents // sp_count
    latent_total = pair_latents * fsdp_count
    tokens_all = latents.shape[1] * sp_count
    scale_factor = HD ** (-0.5)

    small = [condition.reshape(-1), b_ada, b_query, b_value, b_out, b_up, b_down]
    width = sum(part.size for part in small)
    padded = -(-width // LANES) * LANES
    small.append(jnp.zeros((padded - width,), bf16))
    small_all = lax.all_gather(
        jnp.concatenate(small).reshape(1, padded // 128, 128), "fsdp", axis=0, tiled=True
    ).reshape(fsdp_count, padded)
    pieces = []
    start = 0
    for part in small[:-1]:
        pieces.append(small_all[:, start : start + part.size].reshape(-1))
        start = start + part.size
    cond_all, ada_bias, query_bias, value_bias, out_bias, up_bias, down_bias = pieces
    cond_all = cond_all.reshape(latent_total, D).astype(f32)
    silu_all = jax.nn.silu(cond_all)

    inputs = lax.all_to_all(latents, "sp", split_axis=0, concat_axis=1, tiled=True).astype(f32)
    grad_out = lax.all_to_all(cotangent, "sp", split_axis=0, concat_axis=1, tiled=True).astype(f32)

    ada_rows = w_ada.shape[0]
    silu_mine = lax.dynamic_index_in_dim(
        silu_all.astype(bf16).reshape(fsdp_count, sp_count, own_latents, D), sp_index, 1, False
    )
    silu_mine = lax.dynamic_index_in_dim(
        silu_mine.reshape(fsdp_count * own_latents, fsdp_count, ada_rows), fsdp_index, 1, False
    )
    mod_part = jnp.dot(silu_mine, w_ada, preferred_element_type=f32)
    mod_part = lax.all_to_all(
        mod_part.reshape(fsdp_count, own_latents * 6 * D), "fsdp", split_axis=0, concat_axis=0, tiled=True
    )
    modulate = jnp.sum(mod_part, axis=0).reshape(own_latents, 6 * D) + ada_bias.astype(f32)
    mod_parts = modulate.reshape(own_latents, 6, 1, D)
    shift_one, scale_one, gate_one = (mod_parts[:, 0], mod_parts[:, 1], mod_parts[:, 2])
    shift_two, scale_two, gate_two = (mod_parts[:, 3], mod_parts[:, 4], mod_parts[:, 5])

    qkv_full = lax.all_gather(w_qkv, "fsdp", axis=0, tiled=True)
    out_full = lax.all_gather(w_out, "fsdp", axis=0, tiled=True)
    up_full = lax.all_gather(w_up, "fsdp", axis=0, tiled=True)
    down_full = lax.all_gather(w_down, "fsdp", axis=0, tiled=True)

    normed_one, inverse_one = normalize(inputs)
    attn_in = (normed_one * (1.0 + scale_one) + shift_one).astype(bf16)
    qkv_bias = jnp.concatenate([query_bias, jnp.zeros_like(query_bias), value_bias]).astype(f32)
    projected = (
        jnp.einsum("btd,de->bte", attn_in, qkv_full, preferred_element_type=f32) + qkv_bias
    ).astype(bf16)
    heads = projected.reshape(own_latents, tokens_all, 3, H, HD).transpose(2, 0, 3, 1, 4)
    queries, key_heads, value_heads = heads[0], heads[1], heads[2]
    scores = (
        jnp.einsum("bhqd,bhkd->bhqk", queries, key_heads, preferred_element_type=f32) * scale_factor
    )
    log_total = jnp.log(jnp.sum(jnp.exp(scores), axis=-1, keepdims=True))
    soft_float = jnp.exp(scores - log_total)
    soft_half = soft_float.astype(bf16)
    mixed = jnp.einsum("bhqk,bhkd->bhqd", soft_half, value_heads, preferred_element_type=f32).astype(
        bf16
    )
    mixed_tokens = mixed.transpose(0, 2, 1, 3).reshape(own_latents, tokens_all, D)
    attn_proj = jnp.einsum(
        "btd,de->bte", mixed_tokens, out_full, preferred_element_type=f32
    ) + out_bias.astype(f32)
    residual = inputs + gate_one * attn_proj
    normed_two, inverse_two = normalize(residual)
    mlp_in = (normed_two * (1.0 + scale_two) + shift_two).astype(bf16)
    up_value = jnp.einsum(
        "btd,df->btf", mlp_in, up_full, preferred_element_type=f32
    ) + up_bias.astype(f32)
    activated = gelu_tanh(up_value).astype(bf16)
    down_value = jnp.einsum(
        "btf,fd->btd", activated, down_full, preferred_element_type=f32
    ) + down_bias.astype(f32)
    output = (residual + gate_two * down_value).astype(bf16)
    output = lax.all_to_all(output, "sp", split_axis=1, concat_axis=0, tiled=True)

    grad_gate_two = jnp.sum(grad_out * down_value, axis=1)
    grad_down = (grad_out * gate_two).astype(bf16)
    gw_down = jnp.einsum("btf,btd->fd", activated, grad_down, preferred_element_type=f32)
    gb_down = jnp.sum(grad_down.astype(f32), axis=(0, 1))
    grad_act = jnp.einsum("btd,fd->btf", grad_down, down_full, preferred_element_type=f32)
    grad_up = gelu_back(up_value, grad_act).astype(bf16)
    gw_up = jnp.einsum("btd,btf->df", mlp_in, grad_up, preferred_element_type=f32)
    gb_up = jnp.sum(grad_up.astype(f32), axis=(0, 1))
    grad_mlp = jnp.einsum("btf,df->btd", grad_up, up_full, preferred_element_type=f32)
    grad_scale_two = jnp.sum(grad_mlp * normed_two, axis=1)
    grad_shift_two = jnp.sum(grad_mlp, axis=1)
    grad_resid = grad_out + norm_back(grad_mlp * (1.0 + scale_two), normed_two, inverse_two)
    grad_gate_one = jnp.sum(grad_resid * attn_proj, axis=1)
    grad_proj = (grad_resid * gate_one).astype(bf16)
    gw_out = jnp.einsum("btd,bte->de", mixed_tokens, grad_proj, preferred_element_type=f32)
    gb_out = jnp.sum(grad_proj.astype(f32), axis=(0, 1))
    grad_mixed = jnp.einsum("bte,de->btd", grad_proj, out_full, preferred_element_type=f32).astype(
        bf16
    )
    grad_heads = grad_mixed.reshape(own_latents, tokens_all, H, HD).transpose(0, 2, 1, 3)
    grad_soft = jnp.einsum("bhqd,bhkd->bhqk", grad_heads, value_heads, preferred_element_type=f32)
    delta_sum = jnp.sum(soft_float * grad_soft, axis=-1, keepdims=True)
    grad_scores = (soft_float * (grad_soft - delta_sum)).astype(bf16)
    grad_queries = (
        jnp.einsum("bhqk,bhkd->bhqd", grad_scores, key_heads, preferred_element_type=f32)
        * scale_factor
    ).astype(bf16)
    grad_keys = (
        jnp.einsum("bhqk,bhqd->bhkd", grad_scores, queries, preferred_element_type=f32)
        * scale_factor
    ).astype(bf16)
    grad_values = jnp.einsum(
        "bhqk,bhqd->bhkd", soft_half, grad_heads, preferred_element_type=f32
    ).astype(bf16)
    grad_tokens = (
        jnp.stack([grad_queries, grad_keys, grad_values], axis=0)
        .transpose(1, 3, 0, 2, 4)
        .reshape(own_latents, tokens_all, 3 * D)
    )
    gw_qkv = jnp.einsum("btd,bte->de", attn_in, grad_tokens, preferred_element_type=f32)
    grad_tok_float = grad_tokens.astype(f32)
    gb_query = jnp.sum(grad_tok_float[:, :, :D], axis=(0, 1))
    gb_value = jnp.sum(grad_tok_float[:, :, 2 * D :], axis=(0, 1))
    grad_attn_in = jnp.einsum("bte,de->btd", grad_tokens, qkv_full, preferred_element_type=f32)
    grad_scale_one = jnp.sum(grad_attn_in * normed_one, axis=1)
    grad_shift_one = jnp.sum(grad_attn_in, axis=1)
    grad_latents = grad_resid + norm_back(grad_attn_in * (1.0 + scale_one), normed_one, inverse_one)
    grad_latents = lax.all_to_all(grad_latents, "sp", split_axis=1, concat_axis=0, tiled=True)

    grad_mod = jnp.concatenate(
        [
            grad_shift_one,
            grad_scale_one,
            grad_gate_one,
            grad_shift_two,
            grad_scale_two,
            grad_gate_two,
        ],
        axis=1,
    )
    grad_mod = lax.all_to_all(
        jnp.broadcast_to(grad_mod[None], (owners, own_latents, 6 * D)),
        ("fsdp", "sp"),
        split_axis=0,
        concat_axis=0,
        tiled=True,
    ).reshape(latent_total, 6 * D)

    rows = D // owners
    biases = (gb_query, gb_value, gb_out, gb_up, gb_down)
    bias_rows = jnp.concatenate([part.reshape(owners, -1) for part in biases], axis=1)
    bias_width = bias_rows.shape[1]
    bias_lanes = -(-bias_width // (rows * 128)) * 128
    bias_rows = jnp.pad(bias_rows, ((0, 0), (0, rows * bias_lanes - bias_width)))
    stack = down_full.shape[0] // D
    gw_down = (
        gw_down.astype(bf16)
        .reshape(owners, stack, rows, D)
        .transpose(0, 2, 1, 3)
        .reshape(D, stack * D)
    )
    packed = jnp.concatenate(
        [
            gw_down,
            gw_up.astype(bf16),
            gw_qkv.astype(bf16),
            gw_out.astype(bf16),
            bias_rows.astype(bf16).reshape(D, bias_lanes),
        ],
        axis=1,
    )
    owned = lax.psum_scatter(packed, ("fsdp", "sp"), scatter_dimension=0, tiled=True).astype(f32)
    own_weights = []
    start = 0
    for width in (stack * D, up_full.shape[1], 3 * D, D, bias_lanes):
        own_weights.append(owned[:, start : start + width])
        start = start + width
    own_down, own_up, own_qkv, own_out, bias_sums = own_weights
    own_down = own_down.reshape(rows, stack, D).transpose(1, 0, 2).reshape(stack * rows, D)
    bias_sums = bias_sums.reshape(-1)
    own_bias = []
    start = 0
    for part in biases:
        width = part.size // owners
        own_bias.append(bias_sums[start : start + width])
        start = start + width
    own_gb_query, own_gb_value, own_gb_out, own_gb_up, own_gb_down = own_bias
    silu_rows = lax.dynamic_index_in_dim(
        silu_all.reshape(latent_total, owners, D // owners), owner_index, 1, False
    )
    own_ada = jnp.dot(silu_rows.T, grad_mod, precision=lax.Precision.HIGHEST)
    own_gb_ada = lax.dynamic_index_in_dim(
        jnp.sum(grad_mod, axis=0).reshape(owners, -1), owner_index, 0, False
    )
    grad_silu = jnp.dot(grad_mod.astype(bf16), w_ada.T, preferred_element_type=f32)
    grad_silu = lax.all_to_all(
        grad_silu.reshape(fsdp_count, pair_latents * ada_rows),
        "fsdp",
        split_axis=0,
        concat_axis=0,
        tiled=True,
    )
    grad_silu = (
        grad_silu.reshape(fsdp_count, pair_latents, ada_rows)
        .transpose(1, 0, 2)
        .reshape(pair_latents, D)
    )
    grad_condition = silu_back(condition.astype(f32), grad_silu)
    return (
        output,
        grad_latents,
        grad_condition,
        own_ada,
        own_gb_ada,
        own_qkv,
        own_gb_query,
        own_gb_value,
        own_out,
        own_gb_out,
        own_up,
        own_gb_up,
        own_down,
        own_gb_down,
    )


MESH = pl.DeviceIdType.MESH


class Plan:
    def __init__(self, rows, cols):
        self.rows, self.cols = rows, cols
        self.by_rows = rows % 64 == 0
        n = (rows // 32) if self.by_rows else (cols // 256)
        unit = 16 if self.by_rows else 128
        big = -(-2 * n // 3)
        self.half = n * unit
        self.big = big * unit
        self.unit = unit
    def at(self, ref, row, h=None, q=None):
        rows, cols, unit = self.rows, self.cols, self.unit
        if h is None:
            return ref.at[pl.ds(pl.multiple_of(row, 16), rows), :]
        start = h * self.half + (self.big if q == 1 else 0)
        size = self.half if q is None else (self.big if q == 0 else self.half - self.big)
        if self.by_rows:
            return ref.at[pl.ds(pl.multiple_of(row + start, 16), size), :]
        return ref.at[pl.ds(pl.multiple_of(row, 16), rows), pl.ds(pl.multiple_of(start, 128), size)]

def gather_kernel(F, plans, *refs):
    n = len(plans)
    f32, bf16 = jnp.float32, jnp.bfloat16
    ins, (cond, bias, lat, cot, wada) = refs[:n], refs[n:n + 5]
    outs, (cond_all, bias_all, mod, lat_all, cot_all) = refs[n + 5:2 * n + 5], refs[2 * n + 5:2 * n + 10]
    part, parts, zs, zr, xs, xr, ys, yr, xds, xdr, yds, ydr, ss, sr, loc, es, er, ps, pr = refs[2 * n + 10:]
    f = lax.axis_index("fsdp"); x = lax.axis_index("sp")
    c = f % 2; y = (f // 2) % 2; z = f // 4; Z = F // 4
    def dev(x_, y_, z_, c_):
        return ((z_ * 2 + y_) * 2 + c_, x_)
    xn, yn, sib = dev(1 - x, y, z, c), dev(x, 1 - y, z, c), dev(x, y, z, 1 - c)
    zu, zd = dev(x, y, z + 1, c), dev(x, y, z - 1, c)
    def peer(k):
        return (lax.rem(f + k, F), x)
    bar = pltpu.get_barrier_semaphore()
    pl.semaphore_signal(bar, inc=1, device_id=xn, device_id_type=MESH)
    for k in range(1, F):
        pl.semaphore_signal(bar, inc=1, device_id=peer(k), device_id_type=MESH)
    pl.semaphore_wait(bar, F)

    sends = []
    def send(ok, build):
        if ok is None:
            build().start()
        else:
            pl.when(ok)(lambda: build().start())
        sends.append((ok, build))
    def rc(src, dst, s, r, d):
        return pltpu.make_async_remote_copy(src_ref=src, dst_ref=dst, send_sem=s, recv_sem=r, device_id=d, device_id_type=MESH)

    def base(m, y_, z_, c_=c):
        return ((z_ * 2 + y_) * 2 + c_) * plans[m].rows
    def piece(m, y_, z_, h=None, q=None, c_=None):
        return plans[m].at(outs[m], base(m, y_, z_, c if c_ is None else c_), h, q)
    def mine(m, h=None, q=None):
        return plans[m].at(ins[m], 0, h, q)
    def to_sib(m, ok, kind, y_, z_, h=None, q=None, own=False):
        send(ok, lambda: rc(mine(m, h, q) if own else piece(m, y_, z_, h, q), piece(m, y_, z_, h, q),
                              ss.at[m, kind, z_], sr.at[m, kind, z_], sib))
    def arrived(m, ok, sem_s, sem_r, *where, c_=None):
        def go():
            p = piece(m, *where, c_=c_)
            rc(p, p, sem_s, sem_r, xn).wait_recv()
        if ok is None: go()
        else: pl.when(ok)(go)

    def start_own(m):
        send(None, lambda: rc(mine(m, x), piece(m, y, z, x), ys.at[m, z], yr.at[m, z], yn))
        send(z + 1 < Z, lambda: rc(mine(m, x), piece(m, y, z, x), zs.at[m, 0, z], zr.at[m, z], zu))
        send(z > 0, lambda: rc(mine(m, x), piece(m, y, z, x), zs.at[m, 1, z], zr.at[m, z], zd))
        send(None, lambda: rc(mine(m, 1 - x, 1), piece(m, y, z, 1 - x, 1), yds.at[m, z], ydr.at[m, z], yn))
        to_sib(m, None, 0, y, z, own=True)
        pltpu.make_async_copy(mine(m), piece(m, y, z), loc.at[m]).start()

    def z_round(m, d):
        for sign in (-1, 1):
            o = z + sign * d
            ok = (o >= 0) if sign < 0 else (o < Z)
            arrived(m, ok, zs.at[m, 0, o], zr.at[m, o], y, o, x)
            if sign < 0:
                send(ok & (z + 1 < Z), lambda o=o: rc(piece(m, y, o, x), piece(m, y, o, x), zs.at[m, 0, o], zr.at[m, o], zu))
            else:
                send(ok & (z > 0), lambda o=o: rc(piece(m, y, o, x), piece(m, y, o, x), zs.at[m, 1, o], zr.at[m, o], zd))
            send(ok, lambda o=o: rc(piece(m, y, o, x), piece(m, y, o, x), xs.at[m, o], xr.at[m, o], xn))
            send(ok, lambda o=o: rc(piece(m, y, o, x), piece(m, y, o, x), ys.at[m, o], yr.at[m, o], yn))
            to_sib(m, ok, 0, y, o, x)

    def xy_round(m, d):
        for sign in ((-1, 1) if d else (0,)):
            o = z + sign * d
            ok = None if d == 0 else ((o >= 0) if sign < 0 else (o < Z))
            arrived(m, ok, ys.at[m, o], yr.at[m, o], 1 - y, o, x)
            send(ok, lambda o=o: rc(piece(m, 1 - y, o, x, 0), piece(m, 1 - y, o, x, 0), xds.at[m, o], xdr.at[m, o], xn))
            to_sib(m, ok, 2, 1 - y, o, x)
            if d:
                arrived(m, ok, xs.at[m, o], xr.at[m, o], y, o, 1 - x)
                send(ok, lambda o=o: rc(piece(m, y, o, 1 - x, 1), piece(m, y, o, 1 - x, 1), yds.at[m, o], ydr.at[m, o], yn))
                to_sib(m, ok, 1, y, o, 1 - x)

    def last_round(m, d):
        for sign in ((-1, 1) if d else (0,)):
            o = z + sign * d
            ok = None if d == 0 else ((o >= 0) if sign < 0 else (o < Z))
            arrived(m, ok, xds.at[m, o], xdr.at[m, o], 1 - y, o, 1 - x, 0)
            to_sib(m, ok, 3, 1 - y, o, 1 - x, 0)
            arrived(m, ok, yds.at[m, o], ydr.at[m, o], 1 - y, o, 1 - x, 1)
            to_sib(m, ok, 4, 1 - y, o, 1 - x, 1)

    def finish(m):
        pltpu.make_async_copy(mine(m), piece(m, y, z), loc.at[m]).wait()
        b = 1 - c
        arrived(m, None, ss.at[m, 0, z], sr.at[m, 0, z], y, z, c_=b)
        for d in range(Z):
            for sign in ((-1, 1) if d else (0,)):
                o = z + sign * d
                ok = None if d == 0 else ((o >= 0) if sign < 0 else (o < Z))
                if d:
                    arrived(m, ok, ss.at[m, 0, o], sr.at[m, 0, o], y, o, x, c_=b)
                    arrived(m, ok, ss.at[m, 1, o], sr.at[m, 1, o], y, o, 1 - x, c_=b)
                arrived(m, ok, ss.at[m, 2, o], sr.at[m, 2, o], 1 - y, o, x, c_=b)
                arrived(m, ok, ss.at[m, 3, o], sr.at[m, 3, o], 1 - y, o, 1 - x, 0, c_=b)
                arrived(m, ok, ss.at[m, 4, o], sr.at[m, 4, o], 1 - y, o, 1 - x, 1, c_=b)

    rows = plans[0].rows
    tokens = lat.shape[1]
    for k in range(1, F):
        to = peer(k)
        rc(cond.at[to[0]], cond_all.at[f], es.at[0, k], er.at[0, k], to).start()
        rc(bias, bias_all.at[f], es.at[1, k], er.at[1, k], to).start()
    def swap(i, a, b):
        return rc(a.at[1 - x], b.at[pl.ds(pl.multiple_of(x * tokens, 128), tokens), :], es.at[2, i], er.at[2, i], xn)
    def keep(i, a, b):
        return pltpu.make_async_copy(a.at[x], b.at[pl.ds(pl.multiple_of(x * tokens, 128), tokens), :], loc.at[n + i])
    for i, (a, b) in enumerate(((lat, lat_all), (cot, cot_all))):
        swap(i, a, b).start()
        keep(i, a, b).start()
    start_own(0)
    cond_all[f] = cond[f]
    bias_all[f] = bias[...]
    for m in range(1, n):
        start_own(m)
    for k in range(1, F):
        rc(cond.at[0], cond_all.at[lax.rem(f + F - k, F)], es.at[0, k], er.at[0, k], xn).wait_recv()
    picked = jnp.where(x == 0, cond_all[:, 0, :], cond_all[:, 1, :])[:, :rows]
    picked = (picked / (1.0 + jnp.exp(-picked))).astype(bf16)
    made = jnp.dot(picked, wada[...], preferred_element_type=f32)
    for i in range(F):
        part[i] = made[i : i + 1, :]
    for k in range(1, F):
        to = peer(k)
        rc(part.at[to[0]], parts.at[f], ps.at[k], pr.at[k], to).start()
    parts[f] = part[f]
    for d in range(Z + 2):
        for m in range(n):
            if 0 < d < Z: z_round(m, d)
            if 0 < d <= Z: xy_round(m, d - 1)
            if d > 1: last_round(m, d - 2)
        if d == 1:
            for k in range(1, F):
                rc(part.at[0], parts.at[lax.rem(f + F - k, F)], ps.at[k], pr.at[k], xn).wait_recv()
            mod[...] = jnp.sum(parts[...], axis=0)
    for m in range(n): finish(m)
    for k in range(1, F):
        to = peer(k)
        rc(bias, bias_all.at[lax.rem(f + F - k, F)], es.at[1, k], er.at[1, k], xn).wait_recv()
        rc(cond.at[to[0]], cond_all.at[f], es.at[0, k], er.at[0, k], to).wait_send()
        rc(bias, bias_all.at[f], es.at[1, k], er.at[1, k], to).wait_send()
        rc(part.at[to[0]], parts.at[f], ps.at[k], pr.at[k], to).wait_send()
    for i, (a, b) in enumerate(((lat, lat_all), (cot, cot_all))):
        keep(i, a, b).wait()
        swap(i, a, b).wait_send()
        got = b.at[pl.ds(pl.multiple_of((1 - x) * tokens, 128), tokens), :]
        rc(got, got, es.at[2, i], er.at[2, i], xn).wait_recv()
    for cond_, build in sends:
        if cond_ is None: build().wait_send()
        else: pl.when(cond_)(lambda build=build: build().wait_send())


def gather(shards, cond, bias, lat, cot, wada, F):
    plans = [Plan(*s.shape) for s in shards]
    n, Z = len(shards), F // 4
    D = pltpu.SemaphoreType.DMA
    f32 = jnp.float32
    hbm, vm = pl.BlockSpec(memory_space=pl.ANY), pl.BlockSpec(memory_space=pltpu.VMEM)
    width = wada.shape[1]
    whole = jax.ShapeDtypeStruct((lat.shape[0] * lat.shape[1], lat.shape[2]), lat.dtype)
    return pl.pallas_call(
        functools.partial(gather_kernel, F, plans),
        out_shape=[jax.ShapeDtypeStruct((s.shape[0] * F, s.shape[1]), s.dtype) for s in shards]
        + [
            jax.ShapeDtypeStruct(cond.shape, f32),
            jax.ShapeDtypeStruct((F, *bias.shape), f32),
            jax.ShapeDtypeStruct((1, width), f32),
            whole,
            whole,
        ],
        in_specs=[hbm] * n + [vm, vm, hbm, hbm, vm],
        out_specs=[hbm] * n + [vm, vm, vm, hbm, hbm],
        scratch_shapes=[pltpu.VMEM((F, 1, width), f32)] * 2
        + [D((n, 2, Z)), D((n, Z))]
        + [D((n, Z))] * 8
        + [D((n, 5, Z))] * 2
        + [D((n + 2,)), D((3, F)), D((3, F)), D((F,)), D((F,))],
        compiler_params=pltpu.CompilerParams(
            collective_id=0, has_side_effects=True, vmem_limit_bytes=32 * 2**20
        ),
        name="gather_weights",
    )(*shards, cond, bias, lat, cot, wada)


def chunks_of(width, count):
    tiles = width // 128
    edges = [128 * (tiles * i // count) for i in range(count + 1)]
    return [(a, b - a) for a, b in zip(edges[:-1], edges[1:])]

def scatter_kernel(
    F, cuts, g, outp, glat, gmod, wada, silu_t, out, outp_own, glat_own, ada, bada, gcond,
    r0, r1, r2, up, dn, gm, cpart, s0, q0, s1, q1, s2, q2, s3, q3, gs, gr, ks, kr, es, er, loc
):
    f32, bf16 = jnp.float32, jnp.bfloat16
    f = lax.axis_index("fsdp"); x = lax.axis_index("sp")
    c = f % 2; y = (f // 2) % 2; z = f // 4; Z = F // 4; Zh = Z // 2
    def dev(x_, y_, z_, c_):
        return ((z_ * 2 + y_) * 2 + c_, x_)
    xn, yn, sib = dev(1 - x, y, z, c), dev(x, 1 - y, z, c), dev(x, y, z, 1 - c)
    zu, zd = dev(x, y, z + 1, c), dev(x, y, z - 1, c)
    owner = f * 2 + x
    def other(k):
        o = lax.rem(owner + k, 2 * F)
        return (o // 2, o % 2)
    def peer(k):
        return (lax.rem(f + k, F), x)
    bar = pltpu.get_barrier_semaphore()
    for k in range(1, 2 * F):
        pl.semaphore_signal(bar, inc=1, device_id=other(k), device_id_type=MESH)
    pl.semaphore_wait(bar, 2 * F - 1)

    def rc(src, dst, s, r, d):
        return pltpu.make_async_remote_copy(src_ref=src, dst_ref=dst, send_sem=s, recv_sem=r, device_id=d, device_id_type=MESH)
    def col(k):
        return pl.ds(*cuts[k])
    def c0(k):
        return rc(g.at[:, :, :, 1 - c, :, :, col(k)], r0.at[:, :, :, :, :, col(k)], s0.at[k], q0.at[k], sib)
    def c1(k, p):
        if p == 0:
            return rc(r0.at[:, 0, :, 1 - x, :, col(k)], r1.at[:, 0, :, :, col(k)], s1.at[k, 0], q1.at[k, 0], xn)
        return rc(r0.at[:, 1, 1 - y, :, :, col(k)], r1.at[:, 1, :, :, col(k)], s1.at[k, 1], q1.at[k, 1], yn)
    def c2(k, p):
        if p == 0:
            return rc(r1.at[:, 0, 1 - y, :, col(k)], r2.at[:, 0, :, col(k)], s2.at[k, 0], q2.at[k, 0], yn)
        return rc(r1.at[:, 1, 1 - x, :, col(k)], r2.at[:, 1, :, col(k)], s2.at[k, 1], q2.at[k, 1], xn)
    def c3(k, o, way, edge):
        buf = dn if way else up
        src = r2.at[o // 2, o % 2, :, col(k)] if edge else buf.at[o, :, col(k)]
        return rc(src, buf.at[o, :, col(k)], s3.at[k, way, o], q3.at[k, way, o], zd if way else zu)

    def stage0(k):
        c0(k).start()
    def stage1(k):
        c0(k).wait_recv()
        for p in (0, 1):
            for zh in range(Zh):
                for j in range(2):
                    at = (zh, 0, j, 1 - x) if p == 0 else (zh, 1, 1 - y, j)
                    own = g[at[0], at[1], at[2], c, at[3], :, col(k)].astype(f32)
                    r0[(*at, slice(None), col(k))] = (r0[(*at, slice(None), col(k))].astype(f32) + own).astype(bf16)
            c1(k, p).start()
    def pair(k, at):
        return g[at[0], at[1], at[2], c, at[3], :, col(k)].astype(f32) + r0[(*at, slice(None), col(k))].astype(f32)
    def stage2(k):
        for p in (0, 1):
            c1(k, p).wait_recv()
            j = (1 - y) if p == 0 else (1 - x)
            for zh in range(Zh):
                at = (zh, 0, j, x) if p == 0 else (zh, 1, y, j)
                r1[zh, p, j, :, col(k)] = (r1[zh, p, j, :, col(k)].astype(f32) + pair(k, at)).astype(bf16)
            c2(k, p).start()
    def stage3(k):
        for p in (0, 1):
            c2(k, p).wait_recv()
            j = y if p == 0 else x
            for zh in range(Zh):
                mine = r1[zh, p, j, :, col(k)].astype(f32) + pair(k, (zh, p, y, x))
                r2[zh, p, :, col(k)] = (r2[zh, p, :, col(k)].astype(f32) + mine).astype(bf16)
        @pl.when(z == 0)
        def _():
            for o in reversed(range(1, Z)): c3(k, o, 0, True).start()
        @pl.when(z == Z - 1)
        def _():
            for o in range(Z - 1): c3(k, o, 1, True).start()
    def hop(k, h):
        def go(way):
            for o in (reversed(range(h + 1, Z)) if way == 0 else range(Z - 1 - h)):
                buf = dn if way else up
                c3(k, o, way, False).wait_recv()
                buf[o, :, col(k)] = (buf[o, :, col(k)].astype(f32) + r2[o // 2, o % 2, :, col(k)].astype(f32)).astype(bf16)
                c3(k, o, way, False).start()
        pl.when(z == h)(lambda: go(0))
        pl.when(z == Z - 1 - h)(lambda: go(1))
    def final(k):
        out[:, col(k)] = r2[z // 2, z % 2, :, col(k)].astype(f32)
        @pl.when(z > 0)
        def _():
            c3(k, z, 0, False).wait_recv()
            out[:, col(k)] += up[z, :, col(k)].astype(f32)
        @pl.when(z < Z - 1)
        def _():
            c3(k, z, 1, False).wait_recv()
            out[:, col(k)] += dn[z, :, col(k)].astype(f32)
    def drain(k):
        c0(k).wait_send()
        for p in (0, 1):
            c1(k, p).wait_send(); c2(k, p).wait_send()
        for o in range(Z):
            pl.when(o > z)(lambda o=o: c3(k, o, 0, False).wait_send())
            pl.when(o < z)(lambda o=o: c3(k, o, 1, False).wait_send())

    n = len(cuts)
    stages = [stage1, stage2, stage3] + [functools.partial(lambda k, h: hop(k, h), h=h) for h in range(1, Z - 1)] + [final]
    for k in range(n): stage0(k)
    for k in range(1, 2 * F):
        rc(gmod, gm.at[owner], gs.at[k], gr.at[k], other(k)).start()
    gm[owner] = gmod[...]
    tokens = outp_own.shape[1]
    def swap(i, a, b):
        return rc(a.at[pl.ds(pl.multiple_of((1 - x) * tokens, 128), tokens), :], b.at[x], es.at[i], er.at[i], xn)
    def keep(i, a, b):
        return pltpu.make_async_copy(a.at[pl.ds(pl.multiple_of(x * tokens, 128), tokens), :], b.at[x], loc.at[i])
    pairs = ((outp, outp_own), (glat, glat_own))
    for i, (a, b) in enumerate(pairs):
        swap(i, a, b).start()
        keep(i, a, b).start()
    def conditioning():
        for k in range(1, 2 * F):
            rc(gmod, gm.at[lax.rem(owner + 2 * F - k, 2 * F)], gs.at[k], gr.at[k], xn).wait_recv()
        rows = wada.shape[0]
        step = wada.shape[1] // 6
        total = jnp.zeros((2 * F, rows), f32)
        for j in range(6):
            span = pl.ds(j * step, step)
            block = gm[:, 0, span]
            ada[:, span] = jnp.dot(silu_t[...], block, precision=lax.Precision.HIGHEST, preferred_element_type=f32)
            bada[:, span] = jnp.sum(block, axis=0, keepdims=True)
            total += lax.dot_general(block.astype(bf16), wada[:, span], (((1,), (1,)), ((), ())), preferred_element_type=f32)
        for i in range(F):
            cpart[i, 0:2, 0:rows] = total[2 * i : 2 * i + 2, :]
        for k in range(1, F):
            rc(cpart.at[peer(k)[0]], gcond.at[f], ks.at[k], kr.at[k], peer(k)).start()
        gcond[f] = cpart[f]
    def finish():
        for k in range(1, F):
            rc(cpart.at[0], gcond.at[lax.rem(f + F - k, F)], ks.at[k], kr.at[k], xn).wait_recv()
            rc(cpart.at[peer(k)[0]], gcond.at[f], ks.at[k], kr.at[k], peer(k)).wait_send()
        for k in range(1, 2 * F):
            rc(gmod, gm.at[owner], gs.at[k], gr.at[k], other(k)).wait_send()
        for i, (a, b) in enumerate(pairs):
            keep(i, a, b).wait()
            swap(i, a, b).wait_send()
            rc(b.at[1 - x], b.at[1 - x], es.at[i], er.at[i], xn).wait_recv()
    cpart[...] = jnp.zeros_like(cpart)
    for t in range(n + len(stages) - 1):
        for i, st in enumerate(stages):
            if 0 <= t - i < n: st(t - i)
        if t == 2: conditioning()
    for k in range(n): drain(k)
    finish()


def scatter(packed, outp, glat, gmod, wada, silu_t, F, count):
    owners, rows, width = packed.shape
    Z = F // 4
    Zh = Z // 2
    cuts = chunks_of(width, count)
    n = len(cuts)
    D = pltpu.SemaphoreType.DMA
    f32, bf16 = jnp.float32, jnp.bfloat16
    hbm, vm = pl.BlockSpec(memory_space=pl.ANY), pl.BlockSpec(memory_space=pltpu.VMEM)
    half = (2, outp.shape[0] // 2, outp.shape[1])
    mods = wada.shape[1]
    return pl.pallas_call(
        functools.partial(scatter_kernel, F, cuts),
        out_shape=[
            jax.ShapeDtypeStruct((rows, width), f32),
            jax.ShapeDtypeStruct(half, outp.dtype),
            jax.ShapeDtypeStruct(half, glat.dtype),
            jax.ShapeDtypeStruct((silu_t.shape[0], mods), f32),
            jax.ShapeDtypeStruct((1, mods), f32),
            jax.ShapeDtypeStruct((F, 8, 128), f32),
        ],
        in_specs=[vm, hbm, hbm, vm, vm, vm],
        out_specs=[vm, hbm, hbm, vm, vm, vm],
        scratch_shapes=[
            pltpu.VMEM((Zh, 2, 2, 2, rows, width), bf16),
            pltpu.VMEM((Zh, 2, 2, rows, width), bf16),
            pltpu.VMEM((Zh, 2, rows, width), bf16),
            pltpu.VMEM((Z, rows, width), bf16),
            pltpu.VMEM((Z, rows, width), bf16),
            pltpu.VMEM((owners, 1, mods), f32),
            pltpu.VMEM((F, 8, 128), f32),
            D((n,)), D((n,)), D((n, 2)), D((n, 2)), D((n, 2)), D((n, 2)), D((n, 2, Z)), D((n, 2, Z)),
            D((owners,)), D((owners,)), D((F,)), D((F,)), D((2,)), D((2,)), D((2,)),
        ],
        compiler_params=pltpu.CompilerParams(
            collective_id=1, has_side_effects=True, vmem_limit_bytes=60 * 2**20
        ),
        name="scatter_grads",
    )(packed.reshape(Zh, 2, 2, 2, 2, rows, width), outp, glat, gmod, wada, silu_t)


def body_fast(
    latents,
    condition,
    cotangent,
    w_ada,
    b_ada,
    w_qkv,
    b_query,
    b_value,
    w_out,
    b_out,
    w_up,
    b_up,
    w_down,
    b_down,
):
    f32 = jnp.float32
    bf16 = jnp.bfloat16
    F = lax.axis_size("fsdp")
    owners = F * lax.axis_size("sp")
    sp_index = lax.axis_index("sp")
    own_latents = 1
    tokens_all = latents.shape[1] * 2
    scale_factor = HD ** (-0.5)
    rows = w_qkv.shape[0]
    cond = jnp.pad(
        condition.astype(f32).reshape(2, F, rows).transpose(1, 0, 2), ((0, 0), (0, 6), (0, 128 - rows))
    )
    vectors = (b_query, b_value, b_out, b_down, b_up, b_ada)
    width = sum(part.size for part in vectors)
    bias = jnp.pad(jnp.concatenate(vectors).astype(f32), (0, -width % 1024)).reshape(-1, 128)
    qkv_full, out_full, up_full, down_full, cond_all, bias_all, modulate, inputs, grad_out = gather(
        (w_qkv, w_out, w_up, w_down), cond, bias, latents, cotangent, w_ada, F
    )
    bias_all = bias_all.reshape(F, -1)
    pieces = []
    start = 0
    for part in vectors:
        pieces.append(bias_all[:, start : start + part.size].reshape(-1))
        start = start + part.size
    query_bias, value_bias, out_bias, down_bias, up_bias, ada_bias = pieces
    inputs = inputs.astype(f32)[None]
    grad_out = grad_out.astype(f32)[None]
    modulate = modulate + ada_bias
    mod_parts = modulate.reshape(own_latents, 6, 1, D)
    shift_one, scale_one, gate_one = (mod_parts[:, 0], mod_parts[:, 1], mod_parts[:, 2])
    shift_two, scale_two, gate_two = (mod_parts[:, 3], mod_parts[:, 4], mod_parts[:, 5])

    normed_one, inverse_one = normalize(inputs)
    attn_in = (normed_one * (1.0 + scale_one) + shift_one).astype(bf16)
    qkv_bias = jnp.concatenate([query_bias, jnp.zeros_like(query_bias), value_bias]).astype(f32)
    projected = (
        jnp.einsum("btd,de->bte", attn_in, qkv_full, preferred_element_type=f32) + qkv_bias
    ).astype(bf16)
    heads = projected.reshape(own_latents, tokens_all, 3, H, HD).transpose(2, 0, 3, 1, 4)
    queries, key_heads, value_heads = heads[0], heads[1], heads[2]
    scores = (
        jnp.einsum("bhqd,bhkd->bhqk", queries, key_heads, preferred_element_type=f32) * scale_factor
    )
    log_total = jnp.log(jnp.sum(jnp.exp(scores), axis=-1, keepdims=True))
    soft_float = jnp.exp(scores - log_total)
    soft_half = soft_float.astype(bf16)
    mixed = jnp.einsum("bhqk,bhkd->bhqd", soft_half, value_heads, preferred_element_type=f32).astype(
        bf16
    )
    mixed_tokens = mixed.transpose(0, 2, 1, 3).reshape(own_latents, tokens_all, D)
    attn_proj = jnp.einsum(
        "btd,de->bte", mixed_tokens, out_full, preferred_element_type=f32
    ) + out_bias.astype(f32)
    residual = inputs + gate_one * attn_proj
    normed_two, inverse_two = normalize(residual)
    mlp_in = (normed_two * (1.0 + scale_two) + shift_two).astype(bf16)
    up_value = jnp.einsum(
        "btd,df->btf", mlp_in, up_full, preferred_element_type=f32
    ) + up_bias.astype(f32)
    activated = gelu_tanh(up_value).astype(bf16)
    down_value = jnp.einsum(
        "btf,fd->btd", activated, down_full, preferred_element_type=f32
    ) + down_bias.astype(f32)
    output = (residual + gate_two * down_value).astype(bf16)

    grad_gate_two = jnp.sum(grad_out * down_value, axis=1)
    grad_down = (grad_out * gate_two).astype(bf16)
    gw_down = jnp.einsum("btf,btd->fd", activated, grad_down, preferred_element_type=f32)
    gb_down = jnp.sum(grad_down.astype(f32), axis=(0, 1))
    grad_act = jnp.einsum("btd,fd->btf", grad_down, down_full, preferred_element_type=f32)
    grad_up = gelu_back(up_value, grad_act).astype(bf16)
    gw_up = jnp.einsum("btd,btf->df", mlp_in, grad_up, preferred_element_type=f32)
    gb_up = jnp.sum(grad_up.astype(f32), axis=(0, 1))
    grad_mlp = jnp.einsum("btf,df->btd", grad_up, up_full, preferred_element_type=f32)
    grad_scale_two = jnp.sum(grad_mlp * normed_two, axis=1)
    grad_shift_two = jnp.sum(grad_mlp, axis=1)
    grad_resid = grad_out + norm_back(grad_mlp * (1.0 + scale_two), normed_two, inverse_two)
    grad_gate_one = jnp.sum(grad_resid * attn_proj, axis=1)
    grad_proj = (grad_resid * gate_one).astype(bf16)
    gw_out = jnp.einsum("btd,bte->de", mixed_tokens, grad_proj, preferred_element_type=f32)
    gb_out = jnp.sum(grad_proj.astype(f32), axis=(0, 1))
    grad_mixed = jnp.einsum("bte,de->btd", grad_proj, out_full, preferred_element_type=f32).astype(
        bf16
    )
    grad_heads = grad_mixed.reshape(own_latents, tokens_all, H, HD).transpose(0, 2, 1, 3)
    grad_soft = jnp.einsum("bhqd,bhkd->bhqk", grad_heads, value_heads, preferred_element_type=f32)
    delta_sum = jnp.sum(soft_float * grad_soft, axis=-1, keepdims=True)
    grad_scores = (soft_float * (grad_soft - delta_sum)).astype(bf16)
    grad_queries = (
        jnp.einsum("bhqk,bhkd->bhqd", grad_scores, key_heads, preferred_element_type=f32)
        * scale_factor
    ).astype(bf16)
    grad_keys = (
        jnp.einsum("bhqk,bhqd->bhkd", grad_scores, queries, preferred_element_type=f32)
        * scale_factor
    ).astype(bf16)
    grad_values = jnp.einsum(
        "bhqk,bhqd->bhkd", soft_half, grad_heads, preferred_element_type=f32
    ).astype(bf16)
    grad_tokens = (
        jnp.stack([grad_queries, grad_keys, grad_values], axis=0)
        .transpose(1, 3, 0, 2, 4)
        .reshape(own_latents, tokens_all, 3 * D)
    )
    gw_qkv = jnp.einsum("btd,bte->de", attn_in, grad_tokens, preferred_element_type=f32)
    grad_tok_float = grad_tokens.astype(f32)
    gb_query = jnp.sum(grad_tok_float[:, :, :D], axis=(0, 1))
    gb_value = jnp.sum(grad_tok_float[:, :, 2 * D :], axis=(0, 1))
    grad_attn_in = jnp.einsum("bte,de->btd", grad_tokens, qkv_full, preferred_element_type=f32)
    grad_scale_one = jnp.sum(grad_attn_in * normed_one, axis=1)
    grad_shift_one = jnp.sum(grad_attn_in, axis=1)
    grad_latents = grad_resid + norm_back(grad_attn_in * (1.0 + scale_one), normed_one, inverse_one)

    grad_mod = jnp.concatenate(
        [
            grad_shift_one,
            grad_scale_one,
            grad_gate_one,
            grad_shift_two,
            grad_scale_two,
            grad_gate_two,
        ],
        axis=1,
    )
    biases = (gb_query, gb_value, gb_out, gb_up, gb_down)
    bias_rows = jnp.concatenate([part.reshape(owners, -1) for part in biases], axis=1)
    bias_lanes = -(-bias_rows.shape[1] // (rows * 128)) * 128
    bias_rows = jnp.pad(bias_rows, ((0, 0), (0, rows * bias_lanes - bias_rows.shape[1])))
    r2 = rows // 2

    def fold(grad):
        grad = grad.astype(bf16).reshape(owners, r2, 2, -1)
        return grad.transpose(0, 2, 1, 3).reshape(owners, rows, -1)

    stack = gw_down.shape[0] // (owners * rows)
    down_rows = gw_down.astype(bf16).reshape(owners, stack, rows, D).transpose(0, 2, 1, 3)
    packed = jnp.concatenate(
        [
            down_rows.reshape(owners, rows, stack * D),
            fold(gw_up),
            fold(gw_qkv),
            fold(gw_out),
            bias_rows.astype(bf16).reshape(owners, rows, bias_lanes),
        ],
        axis=2,
    )
    cond_rows = cond_all[:, :2, :rows].reshape(owners, 2, r2)
    silu_rows = jax.nn.silu(lax.dynamic_index_in_dim(cond_rows, sp_index, 1, False))
    owned, output, grad_latents, own_ada, own_bada, grad_silu = scatter(
        packed, output[0], grad_latents[0], grad_mod, w_ada, silu_rows.T, F, 6
    )

    def unfold(part):
        return jnp.concatenate([part[:r2], part[r2:]], axis=1)

    start = stack * D
    own_down = owned[:, :start].reshape(rows, stack, D).transpose(1, 0, 2).reshape(stack * rows, D)
    own = []
    for width in (gw_up.shape[1] // 2, gw_qkv.shape[1] // 2, gw_out.shape[1] // 2):
        own.append(unfold(owned[:, start : start + width]))
        start = start + width
    own_up, own_qkv, own_out = own
    sums = owned[:, start:].reshape(-1)
    own_bias = []
    start = 0
    for part in biases:
        own_bias.append(sums[start : start + part.size // owners])
        start = start + part.size // owners
    own_gb_query, own_gb_value, own_gb_out, own_gb_up, own_gb_down = own_bias
    own_gb_ada = lax.dynamic_index_in_dim(
        own_bada.reshape(owners, -1), lax.axis_index("fsdp") * 2 + sp_index, 0, False
    )
    grad_silu = grad_silu[:, :2, :rows].transpose(1, 0, 2).reshape(2, -1)
    grad_condition = silu_back(condition.astype(f32), grad_silu)
    return (
        output,
        grad_latents,
        grad_condition,
        own_ada,
        own_gb_ada,
        own_qkv,
        own_gb_query,
        own_gb_value,
        own_out,
        own_gb_out,
        own_up,
        own_gb_up,
        own_down,
        own_gb_down,
    )


def choose(*args):
    latents, w_qkv, w_down = args[0], args[5], args[12]
    fits = (
        lax.axis_size("sp") == 2
        and lax.axis_size("fsdp") % 8 == 0
        and latents.shape[0] == 2
        and latents.shape[1] % 128 == 0
        and w_qkv.shape[0] % 16 == 0
        and w_qkv.shape[0] <= 128
        and w_down.shape[0] % 64 == 0
        and w_down.shape[0] % (2 * w_qkv.shape[0]) == 0
    )
    return (body_fast if fits else body_general)(*args)


def solution(mesh):
    in_specs = (
        P("fsdp", "sp", None),
        P("fsdp", None),
        P("fsdp", "sp", None),
        P("fsdp", None),
        P("fsdp"),
        P("fsdp", None),
        P("fsdp"),
        P("fsdp"),
        P("fsdp", None),
        P("fsdp"),
        P("fsdp", None),
        P("fsdp"),
        P("fsdp", None),
        P("fsdp"),
    )
    out_specs = (
        P("fsdp", "sp", None),
        P("fsdp", "sp", None),
        P("fsdp", None),
        P(("fsdp", "sp"), None),
        P(("fsdp", "sp")),
        P(("fsdp", "sp"), None),
        P(("fsdp", "sp")),
        P(("fsdp", "sp")),
        P(("fsdp", "sp"), None),
        P(("fsdp", "sp")),
        P(("fsdp", "sp"), None),
        P(("fsdp", "sp")),
        P(("fsdp", "sp"), None),
        P(("fsdp", "sp")),
    )
    return jax.shard_map(choose, mesh=mesh, in_specs=in_specs, out_specs=out_specs, check_vma=False)
```

```python
import functools

import jax
import jax.numpy as jnp
from jax import lax
from jax.experimental import pallas as pl
from jax.experimental.pallas import tpu as pltpu
from jax.sharding import PartitionSpec as P

D = 768
H = 12
HD = 64


eps = 1e-06


def normalize(values):
    centered = values - jnp.mean(values, axis=-1, keepdims=True)
    inverse = lax.rsqrt(jnp.mean(centered * centered, axis=-1, keepdims=True) + eps)
    return (centered * inverse, inverse)


def norm_back(grad_in, normed, inverse):
    return inverse * (
        grad_in
        - jnp.mean(grad_in, axis=-1, keepdims=True)
        - normed * jnp.mean(grad_in * normed, axis=-1, keepdims=True)
    )


def gelu_tanh(values):
    return jax.nn.gelu(values, approximate=True)


def silu_back(values, grad_out):
    return jax.vjp(jax.nn.silu, values)[1](grad_out)[0]


def gelu_back(values, grad_out):
    return jax.vjp(gelu_tanh, values)[1](grad_out)[0]


LANES = 2048


def body_general(
    latents,
    condition,
    cotangent,
    w_ada,
    b_ada,
    w_qkv,
    b_query,
    b_value,
    w_out,
    b_out,
    w_up,
    b_up,
    w_down,
    b_down,
):
    f32 = jnp.float32
    bf16 = jnp.bfloat16
    fsdp_count = lax.axis_size("fsdp")
    sp_count = lax.axis_size("sp")
    owners = fsdp_count * sp_count
    fsdp_index = lax.axis_index("fsdp")
    sp_index = lax.axis_index("sp")
    owner_index = fsdp_index * sp_count + sp_index
    pair_latents = latents.shape[0]
    own_latents = pair_latents // sp_count
    latent_total = pair_latents * fsdp_count
    tokens_all = latents.shape[1] * sp_count
    scale_factor = HD ** (-0.5)

    small = [condition.reshape(-1), b_ada, b_query, b_value, b_out, b_up, b_down]
    width = sum(part.size for part in small)
    padded = -(-width // LANES) * LANES
    small.append(jnp.zeros((padded - width,), bf16))
    small_all = lax.all_gather(
        jnp.concatenate(small).reshape(1, padded // 128, 128), "fsdp", axis=0, tiled=True
    ).reshape(fsdp_count, padded)
    pieces = []
    start = 0
    for part in small[:-1]:
        pieces.append(small_all[:, start : start + part.size].reshape(-1))
        start = start + part.size
    cond_all, ada_bias, query_bias, value_bias, out_bias, up_bias, down_bias = pieces
    cond_all = cond_all.reshape(latent_total, D).astype(f32)
    silu_all = jax.nn.silu(cond_all)

    inputs = lax.all_to_all(latents, "sp", split_axis=0, concat_axis=1, tiled=True).astype(f32)
    grad_out = lax.all_to_all(cotangent, "sp", split_axis=0, concat_axis=1, tiled=True).astype(f32)

    ada_rows = w_ada.shape[0]
    silu_mine = lax.dynamic_index_in_dim(
        silu_all.astype(bf16).reshape(fsdp_count, sp_count, own_latents, D), sp_index, 1, False
    )
    silu_mine = lax.dynamic_index_in_dim(
        silu_mine.reshape(fsdp_count * own_latents, fsdp_count, ada_rows), fsdp_index, 1, False
    )
    mod_part = jnp.dot(silu_mine, w_ada, preferred_element_type=f32)
    mod_part = lax.all_to_all(
        mod_part.reshape(fsdp_count, own_latents * 6 * D), "fsdp", split_axis=0, concat_axis=0, tiled=True
    )
    modulate = jnp.sum(mod_part, axis=0).reshape(own_latents, 6 * D) + ada_bias.astype(f32)
    mod_parts = modulate.reshape(own_latents, 6, 1, D)
    shift_one, scale_one, gate_one = (mod_parts[:, 0], mod_parts[:, 1], mod_parts[:, 2])
    shift_two, scale_two, gate_two = (mod_parts[:, 3], mod_parts[:, 4], mod_parts[:, 5])

    qkv_full = lax.all_gather(w_qkv, "fsdp", axis=0, tiled=True)
    out_full = lax.all_gather(w_out, "fsdp", axis=0, tiled=True)
    up_full = lax.all_gather(w_up, "fsdp", axis=0, tiled=True)
    down_full = lax.all_gather(w_down, "fsdp", axis=0, tiled=True)

    normed_one, inverse_one = normalize(inputs)
    attn_in = (normed_one * (1.0 + scale_one) + shift_one).astype(bf16)
    qkv_bias = jnp.concatenate([query_bias, jnp.zeros_like(query_bias), value_bias]).astype(f32)
    projected = (
        jnp.einsum("btd,de->bte", attn_in, qkv_full, preferred_element_type=f32) + qkv_bias
    ).astype(bf16)
    heads = projected.reshape(own_latents, tokens_all, 3, H, HD).transpose(2, 0, 3, 1, 4)
    queries, key_heads, value_heads = heads[0], heads[1], heads[2]
    scores = (
        jnp.einsum("bhqd,bhkd->bhqk", queries, key_heads, preferred_element_type=f32) * scale_factor
    )
    log_total = jnp.log(jnp.sum(jnp.exp(scores), axis=-1, keepdims=True))
    soft_float = jnp.exp(scores - log_total)
    soft_half = soft_float.astype(bf16)
    mixed = jnp.einsum("bhqk,bhkd->bhqd", soft_half, value_heads, preferred_element_type=f32).astype(
        bf16
    )
    mixed_tokens = mixed.transpose(0, 2, 1, 3).reshape(own_latents, tokens_all, D)
    attn_proj = jnp.einsum(
        "btd,de->bte", mixed_tokens, out_full, preferred_element_type=f32
    ) + out_bias.astype(f32)
    residual = inputs + gate_one * attn_proj
    normed_two, inverse_two = normalize(residual)
    mlp_in = (normed_two * (1.0 + scale_two) + shift_two).astype(bf16)
    up_value = jnp.einsum(
        "btd,df->btf", mlp_in, up_full, preferred_element_type=f32
    ) + up_bias.astype(f32)
    activated = gelu_tanh(up_value).astype(bf16)
    down_value = jnp.einsum(
        "btf,fd->btd", activated, down_full, preferred_element_type=f32
    ) + down_bias.astype(f32)
    output = (residual + gate_two * down_value).astype(bf16)
    output = lax.all_to_all(output, "sp", split_axis=1, concat_axis=0, tiled=True)

    grad_gate_two = jnp.sum(grad_out * down_value, axis=1)
    grad_down = (grad_out * gate_two).astype(bf16)
    gw_down = jnp.einsum("btf,btd->fd", activated, grad_down, preferred_element_type=f32)
    gb_down = jnp.sum(grad_down.astype(f32), axis=(0, 1))
    grad_act = jnp.einsum("btd,fd->btf", grad_down, down_full, preferred_element_type=f32)
    grad_up = gelu_back(up_value, grad_act).astype(bf16)
    gw_up = jnp.einsum("btd,btf->df", mlp_in, grad_up, preferred_element_type=f32)
    gb_up = jnp.sum(grad_up.astype(f32), axis=(0, 1))
    grad_mlp = jnp.einsum("btf,df->btd", grad_up, up_full, preferred_element_type=f32)
    grad_scale_two = jnp.sum(grad_mlp * normed_two, axis=1)
    grad_shift_two = jnp.sum(grad_mlp, axis=1)
    grad_resid = grad_out + norm_back(grad_mlp * (1.0 + scale_two), normed_two, inverse_two)
    grad_gate_one = jnp.sum(grad_resid * attn_proj, axis=1)
    grad_proj = (grad_resid * gate_one).astype(bf16)
    gw_out = jnp.einsum("btd,bte->de", mixed_tokens, grad_proj, preferred_element_type=f32)
    gb_out = jnp.sum(grad_proj.astype(f32), axis=(0, 1))
    grad_mixed = jnp.einsum("bte,de->btd", grad_proj, out_full, preferred_element_type=f32).astype(
        bf16
    )
    grad_heads = grad_mixed.reshape(own_latents, tokens_all, H, HD).transpose(0, 2, 1, 3)
    grad_soft = jnp.einsum("bhqd,bhkd->bhqk", grad_heads, value_heads, preferred_element_type=f32)
    delta_sum = jnp.sum(soft_float * grad_soft, axis=-1, keepdims=True)
    grad_scores = (soft_float * (grad_soft - delta_sum)).astype(bf16)
    grad_queries = (
        jnp.einsum("bhqk,bhkd->bhqd", grad_scores, key_heads, preferred_element_type=f32)
        * scale_factor
    ).astype(bf16)
    grad_keys = (
        jnp.einsum("bhqk,bhqd->bhkd", grad_scores, queries, preferred_element_type=f32)
        * scale_factor
    ).astype(bf16)
    grad_values = jnp.einsum(
        "bhqk,bhqd->bhkd", soft_half, grad_heads, preferred_element_type=f32
    ).astype(bf16)
    grad_tokens = (
        jnp.stack([grad_queries, grad_keys, grad_values], axis=0)
        .transpose(1, 3, 0, 2, 4)
        .reshape(own_latents, tokens_all, 3 * D)
    )
    gw_qkv = jnp.einsum("btd,bte->de", attn_in, grad_tokens, preferred_element_type=f32)
    grad_tok_float = grad_tokens.astype(f32)
    gb_query = jnp.sum(grad_tok_float[:, :, :D], axis=(0, 1))
    gb_value = jnp.sum(grad_tok_float[:, :, 2 * D :], axis=(0, 1))
    grad_attn_in = jnp.einsum("bte,de->btd", grad_tokens, qkv_full, preferred_element_type=f32)
    grad_scale_one = jnp.sum(grad_attn_in * normed_one, axis=1)
    grad_shift_one = jnp.sum(grad_attn_in, axis=1)
    grad_latents = grad_resid + norm_back(grad_attn_in * (1.0 + scale_one), normed_one, inverse_one)
    grad_latents = lax.all_to_all(grad_latents, "sp", split_axis=1, concat_axis=0, tiled=True)

    grad_mod = jnp.concatenate(
        [
            grad_shift_one,
            grad_scale_one,
            grad_gate_one,
            grad_shift_two,
            grad_scale_two,
            grad_gate_two,
        ],
        axis=1,
    )
    grad_mod = lax.all_to_all(
        jnp.broadcast_to(grad_mod[None], (owners, own_latents, 6 * D)),
        ("fsdp", "sp"),
        split_axis=0,
        concat_axis=0,
        tiled=True,
    ).reshape(latent_total, 6 * D)

    rows = D // owners
    biases = (gb_query, gb_value, gb_out, gb_up, gb_down)
    bias_rows = jnp.concatenate([part.reshape(owners, -1) for part in biases], axis=1)
    bias_width = bias_rows.shape[1]
    bias_lanes = -(-bias_width // (rows * 128)) * 128
    bias_rows = jnp.pad(bias_rows, ((0, 0), (0, rows * bias_lanes - bias_width)))
    stack = down_full.shape[0] // D
    gw_down = (
        gw_down.astype(bf16)
        .reshape(owners, stack, rows, D)
        .transpose(0, 2, 1, 3)
        .reshape(D, stack * D)
    )
    packed = jnp.concatenate(
        [
            gw_down,
            gw_up.astype(bf16),
            gw_qkv.astype(bf16),
            gw_out.astype(bf16),
            bias_rows.astype(bf16).reshape(D, bias_lanes),
        ],
        axis=1,
    )
    owned = lax.psum_scatter(packed, ("fsdp", "sp"), scatter_dimension=0, tiled=True).astype(f32)
    own_weights = []
    start = 0
    for width in (stack * D, up_full.shape[1], 3 * D, D, bias_lanes):
        own_weights.append(owned[:, start : start + width])
        start = start + width
    own_down, own_up, own_qkv, own_out, bias_sums = own_weights
    own_down = own_down.reshape(rows, stack, D).transpose(1, 0, 2).reshape(stack * rows, D)
    bias_sums = bias_sums.reshape(-1)
    own_bias = []
    start = 0
    for part in biases:
        width = part.size // owners
        own_bias.append(bias_sums[start : start + width])
        start = start + width
    own_gb_query, own_gb_value, own_gb_out, own_gb_up, own_gb_down = own_bias
    silu_rows = lax.dynamic_index_in_dim(
        silu_all.reshape(latent_total, owners, D // owners), owner_index, 1, False
    )
    own_ada = jnp.dot(silu_rows.T, grad_mod, precision=lax.Precision.HIGHEST)
    own_gb_ada = lax.dynamic_index_in_dim(
        jnp.sum(grad_mod, axis=0).reshape(owners, -1), owner_index, 0, False
    )
    grad_silu = jnp.dot(grad_mod.astype(bf16), w_ada.T, preferred_element_type=f32)
    grad_silu = lax.all_to_all(
        grad_silu.reshape(fsdp_count, pair_latents * ada_rows),
        "fsdp",
        split_axis=0,
        concat_axis=0,
        tiled=True,
    )
    grad_silu = (
        grad_silu.reshape(fsdp_count, pair_latents, ada_rows)
        .transpose(1, 0, 2)
        .reshape(pair_latents, D)
    )
    grad_condition = silu_back(condition.astype(f32), grad_silu)
    return (
        output,
        grad_latents,
        grad_condition,
        own_ada,
        own_gb_ada,
        own_qkv,
        own_gb_query,
        own_gb_value,
        own_out,
        own_gb_out,
        own_up,
        own_gb_up,
        own_down,
        own_gb_down,
    )


MESH = pl.DeviceIdType.MESH


class Plan:
    def __init__(self, rows, cols):
        self.rows, self.cols = rows, cols
        self.by_rows = rows % 64 == 0
        n = (rows // 32) if self.by_rows else (cols // 256)
        unit = 16 if self.by_rows else 128
        big = -(-2 * n // 3)
        self.half = n * unit
        self.big = big * unit
        self.unit = unit
    def at(self, ref, row, h=None, q=None):
        rows, cols, unit = self.rows, self.cols, self.unit
        if h is None:
            return ref.at[pl.ds(pl.multiple_of(row, 16), rows), :]
        start = h * self.half + (self.big if q == 1 else 0)
        size = self.half if q is None else (self.big if q == 0 else self.half - self.big)
        if self.by_rows:
            return ref.at[pl.ds(pl.multiple_of(row + start, 16), size), :]
        return ref.at[pl.ds(pl.multiple_of(row, 16), rows), pl.ds(pl.multiple_of(start, 128), size)]

def gather_kernel(F, plans, *refs):
    n = len(plans)
    f32, bf16 = jnp.float32, jnp.bfloat16
    ins, (cond, bias, lat, cot, wada) = refs[:n], refs[n:n + 5]
    outs, (cond_all, bias_all, mod, lat_all, cot_all) = refs[n + 5:2 * n + 5], refs[2 * n + 5:2 * n + 10]
    part, parts, zs, zr, xs, xr, ys, yr, xds, xdr, yds, ydr, ss, sr, loc, es, er, ps, pr = refs[2 * n + 10:]
    f = lax.axis_index("fsdp"); x = lax.axis_index("sp")
    c = f % 2; y = (f // 2) % 2; z = f // 4; Z = F // 4
    def dev(x_, y_, z_, c_):
        return ((z_ * 2 + y_) * 2 + c_, x_)
    xn, yn, sib = dev(1 - x, y, z, c), dev(x, 1 - y, z, c), dev(x, y, z, 1 - c)
    zu, zd = dev(x, y, z + 1, c), dev(x, y, z - 1, c)
    def peer(k):
        return (lax.rem(f + k, F), x)
    bar = pltpu.get_barrier_semaphore()
    pl.semaphore_signal(bar, inc=1, device_id=xn, device_id_type=MESH)
    for k in range(1, F):
        pl.semaphore_signal(bar, inc=1, device_id=peer(k), device_id_type=MESH)
    pl.semaphore_wait(bar, F)

    sends = []
    def send(ok, build):
        if ok is None:
            build().start()
        else:
            pl.when(ok)(lambda: build().start())
        sends.append((ok, build))
    def rc(src, dst, s, r, d):
        return pltpu.make_async_remote_copy(src_ref=src, dst_ref=dst, send_sem=s, recv_sem=r, device_id=d, device_id_type=MESH)

    def base(m, y_, z_, c_=c):
        return ((z_ * 2 + y_) * 2 + c_) * plans[m].rows
    def piece(m, y_, z_, h=None, q=None, c_=None):
        return plans[m].at(outs[m], base(m, y_, z_, c if c_ is None else c_), h, q)
    def mine(m, h=None, q=None):
        return plans[m].at(ins[m], 0, h, q)
    def to_sib(m, ok, kind, y_, z_, h=None, q=None, own=False):
        send(ok, lambda: rc(mine(m, h, q) if own else piece(m, y_, z_, h, q), piece(m, y_, z_, h, q),
                              ss.at[m, kind, z_], sr.at[m, kind, z_], sib))
    def arrived(m, ok, sem_s, sem_r, *where, c_=None):
        def go():
            p = piece(m, *where, c_=c_)
            rc(p, p, sem_s, sem_r, xn).wait_recv()
        if ok is None: go()
        else: pl.when(ok)(go)

    def start_own(m):
        send(None, lambda: rc(mine(m, x), piece(m, y, z, x), ys.at[m, z], yr.at[m, z], yn))
        send(z + 1 < Z, lambda: rc(mine(m, x), piece(m, y, z, x), zs.at[m, 0, z], zr.at[m, z], zu))
        send(z > 0, lambda: rc(mine(m, x), piece(m, y, z, x), zs.at[m, 1, z], zr.at[m, z], zd))
        send(None, lambda: rc(mine(m, 1 - x, 1), piece(m, y, z, 1 - x, 1), yds.at[m, z], ydr.at[m, z], yn))
        to_sib(m, None, 0, y, z, own=True)
        pltpu.make_async_copy(mine(m), piece(m, y, z), loc.at[m]).start()

    def z_round(m, d):
        for sign in (-1, 1):
            o = z + sign * d
            ok = (o >= 0) if sign < 0 else (o < Z)
            arrived(m, ok, zs.at[m, 0, o], zr.at[m, o], y, o, x)
            if sign < 0:
                send(ok & (z + 1 < Z), lambda o=o: rc(piece(m, y, o, x), piece(m, y, o, x), zs.at[m, 0, o], zr.at[m, o], zu))
            else:
                send(ok & (z > 0), lambda o=o: rc(piece(m, y, o, x), piece(m, y, o, x), zs.at[m, 1, o], zr.at[m, o], zd))
            send(ok, lambda o=o: rc(piece(m, y, o, x), piece(m, y, o, x), xs.at[m, o], xr.at[m, o], xn))
            send(ok, lambda o=o: rc(piece(m, y, o, x), piece(m, y, o, x), ys.at[m, o], yr.at[m, o], yn))
            to_sib(m, ok, 0, y, o, x)

    def xy_round(m, d):
        for sign in ((-1, 1) if d else (0,)):
            o = z + sign * d
            ok = None if d == 0 else ((o >= 0) if sign < 0 else (o < Z))
            arrived(m, ok, ys.at[m, o], yr.at[m, o], 1 - y, o, x)
            send(ok, lambda o=o: rc(piece(m, 1 - y, o, x, 0), piece(m, 1 - y, o, x, 0), xds.at[m, o], xdr.at[m, o], xn))
            to_sib(m, ok, 2, 1 - y, o, x)
            if d:
                arrived(m, ok, xs.at[m, o], xr.at[m, o], y, o, 1 - x)
                send(ok, lambda o=o: rc(piece(m, y, o, 1 - x, 1), piece(m, y, o, 1 - x, 1), yds.at[m, o], ydr.at[m, o], yn))
                to_sib(m, ok, 1, y, o, 1 - x)

    def last_round(m, d):
        for sign in ((-1, 1) if d else (0,)):
            o = z + sign * d
            ok = None if d == 0 else ((o >= 0) if sign < 0 else (o < Z))
            arrived(m, ok, xds.at[m, o], xdr.at[m, o], 1 - y, o, 1 - x, 0)
            to_sib(m, ok, 3, 1 - y, o, 1 - x, 0)
            arrived(m, ok, yds.at[m, o], ydr.at[m, o], 1 - y, o, 1 - x, 1)
            to_sib(m, ok, 4, 1 - y, o, 1 - x, 1)

    def finish(m):
        pltpu.make_async_copy(mine(m), piece(m, y, z), loc.at[m]).wait()
        b = 1 - c
        arrived(m, None, ss.at[m, 0, z], sr.at[m, 0, z], y, z, c_=b)
        for d in range(Z):
            for sign in ((-1, 1) if d else (0,)):
                o = z + sign * d
                ok = None if d == 0 else ((o >= 0) if sign < 0 else (o < Z))
                if d:
                    arrived(m, ok, ss.at[m, 0, o], sr.at[m, 0, o], y, o, x, c_=b)
                    arrived(m, ok, ss.at[m, 1, o], sr.at[m, 1, o], y, o, 1 - x, c_=b)
                arrived(m, ok, ss.at[m, 2, o], sr.at[m, 2, o], 1 - y, o, x, c_=b)
                arrived(m, ok, ss.at[m, 3, o], sr.at[m, 3, o], 1 - y, o, 1 - x, 0, c_=b)
                arrived(m, ok, ss.at[m, 4, o], sr.at[m, 4, o], 1 - y, o, 1 - x, 1, c_=b)

    rows = plans[0].rows
    tokens = lat.shape[1]
    for k in range(1, F):
        to = peer(k)
        rc(cond.at[to[0]], cond_all.at[f], es.at[0, k], er.at[0, k], to).start()
        rc(bias, bias_all.at[f], es.at[1, k], er.at[1, k], to).start()
    def swap(i, a, b):
        return rc(a.at[1 - x], b.at[pl.ds(pl.multiple_of(x * tokens, 128), tokens), :], es.at[2, i], er.at[2, i], xn)
    def keep(i, a, b):
        return pltpu.make_async_copy(a.at[x], b.at[pl.ds(pl.multiple_of(x * tokens, 128), tokens), :], loc.at[n + i])
    for i, (a, b) in enumerate(((lat, lat_all), (cot, cot_all))):
        swap(i, a, b).start()
        keep(i, a, b).start()
    start_own(0)
    cond_all[f] = cond[f]
    bias_all[f] = bias[...]
    for m in range(1, n):
        start_own(m)
    for k in range(1, F):
        rc(cond.at[0], cond_all.at[lax.rem(f + F - k, F)], es.at[0, k], er.at[0, k], xn).wait_recv()
    picked = jnp.where(x == 0, cond_all[:, 0, :], cond_all[:, 1, :])[:, :rows]
    picked = (picked / (1.0 + jnp.exp(-picked))).astype(bf16)
    made = jnp.dot(picked, wada[...], preferred_element_type=f32)
    for i in range(F):
        part[i] = made[i : i + 1, :]
    for k in range(1, F):
        to = peer(k)
        rc(part.at[to[0]], parts.at[f], ps.at[k], pr.at[k], to).start()
    parts[f] = part[f]
    for d in range(Z + 2):
        for m in range(n):
            if 0 < d < Z: z_round(m, d)
            if 0 < d <= Z: xy_round(m, d - 1)
            if d > 1: last_round(m, d - 2)
        if d == 1:
            for k in range(1, F):
                rc(part.at[0], parts.at[lax.rem(f + F - k, F)], ps.at[k], pr.at[k], xn).wait_recv()
            mod[...] = jnp.sum(parts[...], axis=0)
    for m in range(n): finish(m)
    for k in range(1, F):
        to = peer(k)
        rc(bias, bias_all.at[lax.rem(f + F - k, F)], es.at[1, k], er.at[1, k], xn).wait_recv()
        rc(cond.at[to[0]], cond_all.at[f], es.at[0, k], er.at[0, k], to).wait_send()
        rc(bias, bias_all.at[f], es.at[1, k], er.at[1, k], to).wait_send()
        rc(part.at[to[0]], parts.at[f], ps.at[k], pr.at[k], to).wait_send()
    for i, (a, b) in enumerate(((lat, lat_all), (cot, cot_all))):
        keep(i, a, b).wait()
        swap(i, a, b).wait_send()
        got = b.at[pl.ds(pl.multiple_of((1 - x) * tokens, 128), tokens), :]
        rc(got, got, es.at[2, i], er.at[2, i], xn).wait_recv()
    for cond_, build in sends:
        if cond_ is None: build().wait_send()
        else: pl.when(cond_)(lambda build=build: build().wait_send())


def gather(shards, cond, bias, lat, cot, wada, F):
    plans = [Plan(*s.shape) for s in shards]
    n, Z = len(shards), F // 4
    D = pltpu.SemaphoreType.DMA
    f32 = jnp.float32
    hbm, vm = pl.BlockSpec(memory_space=pl.ANY), pl.BlockSpec(memory_space=pltpu.VMEM)
    width = wada.shape[1]
    whole = jax.ShapeDtypeStruct((lat.shape[0] * lat.shape[1], lat.shape[2]), lat.dtype)
    return pl.pallas_call(
        functools.partial(gather_kernel, F, plans),
        out_shape=[jax.ShapeDtypeStruct((s.shape[0] * F, s.shape[1]), s.dtype) for s in shards]
        + [
            jax.ShapeDtypeStruct(cond.shape, f32),
            jax.ShapeDtypeStruct((F, *bias.shape), f32),
            jax.ShapeDtypeStruct((1, width), f32),
            whole,
            whole,
        ],
        in_specs=[hbm] * n + [vm, vm, hbm, hbm, vm],
        out_specs=[hbm] * n + [vm, vm, vm, hbm, hbm],
        scratch_shapes=[pltpu.VMEM((F, 1, width), f32)] * 2
        + [D((n, 2, Z)), D((n, Z))]
        + [D((n, Z))] * 8
        + [D((n, 5, Z))] * 2
        + [D((n + 2,)), D((3, F)), D((3, F)), D((F,)), D((F,))],
        compiler_params=pltpu.CompilerParams(
            collective_id=0, has_side_effects=True, vmem_limit_bytes=32 * 2**20
        ),
        name="gather_weights",
    )(*shards, cond, bias, lat, cot, wada)


def chunks_of(width, count):
    tiles = width // 128
    edges = [128 * (tiles * i // count) for i in range(count + 1)]
    return [(a, b - a) for a, b in zip(edges[:-1], edges[1:])]

GELU = 0.7978845608028654


def backward_kernel(F, cuts, *refs):
    (
        lat, cot, mods, proj, mixed, attn_proj, upv, act, outp, ggate, wada, silu_t, wqkv_h, wout_h, wup_h, wdown_h,
        out, outp_own, glat_own, ada, bada, gcond,
        g, r0, r1, r2, up, dn, gm, cpart, w1, w2, gu, gt, norm_one, norm_two, resid, gmod, left, glat,
        s0, q0, s1, q1, s2, q2, s3, q3, gs, gr, ks, kr, es, er, loc, wl,
    ) = refs
    f32, bf16 = jnp.float32, jnp.bfloat16
    f = lax.axis_index("fsdp"); x = lax.axis_index("sp")
    c = f % 2; y = (f // 2) % 2; z = f // 4; Z = F // 4; Zh = Z // 2
    def dev(x_, y_, z_, c_):
        return ((z_ * 2 + y_) * 2 + c_, x_)
    xn, yn, sib = dev(1 - x, y, z, c), dev(x, 1 - y, z, c), dev(x, y, z, 1 - c)
    zu, zd = dev(x, y, z + 1, c), dev(x, y, z - 1, c)
    owner = f * 2 + x
    def other(k):
        o = lax.rem(owner + k, 2 * F)
        return (o // 2, o % 2)
    def peer(k):
        return (lax.rem(f + k, F), x)
    bar = pltpu.get_barrier_semaphore()
    for k in range(1, 2 * F):
        pl.semaphore_signal(bar, inc=1, device_id=other(k), device_id_type=MESH)
    pl.semaphore_wait(bar, 2 * F - 1)

    def rc(src, dst, s, r, d):
        return pltpu.make_async_remote_copy(src_ref=src, dst_ref=dst, send_sem=s, recv_sem=r, device_id=d, device_id_type=MESH)
    def col(k):
        return pl.ds(*cuts[k])
    def c0(k):
        return rc(g.at[:, :, :, 1 - c, :, :, col(k)], r0.at[:, :, :, :, :, col(k)], s0.at[k], q0.at[k], sib)
    def c1(k, p):
        if p == 0:
            return rc(r0.at[:, 0, :, 1 - x, :, col(k)], r1.at[:, 0, :, :, col(k)], s1.at[k, 0], q1.at[k, 0], xn)
        return rc(r0.at[:, 1, 1 - y, :, :, col(k)], r1.at[:, 1, :, :, col(k)], s1.at[k, 1], q1.at[k, 1], yn)
    def c2(k, p):
        if p == 0:
            return rc(r1.at[:, 0, 1 - y, :, col(k)], r2.at[:, 0, :, col(k)], s2.at[k, 0], q2.at[k, 0], yn)
        return rc(r1.at[:, 1, 1 - x, :, col(k)], r2.at[:, 1, :, col(k)], s2.at[k, 1], q2.at[k, 1], xn)
    def c3(k, o, way, edge):
        buf = dn if way else up
        src = r2.at[o // 2, o % 2, :, col(k)] if edge else buf.at[o, :, col(k)]
        return rc(src, buf.at[o, :, col(k)], s3.at[k, way, o], q3.at[k, way, o], zd if way else zu)

    def stage0(k):
        c0(k).start()
    def stage1(k):
        c0(k).wait_recv()
        for p in (0, 1):
            for zh in range(Zh):
                for j in range(2):
                    at = (zh, 0, j, 1 - x) if p == 0 else (zh, 1, 1 - y, j)
                    own = g[at[0], at[1], at[2], c, at[3], :, col(k)].astype(f32)
                    r0[(*at, slice(None), col(k))] = (r0[(*at, slice(None), col(k))].astype(f32) + own).astype(bf16)
            c1(k, p).start()
    def pair(k, at):
        return g[at[0], at[1], at[2], c, at[3], :, col(k)].astype(f32) + r0[(*at, slice(None), col(k))].astype(f32)
    def stage2(k):
        for p in (0, 1):
            c1(k, p).wait_recv()
            j = (1 - y) if p == 0 else (1 - x)
            for zh in range(Zh):
                at = (zh, 0, j, x) if p == 0 else (zh, 1, y, j)
                r1[zh, p, j, :, col(k)] = (r1[zh, p, j, :, col(k)].astype(f32) + pair(k, at)).astype(bf16)
            c2(k, p).start()
    def stage3(k):
        for p in (0, 1):
            c2(k, p).wait_recv()
            j = y if p == 0 else x
            for zh in range(Zh):
                mine = r1[zh, p, j, :, col(k)].astype(f32) + pair(k, (zh, p, y, x))
                r2[zh, p, :, col(k)] = (r2[zh, p, :, col(k)].astype(f32) + mine).astype(bf16)
        @pl.when(z == 0)
        def _():
            for o in reversed(range(1, Z)): c3(k, o, 0, True).start()
        @pl.when(z == Z - 1)
        def _():
            for o in range(Z - 1): c3(k, o, 1, True).start()
    def hop(k, h):
        def go(way):
            for o in (reversed(range(h + 1, Z)) if way == 0 else range(Z - 1 - h)):
                buf = dn if way else up
                c3(k, o, way, False).wait_recv()
                buf[o, :, col(k)] = (buf[o, :, col(k)].astype(f32) + r2[o // 2, o % 2, :, col(k)].astype(f32)).astype(bf16)
                c3(k, o, way, False).start()
        pl.when(z == h)(lambda: go(0))
        pl.when(z == Z - 1 - h)(lambda: go(1))
    def final(k):
        out[:, col(k)] = r2[z // 2, z % 2, :, col(k)].astype(f32)
        @pl.when(z > 0)
        def _():
            c3(k, z, 0, False).wait_recv()
            out[:, col(k)] += up[z, :, col(k)].astype(f32)
        @pl.when(z < Z - 1)
        def _():
            c3(k, z, 1, False).wait_recv()
            out[:, col(k)] += dn[z, :, col(k)].astype(f32)
    def drain(k):
        c0(k).wait_send()
        for p in (0, 1):
            c1(k, p).wait_send(); c2(k, p).wait_send()
        for o in range(Z):
            pl.when(o > z)(lambda o=o: c3(k, o, 0, False).wait_send())
            pl.when(o < z)(lambda o=o: c3(k, o, 1, False).wait_send())

    tokens = outp_own.shape[1]
    def swap(i, a, b):
        return rc(a.at[pl.ds(pl.multiple_of((1 - x) * tokens, 128), tokens), :], b.at[x], es.at[i], er.at[i], xn)
    def keep(i, a, b):
        return pltpu.make_async_copy(a.at[pl.ds(pl.multiple_of(x * tokens, 128), tokens), :], b.at[x], loc.at[i])
    pairs = ((outp, outp_own), (glat, glat_own))
    def hand_over(i):
        swap(i, *pairs[i]).start()
        keep(i, *pairs[i]).start()
    def conditioning():
        for k in range(1, 2 * F):
            rc(gmod, gm.at[lax.rem(owner + 2 * F - k, 2 * F)], gs.at[k], gr.at[k], xn).wait_recv()
        rows = wada.shape[0]
        step = wada.shape[1] // 6
        total = jnp.zeros((2 * F, rows), f32)
        for j in range(6):
            span = pl.ds(j * step, step)
            block = gm[:, j, :]
            ada[:, span] = jnp.dot(silu_t[...], block, precision=lax.Precision.HIGHEST, preferred_element_type=f32)
            bada[:, span] = jnp.sum(block, axis=0, keepdims=True)
            total += lax.dot_general(block.astype(bf16), wada[:, span], (((1,), (1,)), ((), ())), preferred_element_type=f32)
        for i in range(F):
            cpart[i, 0:2, 0:rows] = total[2 * i : 2 * i + 2, :]
        for k in range(1, F):
            rc(cpart.at[peer(k)[0]], gcond.at[f], ks.at[k], kr.at[k], peer(k)).start()
        gcond[f] = cpart[f]
    def finish():
        for k in range(1, F):
            rc(cpart.at[0], gcond.at[lax.rem(f + F - k, F)], ks.at[k], kr.at[k], xn).wait_recv()
            rc(cpart.at[peer(k)[0]], gcond.at[f], ks.at[k], kr.at[k], peer(k)).wait_send()
        for k in range(1, 2 * F):
            rc(gmod, gm.at[owner], gs.at[k], gr.at[k], other(k)).wait_send()
        for i, (a, b) in enumerate(pairs):
            keep(i, a, b).wait()
            swap(i, a, b).wait_send()
            rc(b.at[1 - x], b.at[1 - x], es.at[i], er.at[i], xn).wait_recv()
    d_model = lat.shape[1]
    ff = act.shape[1]
    owners = 2 * F
    rows = g.shape[5]
    half = rows // 2
    loads = [
        (wdown_h, w1),
        (wup_h, w2),
    ]
    late = [(wqkv_h.at[:, pl.ds(d_model * j, d_model)], w1.at[pl.ds(d_model * j, d_model), :]) for j in range(3)]
    late.append((wout_h, w1.at[pl.ds(3 * d_model, d_model), :]))
    def load(i, pair):
        return pltpu.make_async_copy(pair[0], pair[1], wl.at[i])
    for i, pair_ in enumerate(loads): load(i, pair_).start()
    hand_over(0)
    cpart[...] = jnp.zeros_like(cpart)

    def slot(o):
        zo = o // 8
        return (zo // 2, zo % 2, (o // 4) % 2, (o // 2) % 2, o % 2)
    def norm(v):
        v = v - jnp.mean(v, axis=-1, keepdims=True)
        inv = lax.rsqrt(jnp.mean(v * v, axis=-1, keepdims=True) + eps)
        return v * inv, inv
    def norm_grad(gv, nv, inv):
        return inv * (gv - jnp.mean(gv, axis=-1, keepdims=True) - nv * jnp.mean(gv * nv, axis=-1, keepdims=True))
    def tdot(p, q):
        return lax.dot_general(p, q, (((0,), (0,)), ((), ())), preferred_element_type=f32)
    def dott(p, q):
        return lax.dot_general(p, q, (((1,), (1,)), ((), ())), preferred_element_type=f32)
    def mod(i):
        return mods[i : i + 1, :]
    def fold(col0, right, span, first):
        step = 128
        def one(i, carry):
            off = first + i * step
            lo = jnp.dot(left[...], right[:, pl.ds(pl.multiple_of(off, 128), step)], preferred_element_type=f32)
            hi_at = right.shape[1] // 2 + off
            hi = jnp.dot(left[...], right[:, pl.ds(pl.multiple_of(hi_at, 128), step)], preferred_element_type=f32)
            to = pl.ds(pl.multiple_of(col0 + off, 128), step)
            for o in range(owners):
                both = jnp.concatenate([lo[o * half : o * half + half], hi[o * half : o * half + half]], axis=0)
                g[(*slot(o), slice(None), to)] = both.astype(bf16)
            return carry
        lax.fori_loop(0, span // step, one, 0)
    def owner_sums(total):
        wide = total.shape[1]
        per = wide // owners
        cols = lax.broadcasted_iota(jnp.int32, (owners, wide), 1)
        mine = cols // per == lax.broadcasted_iota(jnp.int32, (owners, wide), 0)
        spread = jnp.where(mine, jnp.broadcast_to(total, (owners, wide)), 0.0).astype(bf16)
        pick = lax.broadcasted_iota(jnp.int32, (wide, 128), 0) % per == lax.broadcasted_iota(jnp.int32, (wide, 128), 1)
        return jnp.dot(spread, jnp.where(pick, 1.0, 0.0).astype(bf16), preferred_element_type=f32)

    n = len(cuts)
    stages = [stage1, stage2, stage3] + [functools.partial(lambda k, h: hop(k, h), h=h) for h in range(1, Z - 1)] + [final]
    def advance(t):
        for i, st in enumerate(stages):
            if 0 <= t - i < n: st(t - i)
    def rowsum(v):
        return jnp.sum(v.astype(f32), axis=0, keepdims=True)

    cotf = cot[...].astype(f32)
    gdown = (cotf * mod(5)).astype(bf16)
    sums_down = owner_sums(rowsum(gdown))
    group = owners // 4
    wide = ff // 4
    for i in range(4):
        made = tdot(act[:, i * wide : (i + 1) * wide], gdown)
        for j in range(group):
            o = i * group + j
            for b in range(2):
                at = j * 2 * rows + b * rows
                g[(*slot(o), slice(None), slice(b * d_model, (b + 1) * d_model))] = made[at : at + rows].astype(bf16)
    stage0(0)
    stage0(1)
    v, inv_one = norm(lat[...].astype(f32))
    norm_one[...] = v
    resid_v = lat[...].astype(f32) + mod(2) * attn_proj[...]
    n2, inv_two = norm(resid_v)
    norm_two[...] = n2
    left[...] = (n2 * (1.0 + mod(4)) + mod(3)).T.astype(bf16)
    load(0, loads[0]).wait()
    step = 512
    for i in range(ff // step):
        span = slice(i * step, (i + 1) * step)
        u = upv[:, span]
        th = jnp.tanh(GELU * (u + 0.044715 * (u * u * u)))
        slope = 0.5 * (1.0 + th) + 0.5 * u * (1.0 - th * th) * (GELU * (1.0 + 3.0 * 0.044715 * (u * u)))
        gu[:, span] = (dott(gdown, w1[span, :]) * slope).astype(bf16)
    for i, pair_ in enumerate(late): load(2 + i, pair_).start()
    advance(0)
    base = 2 * d_model
    fold(base, gu, ff // 4, 0)
    stage0(2)
    advance(1)
    fold(base, gu, ff // 4, ff // 4)
    stage0(3)
    sums_up = owner_sums(rowsum(gu[...]))
    load(1, loads[1]).wait()
    gmlp = dott(gu[...], w2[...])
    gmod[4:5, :] = rowsum(gmlp * norm_two[...])
    gmod[3:4, :] = rowsum(gmlp)
    gmod[5:6, :] = ggate[...]
    gres = cot[...].astype(f32) + norm_grad(gmlp * (1.0 + mod(4)), norm_two[...], inv_two)
    resid[...] = gres
    gmod[2:3, :] = rowsum(gres * attn_proj[...])
    gproj = (gres * mod(2)).astype(bf16)
    sums_out = owner_sums(rowsum(gproj))
    advance(2)
    left[...] = mixed[...].astype(f32).T.astype(bf16)
    gu[:, 0:d_model] = gproj
    base += ff // 2
    fold(base, gu.at[:, 0:d_model], d_model // 2, 0)
    stage0(4)
    for i, pair_ in enumerate(late): load(2 + i, pair_).wait()
    gmix = dott(gproj, w1[3 * d_model : 4 * d_model, :]).astype(bf16)
    gu[:, d_model : 2 * d_model] = gmix
    scale = HD ** (-0.5)
    lanes = lax.broadcasted_iota(jnp.int32, (1, 2 * HD), 1)
    def heads(i, carry):
        at = pl.multiple_of(i * 2 * HD, 128)
        qp = proj[:, pl.ds(at, 2 * HD)]
        kp = proj[:, pl.ds(pl.multiple_of(d_model + i * 2 * HD, 128), 2 * HD)]
        vp = proj[:, pl.ds(pl.multiple_of(2 * d_model + i * 2 * HD, 128), 2 * HD)]
        gp = gu[:, pl.ds(pl.multiple_of(d_model + i * 2 * HD, 128), 2 * HD)]
        dq = dk = dv = None
        for j in range(2):
            own = (lanes // HD) == j
            q_j, k_j, g_j = (jnp.where(own, m, jnp.zeros_like(m)) for m in (qp, kp, gp))
            e = jnp.exp(dott(q_j, kp) * scale)
            soft = e / jnp.sum(e, axis=-1, keepdims=True)
            gs_ = dott(g_j, vp)
            delta = jnp.sum(soft * gs_, axis=-1, keepdims=True)
            ds_ = (soft * (gs_ - delta)).astype(bf16)
            a = jnp.dot(ds_, k_j, preferred_element_type=f32)
            b = tdot(ds_, q_j)
            c_ = tdot(soft.astype(bf16), g_j)
            dq, dk, dv = (a, b, c_) if dq is None else (dq + a, dk + b, dv + c_)
        gt[:, pl.ds(at, 2 * HD)] = (dq * scale).astype(bf16)
        gt[:, pl.ds(pl.multiple_of(d_model + i * 2 * HD, 128), 2 * HD)] = (dk * scale).astype(bf16)
        gt[:, pl.ds(pl.multiple_of(2 * d_model + i * 2 * HD, 128), 2 * HD)] = dv.astype(bf16)
        return carry
    lax.fori_loop(0, d_model // (2 * HD), heads, 0)
    advance(3)
    left[...] = (norm_one[...] * (1.0 + mod(1)) + mod(0)).T.astype(bf16)
    base += d_model // 2
    first = cuts[5][1]
    fold(base, gt, first, 0)
    stage0(5)
    advance(4)
    fold(base, gt, 3 * d_model // 2 - first, first)
    tail_at = pl.ds(base + 3 * d_model // 2, 128)
    sums = (
        owner_sums(rowsum(gt[:, 0:d_model])), owner_sums(rowsum(gt[:, 2 * d_model : 3 * d_model])),
        sums_out, sums_down, sums_up,
    )
    fill = jnp.zeros((rows - len(sums), 128), f32)
    for o in range(owners):
        g[(*slot(o), slice(None), tail_at)] = jnp.concatenate([m[o : o + 1] for m in sums] + [fill], axis=0).astype(bf16)
    stage0(6)
    advance(5)
    gain = None
    for j in range(3):
        part = dott(gt[:, j * d_model : (j + 1) * d_model], w1[j * d_model : (j + 1) * d_model, :])
        gain = part if gain is None else gain + part
    gmod[1:2, :] = rowsum(gain * norm_one[...])
    gmod[0:1, :] = rowsum(gain)
    gmod[6:8, :] = jnp.zeros((2, d_model), f32)
    glat[...] = resid[...] + norm_grad(gain * (1.0 + mod(1)), norm_one[...], inv_one)
    hand_over(1)
    for k in range(1, owners):
        rc(gmod, gm.at[owner], gs.at[k], gr.at[k], other(k)).start()
    gm[owner] = gmod[...]
    advance(6)
    advance(7)
    conditioning()
    for t in range(8, n + len(stages) - 1):
        advance(t)
    for k in range(n): drain(k)
    finish()


def backward(lat, cot, mods, proj, mixed, attn_proj, upv, act, outp, ggate, wada, silu_t, weights, F):
    d_model, ff = lat.shape[1], act.shape[1]
    owners = 2 * F
    rows = wada.shape[0]
    Z = F // 4
    Zh = Z // 2
    q_half = 3 * d_model // 2
    first = 128 * -(-q_half // 256)
    cuts = []
    for size in (d_model, d_model, ff // 4, ff // 4, d_model // 2, first, q_half - first + 128):
        cuts.append((sum(c[1] for c in cuts), size))
    n = len(cuts)
    width = sum(c[1] for c in cuts)
    tokens = lat.shape[0]
    D = pltpu.SemaphoreType.DMA
    f32, bf16 = jnp.float32, jnp.bfloat16
    hbm, vm = pl.BlockSpec(memory_space=pl.ANY), pl.BlockSpec(memory_space=pltpu.VMEM)
    half = (2, tokens // 2, d_model)
    return pl.pallas_call(
        functools.partial(backward_kernel, F, cuts),
        out_shape=[
            jax.ShapeDtypeStruct((rows, width), f32),
            jax.ShapeDtypeStruct(half, outp.dtype),
            jax.ShapeDtypeStruct(half, f32),
            jax.ShapeDtypeStruct((silu_t.shape[0], 6 * d_model), f32),
            jax.ShapeDtypeStruct((1, 6 * d_model), f32),
            jax.ShapeDtypeStruct((F, 8, 128), f32),
        ],
        in_specs=[vm] * 8 + [hbm] + [vm] * 3 + [hbm] * 4,
        out_specs=[vm, hbm, hbm, vm, vm, vm],
        scratch_shapes=[
            pltpu.VMEM((Zh, 2, 2, 2, 2, rows, width), bf16),
            pltpu.VMEM((Zh, 2, 2, 2, rows, width), bf16),
            pltpu.VMEM((Zh, 2, 2, rows, width), bf16),
            pltpu.VMEM((Zh, 2, rows, width), bf16),
            pltpu.VMEM((Z, rows, width), bf16),
            pltpu.VMEM((Z, rows, width), bf16),
            pltpu.VMEM((owners, 8, d_model), f32),
            pltpu.VMEM((F, 8, 128), f32),
            pltpu.VMEM((ff, d_model), bf16),
            pltpu.VMEM((d_model, ff), bf16),
            pltpu.VMEM((tokens, ff), bf16),
            pltpu.VMEM((tokens, 3 * d_model), bf16),
            pltpu.VMEM((tokens, d_model), f32),
            pltpu.VMEM((tokens, d_model), f32),
            pltpu.VMEM((tokens, d_model), f32),
            pltpu.VMEM((8, d_model), f32),
            pltpu.VMEM((d_model, tokens), bf16),
            pltpu.VMEM((tokens, d_model), f32),
            D((n,)), D((n,)), D((n, 2)), D((n, 2)), D((n, 2)), D((n, 2)), D((n, 2, Z)), D((n, 2, Z)),
            D((owners,)), D((owners,)), D((F,)), D((F,)), D((2,)), D((2,)), D((2,)), D((6,)),
        ],
        compiler_params=pltpu.CompilerParams(
            collective_id=1, has_side_effects=True, vmem_limit_bytes=62 * 2**20
        ),
        name="backward_and_scatter",
    )(lat, cot, mods, proj, mixed, attn_proj, upv, act, outp, ggate, wada, silu_t, *weights)


def body_fast(
    latents,
    condition,
    cotangent,
    w_ada,
    b_ada,
    w_qkv,
    b_query,
    b_value,
    w_out,
    b_out,
    w_up,
    b_up,
    w_down,
    b_down,
):
    f32 = jnp.float32
    bf16 = jnp.bfloat16
    F = lax.axis_size("fsdp")
    owners = F * lax.axis_size("sp")
    sp_index = lax.axis_index("sp")
    own_latents = 1
    tokens_all = latents.shape[1] * 2
    scale_factor = HD ** (-0.5)
    rows = w_qkv.shape[0]
    cond = jnp.pad(
        condition.astype(f32).reshape(2, F, rows).transpose(1, 0, 2), ((0, 0), (0, 6), (0, 128 - rows))
    )
    vectors = (b_query, b_value, b_out, b_down, b_up, b_ada)
    width = sum(part.size for part in vectors)
    bias = jnp.pad(jnp.concatenate(vectors).astype(f32), (0, -width % 1024)).reshape(-1, 128)
    qkv_full, out_full, up_full, down_full, cond_all, bias_all, modulate, inputs, grad_out = gather(
        (w_qkv, w_out, w_up, w_down), cond, bias, latents, cotangent, w_ada, F
    )
    bias_all = bias_all.reshape(F, -1)
    pieces = []
    start = 0
    for part in vectors:
        pieces.append(bias_all[:, start : start + part.size].reshape(-1))
        start = start + part.size
    query_bias, value_bias, out_bias, down_bias, up_bias, ada_bias = pieces
    lat_all, cot_all = inputs, grad_out
    inputs = inputs.astype(f32)[None]
    grad_out = grad_out.astype(f32)[None]
    modulate = modulate + ada_bias
    mod_parts = modulate.reshape(own_latents, 6, 1, D)
    shift_one, scale_one, gate_one = (mod_parts[:, 0], mod_parts[:, 1], mod_parts[:, 2])
    shift_two, scale_two, gate_two = (mod_parts[:, 3], mod_parts[:, 4], mod_parts[:, 5])

    normed_one, inverse_one = normalize(inputs)
    attn_in = (normed_one * (1.0 + scale_one) + shift_one).astype(bf16)
    qkv_bias = jnp.concatenate([query_bias, jnp.zeros_like(query_bias), value_bias]).astype(f32)
    projected = (
        jnp.einsum("btd,de->bte", attn_in, qkv_full, preferred_element_type=f32) + qkv_bias
    ).astype(bf16)
    heads = projected.reshape(own_latents, tokens_all, 3, H, HD).transpose(2, 0, 3, 1, 4)
    queries, key_heads, value_heads = heads[0], heads[1], heads[2]
    scores = (
        jnp.einsum("bhqd,bhkd->bhqk", queries, key_heads, preferred_element_type=f32) * scale_factor
    )
    log_total = jnp.log(jnp.sum(jnp.exp(scores), axis=-1, keepdims=True))
    soft_float = jnp.exp(scores - log_total)
    soft_half = soft_float.astype(bf16)
    mixed = jnp.einsum("bhqk,bhkd->bhqd", soft_half, value_heads, preferred_element_type=f32).astype(
        bf16
    )
    mixed_tokens = mixed.transpose(0, 2, 1, 3).reshape(own_latents, tokens_all, D)
    attn_proj = jnp.einsum(
        "btd,de->bte", mixed_tokens, out_full, preferred_element_type=f32
    ) + out_bias.astype(f32)
    residual = inputs + gate_one * attn_proj
    normed_two, inverse_two = normalize(residual)
    mlp_in = (normed_two * (1.0 + scale_two) + shift_two).astype(bf16)
    up_value = jnp.einsum(
        "btd,df->btf", mlp_in, up_full, preferred_element_type=f32
    ) + up_bias.astype(f32)
    activated = gelu_tanh(up_value).astype(bf16)
    down_value = jnp.einsum(
        "btf,fd->btd", activated, down_full, preferred_element_type=f32
    ) + down_bias.astype(f32)
    output = (residual + gate_two * down_value).astype(bf16)

    grad_gate_two = jnp.sum(grad_out * down_value, axis=1)
    r2 = rows // 2
    stack = w_down.shape[0] // rows
    cond_rows = cond_all[:, :2, :rows].reshape(owners, 2, r2)
    silu_rows = jax.nn.silu(lax.dynamic_index_in_dim(cond_rows, sp_index, 1, False))
    mods = jnp.pad(modulate.reshape(6, D), ((0, 2), (0, 0)))
    owned, output, grad_latents, own_ada, own_bada, grad_silu = backward(
        lat_all, cot_all, mods, projected[0], mixed_tokens[0], attn_proj[0], up_value[0], activated[0],
        output[0], grad_gate_two, w_ada, silu_rows.T, (qkv_full, out_full, up_full, down_full), F
    )

    def unfold(part):
        return jnp.concatenate([part[:r2], part[r2:]], axis=1)

    start = 2 * D
    own_down = jnp.concatenate([owned[:, :D], owned[:, D:start]], axis=0)
    own = []
    for width in (w_up.shape[1] // 2, D // 2, 3 * D // 2):
        own.append(unfold(owned[:, start : start + width]))
        start = start + width
    own_up, own_out, own_qkv = own
    own_bias = [owned[i, start : start + size // 2] for i, size in enumerate((rows, rows, rows, rows, b_up.shape[0]))]
    own_gb_query, own_gb_value, own_gb_out, own_gb_down, own_gb_up = own_bias
    own_gb_ada = lax.dynamic_index_in_dim(
        own_bada.reshape(owners, -1), lax.axis_index("fsdp") * 2 + sp_index, 0, False
    )
    grad_silu = grad_silu[:, :2, :rows].transpose(1, 0, 2).reshape(2, -1)
    grad_condition = silu_back(condition.astype(f32), grad_silu)
    return (
        output,
        grad_latents,
        grad_condition,
        own_ada,
        own_gb_ada,
        own_qkv,
        own_gb_query,
        own_gb_value,
        own_out,
        own_gb_out,
        own_up,
        own_gb_up,
        own_down,
        own_gb_down,
    )


def choose(*args):
    latents, w_qkv, w_down = args[0], args[5], args[12]
    fits = (
        lax.axis_size("sp") == 2
        and lax.axis_size("fsdp") % 8 == 0
        and latents.shape[0] == 2
        and latents.shape[1] % 128 == 0
        and w_qkv.shape[0] % 16 == 0
        and w_qkv.shape[0] <= 128
        and w_down.shape[0] % 64 == 0
        and w_down.shape[0] == 4 * w_qkv.shape[0]
    )
    return (body_fast if fits else body_general)(*args)


def solution(mesh):
    in_specs = (
        P("fsdp", "sp", None),
        P("fsdp", None),
        P("fsdp", "sp", None),
        P("fsdp", None),
        P("fsdp"),
        P("fsdp", None),
        P("fsdp"),
        P("fsdp"),
        P("fsdp", None),
        P("fsdp"),
        P("fsdp", None),
        P("fsdp"),
        P("fsdp", None),
        P("fsdp"),
    )
    out_specs = (
        P("fsdp", "sp", None),
        P("fsdp", "sp", None),
        P("fsdp", None),
        P(("fsdp", "sp"), None),
        P(("fsdp", "sp")),
        P(("fsdp", "sp"), None),
        P(("fsdp", "sp")),
        P(("fsdp", "sp")),
        P(("fsdp", "sp"), None),
        P(("fsdp", "sp")),
        P(("fsdp", "sp"), None),
        P(("fsdp", "sp")),
        P(("fsdp", "sp"), None),
        P(("fsdp", "sp")),
    )
    return jax.shard_map(choose, mesh=mesh, in_specs=in_specs, out_specs=out_specs, check_vma=False)
```

```python
import functools

import jax
import jax.numpy as jnp
from jax import lax
from jax.experimental import pallas as pl
from jax.experimental.pallas import tpu as pltpu
from jax.sharding import PartitionSpec as P

D = 768
H = 12
HD = 64


eps = 1e-06


def normalize(values):
    centered = values - jnp.mean(values, axis=-1, keepdims=True)
    inverse = lax.rsqrt(jnp.mean(centered * centered, axis=-1, keepdims=True) + eps)
    return (centered * inverse, inverse)


def norm_back(grad_in, normed, inverse):
    return inverse * (
        grad_in
        - jnp.mean(grad_in, axis=-1, keepdims=True)
        - normed * jnp.mean(grad_in * normed, axis=-1, keepdims=True)
    )


def gelu_tanh(values):
    return jax.nn.gelu(values, approximate=True)


def silu_back(values, grad_out):
    return jax.vjp(jax.nn.silu, values)[1](grad_out)[0]


def gelu_back(values, grad_out):
    return jax.vjp(gelu_tanh, values)[1](grad_out)[0]


LANES = 2048


def body_general(
    latents,
    condition,
    cotangent,
    w_ada,
    b_ada,
    w_qkv,
    b_query,
    b_value,
    w_out,
    b_out,
    w_up,
    b_up,
    w_down,
    b_down,
):
    f32 = jnp.float32
    bf16 = jnp.bfloat16
    fsdp_count = lax.axis_size("fsdp")
    sp_count = lax.axis_size("sp")
    owners = fsdp_count * sp_count
    fsdp_index = lax.axis_index("fsdp")
    sp_index = lax.axis_index("sp")
    owner_index = fsdp_index * sp_count + sp_index
    pair_latents = latents.shape[0]
    own_latents = pair_latents // sp_count
    latent_total = pair_latents * fsdp_count
    tokens_all = latents.shape[1] * sp_count
    scale_factor = HD ** (-0.5)

    small = [condition.reshape(-1), b_ada, b_query, b_value, b_out, b_up, b_down]
    width = sum(part.size for part in small)
    padded = -(-width // LANES) * LANES
    small.append(jnp.zeros((padded - width,), bf16))
    small_all = lax.all_gather(
        jnp.concatenate(small).reshape(1, padded // 128, 128), "fsdp", axis=0, tiled=True
    ).reshape(fsdp_count, padded)
    pieces = []
    start = 0
    for part in small[:-1]:
        pieces.append(small_all[:, start : start + part.size].reshape(-1))
        start = start + part.size
    cond_all, ada_bias, query_bias, value_bias, out_bias, up_bias, down_bias = pieces
    cond_all = cond_all.reshape(latent_total, D).astype(f32)
    silu_all = jax.nn.silu(cond_all)

    inputs = lax.all_to_all(latents, "sp", split_axis=0, concat_axis=1, tiled=True).astype(f32)
    grad_out = lax.all_to_all(cotangent, "sp", split_axis=0, concat_axis=1, tiled=True).astype(f32)

    ada_rows = w_ada.shape[0]
    silu_mine = lax.dynamic_index_in_dim(
        silu_all.astype(bf16).reshape(fsdp_count, sp_count, own_latents, D), sp_index, 1, False
    )
    silu_mine = lax.dynamic_index_in_dim(
        silu_mine.reshape(fsdp_count * own_latents, fsdp_count, ada_rows), fsdp_index, 1, False
    )
    mod_part = jnp.dot(silu_mine, w_ada, preferred_element_type=f32)
    mod_part = lax.all_to_all(
        mod_part.reshape(fsdp_count, own_latents * 6 * D), "fsdp", split_axis=0, concat_axis=0, tiled=True
    )
    modulate = jnp.sum(mod_part, axis=0).reshape(own_latents, 6 * D) + ada_bias.astype(f32)
    mod_parts = modulate.reshape(own_latents, 6, 1, D)
    shift_one, scale_one, gate_one = (mod_parts[:, 0], mod_parts[:, 1], mod_parts[:, 2])
    shift_two, scale_two, gate_two = (mod_parts[:, 3], mod_parts[:, 4], mod_parts[:, 5])

    qkv_full = lax.all_gather(w_qkv, "fsdp", axis=0, tiled=True)
    out_full = lax.all_gather(w_out, "fsdp", axis=0, tiled=True)
    up_full = lax.all_gather(w_up, "fsdp", axis=0, tiled=True)
    down_full = lax.all_gather(w_down, "fsdp", axis=0, tiled=True)

    normed_one, inverse_one = normalize(inputs)
    attn_in = (normed_one * (1.0 + scale_one) + shift_one).astype(bf16)
    qkv_bias = jnp.concatenate([query_bias, jnp.zeros_like(query_bias), value_bias]).astype(f32)
    projected = (
        jnp.einsum("btd,de->bte", attn_in, qkv_full, preferred_element_type=f32) + qkv_bias
    ).astype(bf16)
    heads = projected.reshape(own_latents, tokens_all, 3, H, HD).transpose(2, 0, 3, 1, 4)
    queries, key_heads, value_heads = heads[0], heads[1], heads[2]
    scores = (
        jnp.einsum("bhqd,bhkd->bhqk", queries, key_heads, preferred_element_type=f32) * scale_factor
    )
    log_total = jnp.log(jnp.sum(jnp.exp(scores), axis=-1, keepdims=True))
    soft_float = jnp.exp(scores - log_total)
    soft_half = soft_float.astype(bf16)
    mixed = jnp.einsum("bhqk,bhkd->bhqd", soft_half, value_heads, preferred_element_type=f32).astype(
        bf16
    )
    mixed_tokens = mixed.transpose(0, 2, 1, 3).reshape(own_latents, tokens_all, D)
    attn_proj = jnp.einsum(
        "btd,de->bte", mixed_tokens, out_full, preferred_element_type=f32
    ) + out_bias.astype(f32)
    residual = inputs + gate_one * attn_proj
    normed_two, inverse_two = normalize(residual)
    mlp_in = (normed_two * (1.0 + scale_two) + shift_two).astype(bf16)
    up_value = jnp.einsum(
        "btd,df->btf", mlp_in, up_full, preferred_element_type=f32
    ) + up_bias.astype(f32)
    activated = gelu_tanh(up_value).astype(bf16)
    down_value = jnp.einsum(
        "btf,fd->btd", activated, down_full, preferred_element_type=f32
    ) + down_bias.astype(f32)
    output = (residual + gate_two * down_value).astype(bf16)
    output = lax.all_to_all(output, "sp", split_axis=1, concat_axis=0, tiled=True)

    grad_gate_two = jnp.sum(grad_out * down_value, axis=1)
    grad_down = (grad_out * gate_two).astype(bf16)
    gw_down = jnp.einsum("btf,btd->fd", activated, grad_down, preferred_element_type=f32)
    gb_down = jnp.sum(grad_down.astype(f32), axis=(0, 1))
    grad_act = jnp.einsum("btd,fd->btf", grad_down, down_full, preferred_element_type=f32)
    grad_up = gelu_back(up_value, grad_act).astype(bf16)
    gw_up = jnp.einsum("btd,btf->df", mlp_in, grad_up, preferred_element_type=f32)
    gb_up = jnp.sum(grad_up.astype(f32), axis=(0, 1))
    grad_mlp = jnp.einsum("btf,df->btd", grad_up, up_full, preferred_element_type=f32)
    grad_scale_two = jnp.sum(grad_mlp * normed_two, axis=1)
    grad_shift_two = jnp.sum(grad_mlp, axis=1)
    grad_resid = grad_out + norm_back(grad_mlp * (1.0 + scale_two), normed_two, inverse_two)
    grad_gate_one = jnp.sum(grad_resid * attn_proj, axis=1)
    grad_proj = (grad_resid * gate_one).astype(bf16)
    gw_out = jnp.einsum("btd,bte->de", mixed_tokens, grad_proj, preferred_element_type=f32)
    gb_out = jnp.sum(grad_proj.astype(f32), axis=(0, 1))
    grad_mixed = jnp.einsum("bte,de->btd", grad_proj, out_full, preferred_element_type=f32).astype(
        bf16
    )
    grad_heads = grad_mixed.reshape(own_latents, tokens_all, H, HD).transpose(0, 2, 1, 3)
    grad_soft = jnp.einsum("bhqd,bhkd->bhqk", grad_heads, value_heads, preferred_element_type=f32)
    delta_sum = jnp.sum(soft_float * grad_soft, axis=-1, keepdims=True)
    grad_scores = (soft_float * (grad_soft - delta_sum)).astype(bf16)
    grad_queries = (
        jnp.einsum("bhqk,bhkd->bhqd", grad_scores, key_heads, preferred_element_type=f32)
        * scale_factor
    ).astype(bf16)
    grad_keys = (
        jnp.einsum("bhqk,bhqd->bhkd", grad_scores, queries, preferred_element_type=f32)
        * scale_factor
    ).astype(bf16)
    grad_values = jnp.einsum(
        "bhqk,bhqd->bhkd", soft_half, grad_heads, preferred_element_type=f32
    ).astype(bf16)
    grad_tokens = (
        jnp.stack([grad_queries, grad_keys, grad_values], axis=0)
        .transpose(1, 3, 0, 2, 4)
        .reshape(own_latents, tokens_all, 3 * D)
    )
    gw_qkv = jnp.einsum("btd,bte->de", attn_in, grad_tokens, preferred_element_type=f32)
    grad_tok_float = grad_tokens.astype(f32)
    gb_query = jnp.sum(grad_tok_float[:, :, :D], axis=(0, 1))
    gb_value = jnp.sum(grad_tok_float[:, :, 2 * D :], axis=(0, 1))
    grad_attn_in = jnp.einsum("bte,de->btd", grad_tokens, qkv_full, preferred_element_type=f32)
    grad_scale_one = jnp.sum(grad_attn_in * normed_one, axis=1)
    grad_shift_one = jnp.sum(grad_attn_in, axis=1)
    grad_latents = grad_resid + norm_back(grad_attn_in * (1.0 + scale_one), normed_one, inverse_one)
    grad_latents = lax.all_to_all(grad_latents, "sp", split_axis=1, concat_axis=0, tiled=True)

    grad_mod = jnp.concatenate(
        [
            grad_shift_one,
            grad_scale_one,
            grad_gate_one,
            grad_shift_two,
            grad_scale_two,
            grad_gate_two,
        ],
        axis=1,
    )
    grad_mod = lax.all_to_all(
        jnp.broadcast_to(grad_mod[None], (owners, own_latents, 6 * D)),
        ("fsdp", "sp"),
        split_axis=0,
        concat_axis=0,
        tiled=True,
    ).reshape(latent_total, 6 * D)

    rows = D // owners
    biases = (gb_query, gb_value, gb_out, gb_up, gb_down)
    bias_rows = jnp.concatenate([part.reshape(owners, -1) for part in biases], axis=1)
    bias_width = bias_rows.shape[1]
    bias_lanes = -(-bias_width // (rows * 128)) * 128
    bias_rows = jnp.pad(bias_rows, ((0, 0), (0, rows * bias_lanes - bias_width)))
    stack = down_full.shape[0] // D
    gw_down = (
        gw_down.astype(bf16)
        .reshape(owners, stack, rows, D)
        .transpose(0, 2, 1, 3)
        .reshape(D, stack * D)
    )
    packed = jnp.concatenate(
        [
            gw_down,
            gw_up.astype(bf16),
            gw_qkv.astype(bf16),
            gw_out.astype(bf16),
            bias_rows.astype(bf16).reshape(D, bias_lanes),
        ],
        axis=1,
    )
    owned = lax.psum_scatter(packed, ("fsdp", "sp"), scatter_dimension=0, tiled=True).astype(f32)
    own_weights = []
    start = 0
    for width in (stack * D, up_full.shape[1], 3 * D, D, bias_lanes):
        own_weights.append(owned[:, start : start + width])
        start = start + width
    own_down, own_up, own_qkv, own_out, bias_sums = own_weights
    own_down = own_down.reshape(rows, stack, D).transpose(1, 0, 2).reshape(stack * rows, D)
    bias_sums = bias_sums.reshape(-1)
    own_bias = []
    start = 0
    for part in biases:
        width = part.size // owners
        own_bias.append(bias_sums[start : start + width])
        start = start + width
    own_gb_query, own_gb_value, own_gb_out, own_gb_up, own_gb_down = own_bias
    silu_rows = lax.dynamic_index_in_dim(
        silu_all.reshape(latent_total, owners, D // owners), owner_index, 1, False
    )
    own_ada = jnp.dot(silu_rows.T, grad_mod, precision=lax.Precision.HIGHEST)
    own_gb_ada = lax.dynamic_index_in_dim(
        jnp.sum(grad_mod, axis=0).reshape(owners, -1), owner_index, 0, False
    )
    grad_silu = jnp.dot(grad_mod.astype(bf16), w_ada.T, preferred_element_type=f32)
    grad_silu = lax.all_to_all(
        grad_silu.reshape(fsdp_count, pair_latents * ada_rows),
        "fsdp",
        split_axis=0,
        concat_axis=0,
        tiled=True,
    )
    grad_silu = (
        grad_silu.reshape(fsdp_count, pair_latents, ada_rows)
        .transpose(1, 0, 2)
        .reshape(pair_latents, D)
    )
    grad_condition = silu_back(condition.astype(f32), grad_silu)
    return (
        output,
        grad_latents,
        grad_condition,
        own_ada,
        own_gb_ada,
        own_qkv,
        own_gb_query,
        own_gb_value,
        own_out,
        own_gb_out,
        own_up,
        own_gb_up,
        own_down,
        own_gb_down,
    )


MESH = pl.DeviceIdType.MESH


class Plan:
    def __init__(self, rows, cols):
        self.rows, self.cols = rows, cols
        self.by_rows = rows % 64 == 0
        n = (rows // 32) if self.by_rows else (cols // 256)
        unit = 16 if self.by_rows else 128
        big = -(-2 * n // 3)
        self.half = n * unit
        self.big = big * unit
        self.unit = unit
    def at(self, ref, row, h=None, q=None):
        rows, cols, unit = self.rows, self.cols, self.unit
        if h is None:
            return ref.at[pl.ds(pl.multiple_of(row, 16), rows), :]
        start = h * self.half + (self.big if q == 1 else 0)
        size = self.half if q is None else (self.big if q == 0 else self.half - self.big)
        if self.by_rows:
            return ref.at[pl.ds(pl.multiple_of(row + start, 16), size), :]
        return ref.at[pl.ds(pl.multiple_of(row, 16), rows), pl.ds(pl.multiple_of(start, 128), size)]

GELU = 0.7978845608028654


def block_kernel(F, plans, cuts, *refs):
    n = len(cuts)
    w = len(plans)
    f32, bf16 = jnp.float32, jnp.bfloat16
    ins, (cond, lat, cot, wada), vectors = refs[:w], refs[w : w + 4], refs[w + 4 : w + 10]
    outs, refs = refs[w + 10 : 2 * w + 10], refs[2 * w + 10 :]
    (
        outp_own, glat_own, own_down, own_up, own_out, own_qkv, own_bias, ada, bada, gcond,
        cond_all, bias, bias_all, part, parts, mods, vec, lat_all, cot_all, proj, mixed, attn_proj, upv, act, outp,
        acc, silu, g, r0, r1, r2, up, dn, gm, cpart, w1, w2, gu, gt, norm_one, norm_two, resid, gmod, left,
        zs, zr, xs, xr, ys, yr, xds, xdr, yds, ydr, ss, sr, gloc, ges, ger, ps, pr,
        s0, q0, s1, q1, s2, q2, s3, q3, gs, gr, ks, kr, es, er, loc, wl,
    ) = refs
    f = lax.axis_index("fsdp"); x = lax.axis_index("sp")
    c = f % 2; y = (f // 2) % 2; z = f // 4; Z = F // 4; Zh = Z // 2
    owners = 2 * F
    owner = f * 2 + x
    rows = plans[0].rows
    half = rows // 2
    d_model, ff = lat_all.shape[1], act.shape[1]
    def dev(x_, y_, z_, c_):
        return ((z_ * 2 + y_) * 2 + c_, x_)
    xn, yn, sib = dev(1 - x, y, z, c), dev(x, 1 - y, z, c), dev(x, y, z, 1 - c)
    zu, zd = dev(x, y, z + 1, c), dev(x, y, z - 1, c)
    def peer(k):
        return (lax.rem(f + k, F), x)
    def other(k):
        o = lax.rem(owner + k, owners)
        return (o // 2, o % 2)
    bar = pltpu.get_barrier_semaphore()
    for k in range(1, owners):
        pl.semaphore_signal(bar, inc=1, device_id=other(k), device_id_type=MESH)
    bias[...] = jnp.zeros_like(bias)
    layout = []
    row = 0
    for ref in vectors:
        size = ref.shape[1]
        layout.append((row, size))
        for at in range(0, size, 128):
            bias[row : row + 1, 0 : min(128, size - at)] = ref[:, at : min(at + 128, size)].astype(f32)
            row += 1
    pl.semaphore_wait(bar, owners - 1)

    sends = []
    def send(ok, build):
        if ok is None:
            build().start()
        else:
            pl.when(ok)(lambda: build().start())
        sends.append((ok, build))
    def rc(src, dst, s, r, d):
        return pltpu.make_async_remote_copy(src_ref=src, dst_ref=dst, send_sem=s, recv_sem=r, device_id=d, device_id_type=MESH)

    def base(m, y_, z_, c_=c):
        return ((z_ * 2 + y_) * 2 + c_) * plans[m].rows
    def piece(m, y_, z_, h=None, q=None, c_=None):
        return plans[m].at(outs[m], base(m, y_, z_, c if c_ is None else c_), h, q)
    def mine(m, h=None, q=None):
        return plans[m].at(ins[m], 0, h, q)
    def to_sib(m, ok, kind, y_, z_, h=None, q=None, own=False):
        send(ok, lambda: rc(mine(m, h, q) if own else piece(m, y_, z_, h, q), piece(m, y_, z_, h, q),
                              ss.at[m, kind, z_], sr.at[m, kind, z_], sib))
    def arrived(m, ok, sem_s, sem_r, *where, c_=None):
        def go():
            p = piece(m, *where, c_=c_)
            rc(p, p, sem_s, sem_r, xn).wait_recv()
        if ok is None: go()
        else: pl.when(ok)(go)

    def start_own(m):
        send(None, lambda: rc(mine(m, x), piece(m, y, z, x), ys.at[m, z], yr.at[m, z], yn))
        send(z + 1 < Z, lambda: rc(mine(m, x), piece(m, y, z, x), zs.at[m, 0, z], zr.at[m, z], zu))
        send(z > 0, lambda: rc(mine(m, x), piece(m, y, z, x), zs.at[m, 1, z], zr.at[m, z], zd))
        send(None, lambda: rc(mine(m, 1 - x, 1), piece(m, y, z, 1 - x, 1), yds.at[m, z], ydr.at[m, z], yn))
        to_sib(m, None, 0, y, z, own=True)
        pltpu.make_async_copy(mine(m), piece(m, y, z), gloc.at[m]).start()

    def z_round(m, d):
        for sign in (-1, 1):
            o = z + sign * d
            ok = (o >= 0) if sign < 0 else (o < Z)
            arrived(m, ok, zs.at[m, 0, o], zr.at[m, o], y, o, x)
            if sign < 0:
                send(ok & (z + 1 < Z), lambda o=o: rc(piece(m, y, o, x), piece(m, y, o, x), zs.at[m, 0, o], zr.at[m, o], zu))
            else:
                send(ok & (z > 0), lambda o=o: rc(piece(m, y, o, x), piece(m, y, o, x), zs.at[m, 1, o], zr.at[m, o], zd))
            send(ok, lambda o=o: rc(piece(m, y, o, x), piece(m, y, o, x), xs.at[m, o], xr.at[m, o], xn))
            send(ok, lambda o=o: rc(piece(m, y, o, x), piece(m, y, o, x), ys.at[m, o], yr.at[m, o], yn))
            to_sib(m, ok, 0, y, o, x)

    def xy_round(m, d):
        for sign in ((-1, 1) if d else (0,)):
            o = z + sign * d
            ok = None if d == 0 else ((o >= 0) if sign < 0 else (o < Z))
            arrived(m, ok, ys.at[m, o], yr.at[m, o], 1 - y, o, x)
            send(ok, lambda o=o: rc(piece(m, 1 - y, o, x, 0), piece(m, 1 - y, o, x, 0), xds.at[m, o], xdr.at[m, o], xn))
            to_sib(m, ok, 2, 1 - y, o, x)
            if d:
                arrived(m, ok, xs.at[m, o], xr.at[m, o], y, o, 1 - x)
                send(ok, lambda o=o: rc(piece(m, y, o, 1 - x, 1), piece(m, y, o, 1 - x, 1), yds.at[m, o], ydr.at[m, o], yn))
                to_sib(m, ok, 1, y, o, 1 - x)

    def last_round(m, d):
        for sign in ((-1, 1) if d else (0,)):
            o = z + sign * d
            ok = None if d == 0 else ((o >= 0) if sign < 0 else (o < Z))
            arrived(m, ok, xds.at[m, o], xdr.at[m, o], 1 - y, o, 1 - x, 0)
            to_sib(m, ok, 3, 1 - y, o, 1 - x, 0)
            arrived(m, ok, yds.at[m, o], ydr.at[m, o], 1 - y, o, 1 - x, 1)
            to_sib(m, ok, 4, 1 - y, o, 1 - x, 1)

    def landed(m):
        pltpu.make_async_copy(mine(m), piece(m, y, z), gloc.at[m]).wait()
        b = 1 - c
        arrived(m, None, ss.at[m, 0, z], sr.at[m, 0, z], y, z, c_=b)
        for d in range(Z):
            for sign in ((-1, 1) if d else (0,)):
                o = z + sign * d
                ok = None if d == 0 else ((o >= 0) if sign < 0 else (o < Z))
                if d:
                    arrived(m, ok, ss.at[m, 0, o], sr.at[m, 0, o], y, o, x, c_=b)
                    arrived(m, ok, ss.at[m, 1, o], sr.at[m, 1, o], y, o, 1 - x, c_=b)
                arrived(m, ok, ss.at[m, 2, o], sr.at[m, 2, o], 1 - y, o, x, c_=b)
                arrived(m, ok, ss.at[m, 3, o], sr.at[m, 3, o], 1 - y, o, 1 - x, 0, c_=b)
                arrived(m, ok, ss.at[m, 4, o], sr.at[m, 4, o], 1 - y, o, 1 - x, 1, c_=b)

    def col(k):
        return pl.ds(*cuts[k])
    def c0(k):
        return rc(g.at[:, :, :, 1 - c, :, :, col(k)], r0.at[:, :, :, :, :, col(k)], s0.at[k], q0.at[k], sib)
    def c1(k, p):
        if p == 0:
            return rc(r0.at[:, 0, :, 1 - x, :, col(k)], r1.at[:, 0, :, :, col(k)], s1.at[k, 0], q1.at[k, 0], xn)
        return rc(r0.at[:, 1, 1 - y, :, :, col(k)], r1.at[:, 1, :, :, col(k)], s1.at[k, 1], q1.at[k, 1], yn)
    def c2(k, p):
        if p == 0:
            return rc(r1.at[:, 0, 1 - y, :, col(k)], r2.at[:, 0, :, col(k)], s2.at[k, 0], q2.at[k, 0], yn)
        return rc(r1.at[:, 1, 1 - x, :, col(k)], r2.at[:, 1, :, col(k)], s2.at[k, 1], q2.at[k, 1], xn)
    def c3(k, o, way, edge):
        buf = dn if way else up
        src = r2.at[o // 2, o % 2, :, col(k)] if edge else buf.at[o, :, col(k)]
        return rc(src, buf.at[o, :, col(k)], s3.at[k, way, o], q3.at[k, way, o], zd if way else zu)

    def stage0(k):
        c0(k).start()
    def stage1(k):
        c0(k).wait_recv()
        for p in (0, 1):
            for zh in range(Zh):
                for j in range(2):
                    at = (zh, 0, j, 1 - x) if p == 0 else (zh, 1, 1 - y, j)
                    own = g[at[0], at[1], at[2], c, at[3], :, col(k)].astype(f32)
                    r0[(*at, slice(None), col(k))] = (r0[(*at, slice(None), col(k))].astype(f32) + own).astype(bf16)
            c1(k, p).start()
    def pair(k, at):
        return g[at[0], at[1], at[2], c, at[3], :, col(k)].astype(f32) + r0[(*at, slice(None), col(k))].astype(f32)
    def stage2(k):
        for p in (0, 1):
            c1(k, p).wait_recv()
            j = (1 - y) if p == 0 else (1 - x)
            for zh in range(Zh):
                at = (zh, 0, j, x) if p == 0 else (zh, 1, y, j)
                r1[zh, p, j, :, col(k)] = (r1[zh, p, j, :, col(k)].astype(f32) + pair(k, at)).astype(bf16)
            c2(k, p).start()
    def stage3(k):
        for p in (0, 1):
            c2(k, p).wait_recv()
            j = y if p == 0 else x
            for zh in range(Zh):
                mine = r1[zh, p, j, :, col(k)].astype(f32) + pair(k, (zh, p, y, x))
                r2[zh, p, :, col(k)] = (r2[zh, p, :, col(k)].astype(f32) + mine).astype(bf16)
        @pl.when(z == 0)
        def _():
            for o in reversed(range(1, Z)): c3(k, o, 0, True).start()
        @pl.when(z == Z - 1)
        def _():
            for o in range(Z - 1): c3(k, o, 1, True).start()
    def hop(k, h):
        def go(way):
            for o in (reversed(range(h + 1, Z)) if way == 0 else range(Z - 1 - h)):
                buf = dn if way else up
                c3(k, o, way, False).wait_recv()
                buf[o, :, col(k)] = (buf[o, :, col(k)].astype(f32) + r2[o // 2, o % 2, :, col(k)].astype(f32)).astype(bf16)
                c3(k, o, way, False).start()
        pl.when(z == h)(lambda: go(0))
        pl.when(z == Z - 1 - h)(lambda: go(1))
    def final(k):
        acc[:, col(k)] = r2[z // 2, z % 2, :, col(k)].astype(f32)
        @pl.when(z > 0)
        def _():
            c3(k, z, 0, False).wait_recv()
            acc[:, col(k)] += up[z, :, col(k)].astype(f32)
        @pl.when(z < Z - 1)
        def _():
            c3(k, z, 1, False).wait_recv()
            acc[:, col(k)] += dn[z, :, col(k)].astype(f32)
        at, size = cuts[k]
        if k < 2:
            own_down[k * rows : (k + 1) * rows, :] = acc[:, at : at + size]
            return
        ref, begin = ((own_up, 2), (own_up, 2), (own_out, 4), (own_qkv, 5), (own_qkv, 5))[k - 2]
        off = at - cuts[begin][0]
        if k == 6:
            size -= 128
            own_bias[...] = acc[0:8, at + size : at + size + 128]
        wide = ref.shape[1] // 2
        ref[:, off : off + size] = acc[0 : rows // 2, at : at + size]
        ref[:, wide + off : wide + off + size] = acc[rows // 2 : rows, at : at + size]
    def drain(k):
        c0(k).wait_send()
        for p in (0, 1):
            c1(k, p).wait_send(); c2(k, p).wait_send()
        for o in range(Z):
            pl.when(o > z)(lambda o=o: c3(k, o, 0, False).wait_send())
            pl.when(o < z)(lambda o=o: c3(k, o, 1, False).wait_send())

    tokens = outp_own.shape[1]
    def swap(i, a, b):
        return rc(a.at[pl.ds(pl.multiple_of((1 - x) * tokens, 128), tokens), :], b.at[x], es.at[i], er.at[i], xn)
    def keep(i, a, b):
        return pltpu.make_async_copy(a.at[pl.ds(pl.multiple_of(x * tokens, 128), tokens), :], b.at[x], loc.at[i])
    pairs = ((outp, outp_own), (resid, glat_own))
    def hand_over(i):
        swap(i, *pairs[i]).start()
        keep(i, *pairs[i]).start()
    def conditioning():
        for k in range(1, 2 * F):
            rc(gmod, gm.at[lax.rem(owner + 2 * F - k, 2 * F)], gs.at[k], gr.at[k], xn).wait_recv()
        rows = wada.shape[0]
        step = wada.shape[1] // 6
        total = jnp.zeros((2 * F, rows), f32)
        for i in range(F):
            for j in range(2):
                silu[2 * i + j : 2 * i + j + 1, :] = cond_all[i, j : j + 1, :]
        sl = silu[...]
        sl = (sl / (1.0 + jnp.exp(-sl))).T
        sl = jnp.where(x == 0, sl[0 : rows // 2], sl[rows // 2 : rows])
        for j in range(6):
            span = pl.ds(j * step, step)
            block = gm[:, j, :]
            ada[:, span] = jnp.dot(sl, block, precision=lax.Precision.HIGHEST, preferred_element_type=f32)
            bada[:, span] = jnp.sum(block, axis=0, keepdims=True)
            total += lax.dot_general(block.astype(bf16), wada[:, span], (((1,), (1,)), ((), ())), preferred_element_type=f32)
        for i in range(F):
            cpart[i, 0:2, 0:rows] = total[2 * i : 2 * i + 2, :]
        for k in range(1, F):
            rc(cpart.at[peer(k)[0]], gcond.at[f], ks.at[k], kr.at[k], peer(k)).start()
        gcond[f] = cpart[f]
    def finish():
        for k in range(1, F):
            rc(cpart.at[0], gcond.at[lax.rem(f + F - k, F)], ks.at[k], kr.at[k], xn).wait_recv()
            rc(cpart.at[peer(k)[0]], gcond.at[f], ks.at[k], kr.at[k], peer(k)).wait_send()
        for k in range(1, 2 * F):
            rc(gmod, gm.at[owner], gs.at[k], gr.at[k], other(k)).wait_send()
        for i, (a, b) in enumerate(pairs):
            keep(i, a, b).wait()
            swap(i, a, b).wait_send()
            rc(b.at[1 - x], b.at[1 - x], es.at[i], er.at[i], xn).wait_recv()
    def slot(o):
        zo = o // 8
        return (zo // 2, zo % 2, (o // 4) % 2, (o // 2) % 2, o % 2)
    def norm(v):
        v = v - jnp.mean(v, axis=-1, keepdims=True)
        inv = lax.rsqrt(jnp.mean(v * v, axis=-1, keepdims=True) + eps)
        return v * inv, inv
    def norm_grad(gv, nv, inv):
        return inv * (gv - jnp.mean(gv, axis=-1, keepdims=True) - nv * jnp.mean(gv * nv, axis=-1, keepdims=True))
    def tdot(p, q):
        return lax.dot_general(p, q, (((0,), (0,)), ((), ())), preferred_element_type=f32)
    def dott(p, q):
        return lax.dot_general(p, q, (((1,), (1,)), ((), ())), preferred_element_type=f32)
    def mod(i):
        return mods[i : i + 1, :]
    def fold(col0, right, span, first):
        step = 256 if span % 256 == 0 else 128
        def one(i, carry):
            off = first + i * step
            lo = jnp.dot(left[...], right[:, pl.ds(pl.multiple_of(off, 128), step)], preferred_element_type=f32)
            hi_at = right.shape[1] // 2 + off
            hi = jnp.dot(left[...], right[:, pl.ds(pl.multiple_of(hi_at, 128), step)], preferred_element_type=f32)
            to = pl.ds(pl.multiple_of(col0 + off, 128), step)
            for o in range(owners):
                both = jnp.concatenate([lo[o * half : o * half + half], hi[o * half : o * half + half]], axis=0)
                g[(*slot(o), slice(None), to)] = both.astype(bf16)
            return carry
        lax.fori_loop(0, span // step, one, 0)
    def owner_sums(total):
        wide = total.shape[1]
        per = wide // owners
        cols = lax.broadcasted_iota(jnp.int32, (owners, wide), 1)
        begin = lax.broadcasted_iota(jnp.int32, (owners, wide), 0) * per
        mine_ = (cols >= begin) & (cols < begin + per)
        spread = jnp.where(mine_, jnp.broadcast_to(total, (owners, wide)), 0.0).astype(bf16)
        line = lax.broadcasted_iota(jnp.int32, (1, wide), 1)
        pick = jnp.broadcast_to(line - line // per * per, (128, wide)) == lax.broadcasted_iota(jnp.int32, (128, wide), 0)
        return dott(spread, jnp.where(pick, 1.0, 0.0).astype(bf16))

    stages = [stage1, stage2, stage3] + [functools.partial(lambda k, h: hop(k, h), h=h) for h in range(1, Z - 1)] + [final]
    def advance(t):
        for i, st in enumerate(stages):
            if 0 <= t - i < n: st(t - i)
    def rowsum(v):
        return jnp.sum(v.astype(f32), axis=0, keepdims=True)

    def load(i):
        if i == 0:
            pair = (outs[3], w1)
        elif i == 1:
            pair = (outs[2], w2)
        elif i < 5:
            pair = (outs[0].at[:, pl.ds(d_model * (i - 2), d_model)], w1.at[pl.ds(d_model * (i - 2), d_model), :])
        else:
            pair = (outs[1], w1.at[pl.ds(3 * d_model, d_model), :])
        return pltpu.make_async_copy(*pair, wl.at[i])
    own_tokens = lat.shape[1]
    for k in range(1, F):
        to = peer(k)
        rc(cond.at[to[0]], cond_all.at[f], ges.at[0, k], ger.at[0, k], to).start()
        rc(bias, bias_all.at[f], ges.at[1, k], ger.at[1, k], to).start()
    def trade(i, a, b):
        return rc(a.at[1 - x], b.at[pl.ds(pl.multiple_of(x * own_tokens, 128), own_tokens), :], ges.at[2, i], ger.at[2, i], xn)
    def stay(i, a, b):
        return pltpu.make_async_copy(a.at[x], b.at[pl.ds(pl.multiple_of(x * own_tokens, 128), own_tokens), :], gloc.at[w + i])
    given = ((lat, lat_all), (cot, cot_all))
    for i, (a, b) in enumerate(given):
        trade(i, a, b).start()
        stay(i, a, b).start()
    start_own(0)
    start_own(1)
    cond_all[f] = cond[f]
    bias_all[f] = bias[...]
    for k in range(1, F):
        rc(cond.at[0], cond_all.at[lax.rem(f + F - k, F)], ges.at[0, k], ger.at[0, k], xn).wait_recv()
    picked = jnp.where(x == 0, cond_all[:, 0, :], cond_all[:, 1, :])[:, :rows]
    picked = (picked / (1.0 + jnp.exp(-picked))).astype(bf16)
    made = jnp.dot(picked, wada[...], preferred_element_type=f32)
    for i in range(F):
        part[i] = made[i : i + 1, :]
    for k in range(1, F):
        to = peer(k)
        rc(part.at[to[0]], parts.at[f], ps.at[k], pr.at[k], to).start()
    parts[f] = part[f]
    start_own(2)
    def comm(ms, d):
        for m in ms:
            if 0 < d < Z: z_round(m, d)
            if 0 < d <= Z: xy_round(m, d - 1)
            if d > 1: last_round(m, d - 2)
    def assemble(which, lo, hi):
        row, size = layout[which]
        cols = lax.broadcasted_iota(jnp.int32, (1, hi - lo), 1) + lo
        block = cols // size
        place = jnp.broadcast_to(cols - block * size, (128, hi - lo)) - lax.broadcasted_iota(jnp.int32, (128, hi - lo), 0)
        total = None
        for i in range(-(-size // 128)):
            hot = jnp.where(place == i * 128, 1.0, 0.0).astype(bf16)
            term = jnp.dot(bias_all[:, row + i, :].astype(bf16), hot, preferred_element_type=f32)
            total = term if total is None else total + term
        mine_ = jnp.broadcast_to(block, (F, hi - lo)) == lax.broadcasted_iota(jnp.int32, (F, hi - lo), 0)
        return jnp.sum(jnp.where(mine_, total, 0.0), axis=0, keepdims=True)
    comm((0, 1), 1)
    for k in range(1, F):
        rc(bias, bias_all.at[lax.rem(f + F - k, F)], ges.at[1, k], ger.at[1, k], xn).wait_recv()
        rc(part.at[0], parts.at[lax.rem(f + F - k, F)], ps.at[k], pr.at[k], xn).wait_recv()
    for i in range(6):
        span = slice(i * d_model, (i + 1) * d_model)
        mods[i : i + 1, :] = jnp.sum(parts[:, :, span], axis=0) + assemble(5, i * d_model, (i + 1) * d_model)
    comm((0, 1), 2)
    start_own(3)
    places = {}
    at = 0
    for which in (0, 1, 2, 3, 4):
        size = layout[which][1] * F
        places[which] = slice(at, at + size)
        for lo in range(0, size, d_model):
            vec[:, at + lo : at + lo + d_model] = assemble(which, lo, lo + d_model)
        at += size
    def bias_of(which):
        return vec[:, places[which]]
    comm((0, 1), 3)
    for i, (a, b) in enumerate(given):
        stay(i, a, b).wait()
        got = b.at[pl.ds(pl.multiple_of((1 - x) * own_tokens, 128), own_tokens), :]
        rc(got, got, ges.at[2, i], ger.at[2, i], xn).wait_recv()
    v, inv_one = norm(lat_all[...].astype(f32))
    norm_one[...] = v
    gt[:, 0:d_model] = (v * (1.0 + mod(1)) + mod(0)).astype(bf16)
    comm((0, 1), 4)
    comm((2,), 1)
    comm((0, 1), 5)
    for m in (0, 1): landed(m)
    for i in range(2, 6): load(i).start()
    comm((2,), 2)
    for i in range(2, 6): load(i).wait()
    for j in range(3):
        made = jnp.dot(gt[:, 0:d_model], w1[j * d_model : (j + 1) * d_model, :], preferred_element_type=f32)
        if j != 1:
            made = made + bias_of(0 if j == 0 else 1)
        proj[:, j * d_model : (j + 1) * d_model] = made.astype(bf16)
    scale = HD ** (-0.5)
    lanes = lax.broadcasted_iota(jnp.int32, (1, 2 * HD), 1)
    comm((2,), 3)
    def attend(i, carry):
        at = pl.multiple_of(i * 2 * HD, 128)
        qp = proj[:, pl.ds(at, 2 * HD)]
        kp = proj[:, pl.ds(pl.multiple_of(d_model + i * 2 * HD, 128), 2 * HD)]
        vp = proj[:, pl.ds(pl.multiple_of(2 * d_model + i * 2 * HD, 128), 2 * HD)]
        total = None
        for j in range(2):
            own = (lanes // HD) == j
            q_j, v_j = (jnp.where(own, m_, jnp.zeros_like(m_)) for m_ in (qp, vp))
            e = jnp.exp(dott(q_j, kp) * scale)
            soft = e / jnp.sum(e, axis=-1, keepdims=True)
            term = jnp.dot(soft.astype(bf16), v_j, preferred_element_type=f32)
            total = term if total is None else total + term
        mixed[:, pl.ds(at, 2 * HD)] = total.astype(bf16)
        return carry
    pairs_of = d_model // (2 * HD)
    lax.fori_loop(0, pairs_of // 2, attend, 0)
    comm((2,), 4)
    comm((3,), 1)
    lax.fori_loop(pairs_of // 2, pairs_of, attend, 0)
    comm((2,), 5)
    comm((3,), 2)
    attn_proj[...] = jnp.dot(mixed[...], w1[3 * d_model : 4 * d_model, :], preferred_element_type=f32) + bias_of(2)
    resid[...] = lat_all[...].astype(f32) + mod(2) * attn_proj[...]
    n2, inv_two = norm(resid[...])
    norm_two[...] = n2
    n2 = n2 * (1.0 + mod(4)) + mod(3)
    gt[:, 0:d_model] = n2.astype(bf16)
    left[...] = n2.T.astype(bf16)
    landed(2)
    load(1).start()
    comm((3,), 3)
    load(1).wait()
    step = 512
    for i in range(ff // step):
        span = slice(i * step, (i + 1) * step)
        at = places[4].start + i * step
        u = jnp.dot(gt[:, 0:d_model], w2[:, span], preferred_element_type=f32) + vec[:, at : at + step]
        th = jnp.tanh(GELU * (u + 0.044715 * (u * u * u)))
        act[:, span] = (0.5 * u * (1.0 + th)).astype(bf16)
        upv[:, span] = 0.5 * (1.0 + th) + 0.5 * u * (1.0 - th * th) * (GELU * (1.0 + 3.0 * 0.044715 * (u * u)))
        if i == ff // step // 2:
            comm((3,), 4)
    comm((3,), 5)
    landed(3)
    load(0).start()
    load(0).wait()
    down = jnp.dot(act[...], w1[...], preferred_element_type=f32) + bias_of(3)
    outp[...] = (resid[...] + mod(5) * down).astype(bf16)
    hand_over(0)
    gmod[5:6, :] = rowsum(cot_all[...].astype(f32) * down)
    cpart[...] = jnp.zeros_like(cpart)

    cotf = cot_all[...].astype(f32)
    gdown = (cotf * mod(5)).astype(bf16)
    sums_down = owner_sums(rowsum(gdown))
    group = owners // 4
    wide = ff // 4
    for i in range(4):
        made = tdot(act[:, i * wide : (i + 1) * wide], gdown)
        for j in range(group):
            o = i * group + j
            for b in range(2):
                at = j * 2 * rows + b * rows
                g[(*slot(o), slice(None), slice(b * d_model, (b + 1) * d_model))] = made[at : at + rows].astype(bf16)
    stage0(0)
    stage0(1)
    step = 512
    for i in range(ff // step):
        span = slice(i * step, (i + 1) * step)
        gu[:, span] = (dott(gdown, w1[span, :]) * upv[:, span]).astype(bf16)
    for i in range(4): load(2 + i).start()
    advance(0)
    colbase = 2 * d_model
    fold(colbase, gu, ff // 4, 0)
    stage0(2)
    advance(1)
    fold(colbase, gu, ff // 4, ff // 4)
    stage0(3)
    sums_up = owner_sums(rowsum(gu[...]))
    gmlp = dott(gu[...], w2[...])
    gmod[4:5, :] = rowsum(gmlp * norm_two[...])
    gmod[3:4, :] = rowsum(gmlp)
    gres = cot_all[...].astype(f32) + norm_grad(gmlp * (1.0 + mod(4)), norm_two[...], inv_two)
    resid[...] = gres
    gmod[2:3, :] = rowsum(gres * attn_proj[...])
    gproj = (gres * mod(2)).astype(bf16)
    sums_out = owner_sums(rowsum(gproj))
    advance(2)
    left[...] = mixed[...].astype(f32).T.astype(bf16)
    gu[:, 0:d_model] = gproj
    colbase += ff // 2
    fold(colbase, gu.at[:, 0:d_model], d_model // 2, 0)
    stage0(4)
    for i in range(4): load(2 + i).wait()
    gmix = dott(gproj, w1[3 * d_model : 4 * d_model, :]).astype(bf16)
    gu[:, d_model : 2 * d_model] = gmix
    def heads(i, carry):
        at = pl.multiple_of(i * 2 * HD, 128)
        qp = proj[:, pl.ds(at, 2 * HD)]
        kp = proj[:, pl.ds(pl.multiple_of(d_model + i * 2 * HD, 128), 2 * HD)]
        vp = proj[:, pl.ds(pl.multiple_of(2 * d_model + i * 2 * HD, 128), 2 * HD)]
        gp = gu[:, pl.ds(pl.multiple_of(d_model + i * 2 * HD, 128), 2 * HD)]
        dq = dk = dv = None
        for j in range(2):
            own = (lanes // HD) == j
            q_j, k_j, g_j = (jnp.where(own, m, jnp.zeros_like(m)) for m in (qp, kp, gp))
            e = jnp.exp(dott(q_j, kp) * scale)
            soft = e / jnp.sum(e, axis=-1, keepdims=True)
            gs_ = dott(g_j, vp)
            delta = jnp.sum(soft * gs_, axis=-1, keepdims=True)
            ds_ = (soft * (gs_ - delta)).astype(bf16)
            a = jnp.dot(ds_, k_j, preferred_element_type=f32)
            b = tdot(ds_, q_j)
            c_ = tdot(soft.astype(bf16), g_j)
            dq, dk, dv = (a, b, c_) if dq is None else (dq + a, dk + b, dv + c_)
        gt[:, pl.ds(at, 2 * HD)] = (dq * scale).astype(bf16)
        gt[:, pl.ds(pl.multiple_of(d_model + i * 2 * HD, 128), 2 * HD)] = (dk * scale).astype(bf16)
        gt[:, pl.ds(pl.multiple_of(2 * d_model + i * 2 * HD, 128), 2 * HD)] = dv.astype(bf16)
        return carry
    lax.fori_loop(0, d_model // (2 * HD), heads, 0)
    advance(3)
    left[...] = (norm_one[...] * (1.0 + mod(1)) + mod(0)).T.astype(bf16)
    colbase += d_model // 2
    first = cuts[5][1]
    fold(colbase, gt, first, 0)
    stage0(5)
    advance(4)
    fold(colbase, gt, 3 * d_model // 2 - first, first)
    tail_at = pl.ds(colbase + 3 * d_model // 2, 128)
    sums = (
        owner_sums(rowsum(gt[:, 0:d_model])), owner_sums(rowsum(gt[:, 2 * d_model : 3 * d_model])),
        sums_out, sums_down, sums_up,
    )
    fill = jnp.zeros((rows - len(sums), 128), f32)
    for o in range(owners):
        g[(*slot(o), slice(None), tail_at)] = jnp.concatenate([m[o : o + 1] for m in sums] + [fill], axis=0).astype(bf16)
    stage0(6)
    advance(5)
    gain = None
    for j in range(3):
        share = dott(gt[:, j * d_model : (j + 1) * d_model], w1[j * d_model : (j + 1) * d_model, :])
        gain = share if gain is None else gain + share
    gmod[1:2, :] = rowsum(gain * norm_one[...])
    gmod[0:1, :] = rowsum(gain)
    gmod[6:8, :] = jnp.zeros((2, d_model), f32)
    resid[...] += norm_grad(gain * (1.0 + mod(1)), norm_one[...], inv_one)
    hand_over(1)
    for k in range(1, owners):
        rc(gmod, gm.at[owner], gs.at[k], gr.at[k], other(k)).start()
    gm[owner] = gmod[...]
    advance(6)
    advance(7)
    conditioning()
    for t in range(8, n + len(stages) - 1):
        advance(t)
    for k in range(n): drain(k)
    finish()
    for k in range(1, F):
        to = peer(k)
        rc(cond.at[to[0]], cond_all.at[f], ges.at[0, k], ger.at[0, k], to).wait_send()
        rc(bias, bias_all.at[f], ges.at[1, k], ger.at[1, k], to).wait_send()
        rc(part.at[to[0]], parts.at[f], ps.at[k], pr.at[k], to).wait_send()
    for i, (a, b) in enumerate(given):
        trade(i, a, b).wait_send()
    for ok, build in sends:
        if ok is None: build().wait_send()
        else: pl.when(ok)(lambda build=build: build().wait_send())


def block(shards, cond, lat, cot, wada, vectors, F):
    plans = [Plan(*s.shape) for s in shards]
    w = len(plans)
    d_model, ff = shards[3].shape[1], shards[2].shape[1]
    owners = 2 * F
    rows = wada.shape[0]
    Z = F // 4
    Zh = Z // 2
    q_half = 3 * d_model // 2
    first = 256 * -(-q_half // 512)
    cuts = []
    for size in (d_model, d_model, ff // 4, ff // 4, d_model // 2, first, q_half - first + 128):
        cuts.append((sum(c[1] for c in cuts), size))
    n = len(cuts)
    width = sum(c[1] for c in cuts)
    tokens = 2 * lat.shape[1]
    S = pltpu.SemaphoreType.DMA
    f32, bf16 = jnp.float32, jnp.bfloat16
    hbm, vm = pl.BlockSpec(memory_space=pl.ANY), pl.BlockSpec(memory_space=pltpu.VMEM)
    like = jax.ShapeDtypeStruct
    mods = 6 * d_model
    return pl.pallas_call(
        functools.partial(block_kernel, F, plans, cuts),
        out_shape=[like((s.shape[0] * F, s.shape[1]), bf16) for s in shards]
        + [
            like(lat.shape, bf16),
            like(lat.shape, f32),
            like((2 * rows, d_model), f32),
            like((rows // 2, ff), f32),
            like((rows // 2, d_model), f32),
            like((rows // 2, 3 * d_model), f32),
            like((8, 128), f32),
            like((rows // 2, mods), f32),
            like((1, mods), f32),
            like((F, 8, 128), f32),
        ],
        in_specs=[hbm] * w + [vm, hbm, hbm, vm] + [vm] * 6,
        out_specs=[hbm] * w + [hbm, hbm] + [vm] * 8,
        scratch_shapes=[
            pltpu.VMEM((F, 8, 128), f32),
            pltpu.VMEM((16, 128), f32),
            pltpu.VMEM((F, 16, 128), f32),
            pltpu.VMEM((F, 1, mods), f32),
            pltpu.VMEM((F, 1, mods), f32),
            pltpu.VMEM((8, d_model), f32),
            pltpu.VMEM((1, 4 * d_model + ff), f32),
            pltpu.VMEM((tokens, d_model), bf16),
            pltpu.VMEM((tokens, d_model), bf16),
            pltpu.VMEM((tokens, 3 * d_model), bf16),
            pltpu.VMEM((tokens, d_model), bf16),
            pltpu.VMEM((tokens, d_model), f32),
            pltpu.VMEM((tokens, ff), f32),
            pltpu.VMEM((tokens, ff), bf16),
            pltpu.VMEM((tokens, d_model), bf16),
            pltpu.VMEM((rows, width), f32),
            pltpu.VMEM((owners, 128), f32),
            pltpu.VMEM((Zh, 2, 2, 2, 2, rows, width), bf16),
            pltpu.VMEM((Zh, 2, 2, 2, rows, width), bf16),
            pltpu.VMEM((Zh, 2, 2, rows, width), bf16),
            pltpu.VMEM((Zh, 2, rows, width), bf16),
            pltpu.VMEM((Z, rows, width), bf16),
            pltpu.VMEM((Z, rows, width), bf16),
            pltpu.VMEM((owners, 8, d_model), f32),
            pltpu.VMEM((F, 8, 128), f32),
            pltpu.VMEM((ff, d_model), bf16),
            pltpu.VMEM((d_model, ff), bf16),
            pltpu.VMEM((tokens, ff), bf16),
            pltpu.VMEM((tokens, 3 * d_model), bf16),
            pltpu.VMEM((tokens, d_model), f32),
            pltpu.VMEM((tokens, d_model), f32),
            pltpu.VMEM((tokens, d_model), f32),
            pltpu.VMEM((8, d_model), f32),
            pltpu.VMEM((d_model, tokens), bf16),
            S((w, 2, Z)), S((w, Z)), *[S((w, Z))] * 8, S((w, 5, Z)), S((w, 5, Z)), S((w + 2,)), S((3, F)), S((3, F)), S((F,)), S((F,)),
            S((n,)), S((n,)), S((n, 2)), S((n, 2)), S((n, 2)), S((n, 2)), S((n, 2, Z)), S((n, 2, Z)),
            S((owners,)), S((owners,)), S((F,)), S((F,)), S((2,)), S((2,)), S((2,)), S((6,)),
        ],
        compiler_params=pltpu.CompilerParams(
            collective_id=0, has_side_effects=True, vmem_limit_bytes=63 * 2**20
        ),
        name="block_forward_backward",
    )(*shards, cond, lat, cot, wada, *vectors)[w:]


def body_fast(
    latents,
    condition,
    cotangent,
    w_ada,
    b_ada,
    w_qkv,
    b_query,
    b_value,
    w_out,
    b_out,
    w_up,
    b_up,
    w_down,
    b_down,
):
    f32 = jnp.float32
    F = lax.axis_size("fsdp")
    owners = F * lax.axis_size("sp")
    sp_index = lax.axis_index("sp")
    rows = w_qkv.shape[0]
    cond = jnp.pad(
        condition.astype(f32).reshape(2, F, rows).transpose(1, 0, 2), ((0, 0), (0, 6), (0, 128 - rows))
    )
    vectors = [part.reshape(1, -1) for part in (b_query, b_value, b_out, b_down, b_up, b_ada)]
    output, grad_latents, own_down, own_up, own_out, own_qkv, sums, own_ada, own_bada, grad_silu = block(
        (w_qkv, w_out, w_up, w_down), cond, latents, cotangent, w_ada, vectors, F
    )
    sizes = (rows, rows, rows, rows, b_up.shape[0])
    own_gb_query, own_gb_value, own_gb_out, own_gb_down, own_gb_up = (
        sums[i, : size // 2] for i, size in enumerate(sizes)
    )
    own_gb_ada = lax.dynamic_index_in_dim(
        own_bada.reshape(owners, -1), lax.axis_index("fsdp") * 2 + sp_index, 0, False
    )
    grad_silu = grad_silu[:, :2, :rows].transpose(1, 0, 2).reshape(2, -1)
    grad_condition = silu_back(condition.astype(f32), grad_silu)
    return (
        output,
        grad_latents,
        grad_condition,
        own_ada,
        own_gb_ada,
        own_qkv,
        own_gb_query,
        own_gb_value,
        own_out,
        own_gb_out,
        own_up,
        own_gb_up,
        own_down,
        own_gb_down,
    )


def choose(*args):
    latents, w_qkv, w_down = args[0], args[5], args[12]
    fits = (
        lax.axis_size("sp") == 2
        and lax.axis_size("fsdp") % 8 == 0
        and latents.shape[0] == 2
        and latents.shape[1] % 128 == 0
        and w_qkv.shape[0] % 16 == 0
        and w_qkv.shape[0] <= 128
        and w_down.shape[0] % 64 == 0
        and w_down.shape[0] == 4 * w_qkv.shape[0]
    )
    return (body_fast if fits else body_general)(*args)


def solution(mesh):
    in_specs = (
        P("fsdp", "sp", None),
        P("fsdp", None),
        P("fsdp", "sp", None),
        P("fsdp", None),
        P("fsdp"),
        P("fsdp", None),
        P("fsdp"),
        P("fsdp"),
        P("fsdp", None),
        P("fsdp"),
        P("fsdp", None),
        P("fsdp"),
        P("fsdp", None),
        P("fsdp"),
    )
    out_specs = (
        P("fsdp", "sp", None),
        P("fsdp", "sp", None),
        P("fsdp", None),
        P(("fsdp", "sp"), None),
        P(("fsdp", "sp")),
        P(("fsdp", "sp"), None),
        P(("fsdp", "sp")),
        P(("fsdp", "sp")),
        P(("fsdp", "sp"), None),
        P(("fsdp", "sp")),
        P(("fsdp", "sp"), None),
        P(("fsdp", "sp")),
        P(("fsdp", "sp"), None),
        P(("fsdp", "sp")),
    )
    return jax.shard_map(choose, mesh=mesh, in_specs=in_specs, out_specs=out_specs, check_vma=False)
```

```python
import functools

import jax
import jax.numpy as jnp
from jax import lax
from jax.experimental import pallas as pl
from jax.experimental.pallas import tpu as pltpu
from jax.sharding import PartitionSpec as P

D = 768
H = 12
HD = 64


eps = 1e-06


def normalize(values):
    centered = values - jnp.mean(values, axis=-1, keepdims=True)
    inverse = lax.rsqrt(jnp.mean(centered * centered, axis=-1, keepdims=True) + eps)
    return (centered * inverse, inverse)


def norm_back(grad_in, normed, inverse):
    return inverse * (
        grad_in
        - jnp.mean(grad_in, axis=-1, keepdims=True)
        - normed * jnp.mean(grad_in * normed, axis=-1, keepdims=True)
    )


def gelu_tanh(values):
    return jax.nn.gelu(values, approximate=True)


def silu_back(values, grad_out):
    return jax.vjp(jax.nn.silu, values)[1](grad_out)[0]


def gelu_back(values, grad_out):
    return jax.vjp(gelu_tanh, values)[1](grad_out)[0]


LANES = 2048


def body_general(
    latents,
    condition,
    cotangent,
    w_ada,
    b_ada,
    w_qkv,
    b_query,
    b_value,
    w_out,
    b_out,
    w_up,
    b_up,
    w_down,
    b_down,
):
    f32 = jnp.float32
    bf16 = jnp.bfloat16
    fsdp_count = lax.axis_size("fsdp")
    sp_count = lax.axis_size("sp")
    owners = fsdp_count * sp_count
    fsdp_index = lax.axis_index("fsdp")
    sp_index = lax.axis_index("sp")
    owner_index = fsdp_index * sp_count + sp_index
    pair_latents = latents.shape[0]
    own_latents = pair_latents // sp_count
    latent_total = pair_latents * fsdp_count
    tokens_all = latents.shape[1] * sp_count
    scale_factor = HD ** (-0.5)

    small = [condition.reshape(-1), b_ada, b_query, b_value, b_out, b_up, b_down]
    width = sum(part.size for part in small)
    padded = -(-width // LANES) * LANES
    small.append(jnp.zeros((padded - width,), bf16))
    small_all = lax.all_gather(
        jnp.concatenate(small).reshape(1, padded // 128, 128), "fsdp", axis=0, tiled=True
    ).reshape(fsdp_count, padded)
    pieces = []
    start = 0
    for part in small[:-1]:
        pieces.append(small_all[:, start : start + part.size].reshape(-1))
        start = start + part.size
    cond_all, ada_bias, query_bias, value_bias, out_bias, up_bias, down_bias = pieces
    cond_all = cond_all.reshape(latent_total, D).astype(f32)
    silu_all = jax.nn.silu(cond_all)

    inputs = lax.all_to_all(latents, "sp", split_axis=0, concat_axis=1, tiled=True).astype(f32)
    grad_out = lax.all_to_all(cotangent, "sp", split_axis=0, concat_axis=1, tiled=True).astype(f32)

    ada_rows = w_ada.shape[0]
    silu_mine = lax.dynamic_index_in_dim(
        silu_all.astype(bf16).reshape(fsdp_count, sp_count, own_latents, D), sp_index, 1, False
    )
    silu_mine = lax.dynamic_index_in_dim(
        silu_mine.reshape(fsdp_count * own_latents, fsdp_count, ada_rows), fsdp_index, 1, False
    )
    mod_part = jnp.dot(silu_mine, w_ada, preferred_element_type=f32)
    mod_part = lax.all_to_all(
        mod_part.reshape(fsdp_count, own_latents * 6 * D), "fsdp", split_axis=0, concat_axis=0, tiled=True
    )
    modulate = jnp.sum(mod_part, axis=0).reshape(own_latents, 6 * D) + ada_bias.astype(f32)
    mod_parts = modulate.reshape(own_latents, 6, 1, D)
    shift_one, scale_one, gate_one = (mod_parts[:, 0], mod_parts[:, 1], mod_parts[:, 2])
    shift_two, scale_two, gate_two = (mod_parts[:, 3], mod_parts[:, 4], mod_parts[:, 5])

    qkv_full = lax.all_gather(w_qkv, "fsdp", axis=0, tiled=True)
    out_full = lax.all_gather(w_out, "fsdp", axis=0, tiled=True)
    up_full = lax.all_gather(w_up, "fsdp", axis=0, tiled=True)
    down_full = lax.all_gather(w_down, "fsdp", axis=0, tiled=True)

    normed_one, inverse_one = normalize(inputs)
    attn_in = (normed_one * (1.0 + scale_one) + shift_one).astype(bf16)
    qkv_bias = jnp.concatenate([query_bias, jnp.zeros_like(query_bias), value_bias]).astype(f32)
    projected = (
        jnp.einsum("btd,de->bte", attn_in, qkv_full, preferred_element_type=f32) + qkv_bias
    ).astype(bf16)
    heads = projected.reshape(own_latents, tokens_all, 3, H, HD).transpose(2, 0, 3, 1, 4)
    queries, key_heads, value_heads = heads[0], heads[1], heads[2]
    scores = (
        jnp.einsum("bhqd,bhkd->bhqk", queries, key_heads, preferred_element_type=f32) * scale_factor
    )
    log_total = jnp.log(jnp.sum(jnp.exp(scores), axis=-1, keepdims=True))
    soft_float = jnp.exp(scores - log_total)
    soft_half = soft_float.astype(bf16)
    mixed = jnp.einsum("bhqk,bhkd->bhqd", soft_half, value_heads, preferred_element_type=f32).astype(
        bf16
    )
    mixed_tokens = mixed.transpose(0, 2, 1, 3).reshape(own_latents, tokens_all, D)
    attn_proj = jnp.einsum(
        "btd,de->bte", mixed_tokens, out_full, preferred_element_type=f32
    ) + out_bias.astype(f32)
    residual = inputs + gate_one * attn_proj
    normed_two, inverse_two = normalize(residual)
    mlp_in = (normed_two * (1.0 + scale_two) + shift_two).astype(bf16)
    up_value = jnp.einsum(
        "btd,df->btf", mlp_in, up_full, preferred_element_type=f32
    ) + up_bias.astype(f32)
    activated = gelu_tanh(up_value).astype(bf16)
    down_value = jnp.einsum(
        "btf,fd->btd", activated, down_full, preferred_element_type=f32
    ) + down_bias.astype(f32)
    output = (residual + gate_two * down_value).astype(bf16)
    output = lax.all_to_all(output, "sp", split_axis=1, concat_axis=0, tiled=True)

    grad_gate_two = jnp.sum(grad_out * down_value, axis=1)
    grad_down = (grad_out * gate_two).astype(bf16)
    gw_down = jnp.einsum("btf,btd->fd", activated, grad_down, preferred_element_type=f32)
    gb_down = jnp.sum(grad_down.astype(f32), axis=(0, 1))
    grad_act = jnp.einsum("btd,fd->btf", grad_down, down_full, preferred_element_type=f32)
    grad_up = gelu_back(up_value, grad_act).astype(bf16)
    gw_up = jnp.einsum("btd,btf->df", mlp_in, grad_up, preferred_element_type=f32)
    gb_up = jnp.sum(grad_up.astype(f32), axis=(0, 1))
    grad_mlp = jnp.einsum("btf,df->btd", grad_up, up_full, preferred_element_type=f32)
    grad_scale_two = jnp.sum(grad_mlp * normed_two, axis=1)
    grad_shift_two = jnp.sum(grad_mlp, axis=1)
    grad_resid = grad_out + norm_back(grad_mlp * (1.0 + scale_two), normed_two, inverse_two)
    grad_gate_one = jnp.sum(grad_resid * attn_proj, axis=1)
    grad_proj = (grad_resid * gate_one).astype(bf16)
    gw_out = jnp.einsum("btd,bte->de", mixed_tokens, grad_proj, preferred_element_type=f32)
    gb_out = jnp.sum(grad_proj.astype(f32), axis=(0, 1))
    grad_mixed = jnp.einsum("bte,de->btd", grad_proj, out_full, preferred_element_type=f32).astype(
        bf16
    )
    grad_heads = grad_mixed.reshape(own_latents, tokens_all, H, HD).transpose(0, 2, 1, 3)
    grad_soft = jnp.einsum("bhqd,bhkd->bhqk", grad_heads, value_heads, preferred_element_type=f32)
    delta_sum = jnp.sum(soft_float * grad_soft, axis=-1, keepdims=True)
    grad_scores = (soft_float * (grad_soft - delta_sum)).astype(bf16)
    grad_queries = (
        jnp.einsum("bhqk,bhkd->bhqd", grad_scores, key_heads, preferred_element_type=f32)
        * scale_factor
    ).astype(bf16)
    grad_keys = (
        jnp.einsum("bhqk,bhqd->bhkd", grad_scores, queries, preferred_element_type=f32)
        * scale_factor
    ).astype(bf16)
    grad_values = jnp.einsum(
        "bhqk,bhqd->bhkd", soft_half, grad_heads, preferred_element_type=f32
    ).astype(bf16)
    grad_tokens = (
        jnp.stack([grad_queries, grad_keys, grad_values], axis=0)
        .transpose(1, 3, 0, 2, 4)
        .reshape(own_latents, tokens_all, 3 * D)
    )
    gw_qkv = jnp.einsum("btd,bte->de", attn_in, grad_tokens, preferred_element_type=f32)
    grad_tok_float = grad_tokens.astype(f32)
    gb_query = jnp.sum(grad_tok_float[:, :, :D], axis=(0, 1))
    gb_value = jnp.sum(grad_tok_float[:, :, 2 * D :], axis=(0, 1))
    grad_attn_in = jnp.einsum("bte,de->btd", grad_tokens, qkv_full, preferred_element_type=f32)
    grad_scale_one = jnp.sum(grad_attn_in * normed_one, axis=1)
    grad_shift_one = jnp.sum(grad_attn_in, axis=1)
    grad_latents = grad_resid + norm_back(grad_attn_in * (1.0 + scale_one), normed_one, inverse_one)
    grad_latents = lax.all_to_all(grad_latents, "sp", split_axis=1, concat_axis=0, tiled=True)

    grad_mod = jnp.concatenate(
        [
            grad_shift_one,
            grad_scale_one,
            grad_gate_one,
            grad_shift_two,
            grad_scale_two,
            grad_gate_two,
        ],
        axis=1,
    )
    grad_mod = lax.all_to_all(
        jnp.broadcast_to(grad_mod[None], (owners, own_latents, 6 * D)),
        ("fsdp", "sp"),
        split_axis=0,
        concat_axis=0,
        tiled=True,
    ).reshape(latent_total, 6 * D)

    rows = D // owners
    biases = (gb_query, gb_value, gb_out, gb_up, gb_down)
    bias_rows = jnp.concatenate([part.reshape(owners, -1) for part in biases], axis=1)
    bias_width = bias_rows.shape[1]
    bias_lanes = -(-bias_width // (rows * 128)) * 128
    bias_rows = jnp.pad(bias_rows, ((0, 0), (0, rows * bias_lanes - bias_width)))
    stack = down_full.shape[0] // D
    gw_down = (
        gw_down.astype(bf16)
        .reshape(owners, stack, rows, D)
        .transpose(0, 2, 1, 3)
        .reshape(D, stack * D)
    )
    packed = jnp.concatenate(
        [
            gw_down,
            gw_up.astype(bf16),
            gw_qkv.astype(bf16),
            gw_out.astype(bf16),
            bias_rows.astype(bf16).reshape(D, bias_lanes),
        ],
        axis=1,
    )
    owned = lax.psum_scatter(packed, ("fsdp", "sp"), scatter_dimension=0, tiled=True).astype(f32)
    own_weights = []
    start = 0
    for width in (stack * D, up_full.shape[1], 3 * D, D, bias_lanes):
        own_weights.append(owned[:, start : start + width])
        start = start + width
    own_down, own_up, own_qkv, own_out, bias_sums = own_weights
    own_down = own_down.reshape(rows, stack, D).transpose(1, 0, 2).reshape(stack * rows, D)
    bias_sums = bias_sums.reshape(-1)
    own_bias = []
    start = 0
    for part in biases:
        width = part.size // owners
        own_bias.append(bias_sums[start : start + width])
        start = start + width
    own_gb_query, own_gb_value, own_gb_out, own_gb_up, own_gb_down = own_bias
    silu_rows = lax.dynamic_index_in_dim(
        silu_all.reshape(latent_total, owners, D // owners), owner_index, 1, False
    )
    own_ada = jnp.dot(silu_rows.T, grad_mod, precision=lax.Precision.HIGHEST)
    own_gb_ada = lax.dynamic_index_in_dim(
        jnp.sum(grad_mod, axis=0).reshape(owners, -1), owner_index, 0, False
    )
    grad_silu = jnp.dot(grad_mod.astype(bf16), w_ada.T, preferred_element_type=f32)
    grad_silu = lax.all_to_all(
        grad_silu.reshape(fsdp_count, pair_latents * ada_rows),
        "fsdp",
        split_axis=0,
        concat_axis=0,
        tiled=True,
    )
    grad_silu = (
        grad_silu.reshape(fsdp_count, pair_latents, ada_rows)
        .transpose(1, 0, 2)
        .reshape(pair_latents, D)
    )
    grad_condition = silu_back(condition.astype(f32), grad_silu)
    return (
        output,
        grad_latents,
        grad_condition,
        own_ada,
        own_gb_ada,
        own_qkv,
        own_gb_query,
        own_gb_value,
        own_out,
        own_gb_out,
        own_up,
        own_gb_up,
        own_down,
        own_gb_down,
    )


MESH = pl.DeviceIdType.MESH


class Plan:
    def __init__(self, rows, cols):
        self.rows, self.cols = rows, cols
        self.by_rows = rows % 64 == 0
        n = (rows // 32) if self.by_rows else (cols // 256)
        unit = 16 if self.by_rows else 128
        big = -(-2 * n // 3)
        self.half = n * unit
        self.big = big * unit
        self.unit = unit
    def at(self, ref, row, h=None, q=None):
        rows, cols, unit = self.rows, self.cols, self.unit
        if h is None:
            return ref.at[pl.ds(pl.multiple_of(row, 16), rows), :]
        start = h * self.half + (self.big if q == 1 else 0)
        size = self.half if q is None else (self.big if q == 0 else self.half - self.big)
        if self.by_rows:
            return ref.at[pl.ds(pl.multiple_of(row + start, 16), size), :]
        return ref.at[pl.ds(pl.multiple_of(row, 16), rows), pl.ds(pl.multiple_of(start, 128), size)]

GELU = 0.7978845608028654


def block_kernel(F, plans, cuts, *refs):
    n = len(cuts)
    w = len(plans)
    f32, bf16 = jnp.float32, jnp.bfloat16
    ins, (cond, lat, cot, wada), vectors = refs[:w], refs[w : w + 4], refs[w + 4 : w + 10]
    outs, refs = refs[w + 10 : 2 * w + 10], refs[2 * w + 10 :]
    (
        outp_own, glat_own, own_down, own_up, own_out, own_qkv, own_bias, ada, bada, gcond,
        cond_all, bias, bias_all, part, parts, mods, vec, lat_all, cot_all, proj, mixed, attn_proj, upv, act, outp,
        acc, silu, g, r0, r1, r2, up, dn, gm, cpart, w1, w2, gu, gt, norm_one, norm_two, resid, gmod, left,
        zs, zr, xs, xr, ys, yr, xds, xdr, yds, ydr, ss, sr, gloc, ges, ger, ps, pr,
        s0, q0, s1, q1, s2, q2, s3, q3, gs, gr, ks, kr, es, er, loc, wl,
    ) = refs
    f = lax.axis_index("fsdp"); x = lax.axis_index("sp")
    c = f % 2; y = (f // 2) % 2; z = f // 4; Z = F // 4; Zh = Z // 2
    owners = 2 * F
    owner = f * 2 + x
    rows = plans[0].rows
    half = rows // 2
    d_model, ff = lat_all.shape[1], act.shape[1]
    def dev(x_, y_, z_, c_):
        return ((z_ * 2 + y_) * 2 + c_, x_)
    xn, yn, sib = dev(1 - x, y, z, c), dev(x, 1 - y, z, c), dev(x, y, z, 1 - c)
    zu, zd = dev(x, y, z + 1, c), dev(x, y, z - 1, c)
    def peer(k):
        return (lax.rem(f + k, F), x)
    def other(k):
        o = lax.rem(owner + k, owners)
        return (o // 2, o % 2)
    bar = pltpu.get_barrier_semaphore()
    for k in range(1, owners):
        pl.semaphore_signal(bar, inc=1, device_id=other(k), device_id_type=MESH)
    bias[...] = jnp.zeros_like(bias)
    layout = []
    row = 0
    for ref in vectors:
        size = ref.shape[1]
        layout.append((row, size))
        for at in range(0, size, 128):
            bias[row : row + 1, 0 : min(128, size - at)] = ref[:, at : min(at + 128, size)].astype(f32)
            row += 1
    pl.semaphore_wait(bar, owners - 1)

    sends = []
    def send(ok, build):
        if ok is None:
            build().start()
        else:
            pl.when(ok)(lambda: build().start())
        sends.append((ok, build))
    def rc(src, dst, s, r, d):
        return pltpu.make_async_remote_copy(src_ref=src, dst_ref=dst, send_sem=s, recv_sem=r, device_id=d, device_id_type=MESH)

    def base(m, y_, z_, c_=c):
        return ((z_ * 2 + y_) * 2 + c_) * plans[m].rows
    def piece(m, y_, z_, h=None, q=None, c_=None):
        return plans[m].at(outs[m], base(m, y_, z_, c if c_ is None else c_), h, q)
    def mine(m, h=None, q=None):
        return plans[m].at(ins[m], 0, h, q)
    def to_sib(m, ok, kind, y_, z_, h=None, q=None, own=False):
        send(ok, lambda: rc(mine(m, h, q) if own else piece(m, y_, z_, h, q), piece(m, y_, z_, h, q),
                              ss.at[m, kind, z_], sr.at[m, kind, z_], sib))
    def arrived(m, ok, sem_s, sem_r, *where, c_=None):
        def go():
            p = piece(m, *where, c_=c_)
            rc(p, p, sem_s, sem_r, xn).wait_recv()
        if ok is None: go()
        else: pl.when(ok)(go)

    def start_own(m):
        send(None, lambda: rc(mine(m, x), piece(m, y, z, x), ys.at[m, z], yr.at[m, z], yn))
        send(z + 1 < Z, lambda: rc(mine(m, x), piece(m, y, z, x), zs.at[m, 0, z], zr.at[m, z], zu))
        send(z > 0, lambda: rc(mine(m, x), piece(m, y, z, x), zs.at[m, 1, z], zr.at[m, z], zd))
        send(z + 1 < Z, lambda: rc(mine(m, 1 - x, 0), piece(m, y, z, 1 - x, 0), zs.at[m, 2, z], zr.at[w + m, z], zu))
        send(z > 0, lambda: rc(mine(m, 1 - x, 0), piece(m, y, z, 1 - x, 0), zs.at[m, 3, z], zr.at[w + m, z], zd))
        send(None, lambda: rc(mine(m, 1 - x, 1), piece(m, y, z, 1 - x, 1), yds.at[m, z], ydr.at[m, z], yn))
        to_sib(m, None, 0, y, z, own=True)
        pltpu.make_async_copy(mine(m), piece(m, y, z), gloc.at[m]).start()

    def z_round(m, d):
        for sign in (-1, 1):
            o = z + sign * d
            ok = (o >= 0) if sign < 0 else (o < Z)
            arrived(m, ok, zs.at[m, 0, o], zr.at[m, o], y, o, x)
            more = ok & ((z + 1 < Z) if sign < 0 else (z > 0))
            onward, way = (zu, 0) if sign < 0 else (zd, 1)
            send(more, lambda o=o, way=way, onward=onward: rc(piece(m, y, o, x), piece(m, y, o, x), zs.at[m, way, o], zr.at[m, o], onward))
            send(ok, lambda o=o: rc(piece(m, y, o, x, 1), piece(m, y, o, x, 1), xs.at[m, o], xr.at[m, o], xn))
            send(ok, lambda o=o: rc(piece(m, y, o, x), piece(m, y, o, x), ys.at[m, o], yr.at[m, o], yn))
            to_sib(m, ok, 0, y, o, x)
            arrived(m, ok, zs.at[m, 2, o], zr.at[w + m, o], y, o, 1 - x, 0)
            send(more, lambda o=o, way=way, onward=onward: rc(piece(m, y, o, 1 - x, 0), piece(m, y, o, 1 - x, 0), zs.at[m, 2 + way, o], zr.at[w + m, o], onward))
            to_sib(m, ok, 5, y, o, 1 - x, 0)

    def xy_round(m, d):
        for sign in ((-1, 1) if d else (0,)):
            o = z + sign * d
            ok = None if d == 0 else ((o >= 0) if sign < 0 else (o < Z))
            arrived(m, ok, ys.at[m, o], yr.at[m, o], 1 - y, o, x)
            send(ok, lambda o=o: rc(piece(m, 1 - y, o, x, 0), piece(m, 1 - y, o, x, 0), xds.at[m, o], xdr.at[m, o], xn))
            to_sib(m, ok, 2, 1 - y, o, x)
            if d:
                arrived(m, ok, xs.at[m, o], xr.at[m, o], y, o, 1 - x, 1)
                send(ok, lambda o=o: rc(piece(m, y, o, 1 - x, 1), piece(m, y, o, 1 - x, 1), yds.at[m, o], ydr.at[m, o], yn))
                to_sib(m, ok, 1, y, o, 1 - x, 1)

    def last_round(m, d):
        for sign in ((-1, 1) if d else (0,)):
            o = z + sign * d
            ok = None if d == 0 else ((o >= 0) if sign < 0 else (o < Z))
            arrived(m, ok, xds.at[m, o], xdr.at[m, o], 1 - y, o, 1 - x, 0)
            to_sib(m, ok, 3, 1 - y, o, 1 - x, 0)
            arrived(m, ok, yds.at[m, o], ydr.at[m, o], 1 - y, o, 1 - x, 1)
            to_sib(m, ok, 4, 1 - y, o, 1 - x, 1)

    def landed(m):
        pltpu.make_async_copy(mine(m), piece(m, y, z), gloc.at[m]).wait()
        b = 1 - c
        arrived(m, None, ss.at[m, 0, z], sr.at[m, 0, z], y, z, c_=b)
        for d in range(Z):
            for sign in ((-1, 1) if d else (0,)):
                o = z + sign * d
                ok = None if d == 0 else ((o >= 0) if sign < 0 else (o < Z))
                if d:
                    arrived(m, ok, ss.at[m, 0, o], sr.at[m, 0, o], y, o, x, c_=b)
                    arrived(m, ok, ss.at[m, 1, o], sr.at[m, 1, o], y, o, 1 - x, 1, c_=b)
                    arrived(m, ok, ss.at[m, 5, o], sr.at[m, 5, o], y, o, 1 - x, 0, c_=b)
                arrived(m, ok, ss.at[m, 2, o], sr.at[m, 2, o], 1 - y, o, x, c_=b)
                arrived(m, ok, ss.at[m, 3, o], sr.at[m, 3, o], 1 - y, o, 1 - x, 0, c_=b)
                arrived(m, ok, ss.at[m, 4, o], sr.at[m, 4, o], 1 - y, o, 1 - x, 1, c_=b)

    def col(k):
        return pl.ds(*cuts[k])
    def c0(k):
        return rc(g.at[:, :, :, 1 - c, :, :, col(k)], r0.at[:, :, :, :, :, col(k)], s0.at[k], q0.at[k], sib)
    def c1(k, p):
        if p == 0:
            return rc(r0.at[:, 0, :, 1 - x, :, col(k)], r1.at[:, 0, :, :, col(k)], s1.at[k, 0], q1.at[k, 0], xn)
        return rc(r0.at[:, 1, 1 - y, :, :, col(k)], r1.at[:, 1, :, :, col(k)], s1.at[k, 1], q1.at[k, 1], yn)
    def c2(k, p):
        if p == 0:
            return rc(r1.at[:, 0, 1 - y, :, col(k)], r2.at[:, 0, :, col(k)], s2.at[k, 0], q2.at[k, 0], yn)
        return rc(r1.at[:, 1, 1 - x, :, col(k)], r2.at[:, 1, :, col(k)], s2.at[k, 1], q2.at[k, 1], xn)
    def c3(k, o, way, edge):
        buf = dn if way else up
        src = r2.at[o // 2, o % 2, :, col(k)] if edge else buf.at[o, :, col(k)]
        return rc(src, buf.at[o, :, col(k)], s3.at[k, way, o], q3.at[k, way, o], zd if way else zu)

    def stage0(k):
        c0(k).start()
    def stage1(k):
        c0(k).wait_recv()
        for p in (0, 1):
            for zh in range(Zh):
                for j in range(2):
                    at = (zh, 0, j, 1 - x) if p == 0 else (zh, 1, 1 - y, j)
                    own = g[at[0], at[1], at[2], c, at[3], :, col(k)].astype(f32)
                    r0[(*at, slice(None), col(k))] = (r0[(*at, slice(None), col(k))].astype(f32) + own).astype(bf16)
            c1(k, p).start()
    def pair(k, at):
        return g[at[0], at[1], at[2], c, at[3], :, col(k)].astype(f32) + r0[(*at, slice(None), col(k))].astype(f32)
    def stage2(k):
        for p in (0, 1):
            c1(k, p).wait_recv()
            j = (1 - y) if p == 0 else (1 - x)
            for zh in range(Zh):
                at = (zh, 0, j, x) if p == 0 else (zh, 1, y, j)
                r1[zh, p, j, :, col(k)] = (r1[zh, p, j, :, col(k)].astype(f32) + pair(k, at)).astype(bf16)
            c2(k, p).start()
    def stage3(k):
        for p in (0, 1):
            c2(k, p).wait_recv()
            j = y if p == 0 else x
            for zh in range(Zh):
                mine = r1[zh, p, j, :, col(k)].astype(f32) + pair(k, (zh, p, y, x))
                r2[zh, p, :, col(k)] = (r2[zh, p, :, col(k)].astype(f32) + mine).astype(bf16)
        @pl.when(z == 0)
        def _():
            for o in reversed(range(1, Z)): c3(k, o, 0, True).start()
        @pl.when(z == Z - 1)
        def _():
            for o in range(Z - 1): c3(k, o, 1, True).start()
    def hop(k, h):
        def go(way):
            for o in (reversed(range(h + 1, Z)) if way == 0 else range(Z - 1 - h)):
                buf = dn if way else up
                c3(k, o, way, False).wait_recv()
                buf[o, :, col(k)] = (buf[o, :, col(k)].astype(f32) + r2[o // 2, o % 2, :, col(k)].astype(f32)).astype(bf16)
                c3(k, o, way, False).start()
        pl.when(z == h)(lambda: go(0))
        pl.when(z == Z - 1 - h)(lambda: go(1))
    def final(k):
        acc[:, col(k)] = r2[z // 2, z % 2, :, col(k)].astype(f32)
        @pl.when(z > 0)
        def _():
            c3(k, z, 0, False).wait_recv()
            acc[:, col(k)] += up[z, :, col(k)].astype(f32)
        @pl.when(z < Z - 1)
        def _():
            c3(k, z, 1, False).wait_recv()
            acc[:, col(k)] += dn[z, :, col(k)].astype(f32)
        at, size = cuts[k]
        if k < 2:
            own_down[k * rows : (k + 1) * rows, :] = acc[:, at : at + size]
            return
        ref, begin = ((own_up, 2), (own_up, 2), (own_out, 4), (own_qkv, 5), (own_qkv, 5))[k - 2]
        off = at - cuts[begin][0]
        if k == 6:
            size -= 128
            own_bias[...] = acc[0:8, at + size : at + size + 128]
        wide = ref.shape[1] // 2
        ref[:, off : off + size] = acc[0 : rows // 2, at : at + size]
        ref[:, wide + off : wide + off + size] = acc[rows // 2 : rows, at : at + size]
    def drain(k):
        c0(k).wait_send()
        for p in (0, 1):
            c1(k, p).wait_send(); c2(k, p).wait_send()
        for o in range(Z):
            pl.when(o > z)(lambda o=o: c3(k, o, 0, False).wait_send())
            pl.when(o < z)(lambda o=o: c3(k, o, 1, False).wait_send())

    tokens = outp_own.shape[1]
    def swap(i, a, b):
        return rc(a.at[pl.ds(pl.multiple_of((1 - x) * tokens, 128), tokens), :], b.at[x], es.at[i], er.at[i], xn)
    def keep(i, a, b):
        return pltpu.make_async_copy(a.at[pl.ds(pl.multiple_of(x * tokens, 128), tokens), :], b.at[x], loc.at[i])
    pairs = ((outp, outp_own), (resid, glat_own))
    def hand_over(i):
        swap(i, *pairs[i]).start()
        keep(i, *pairs[i]).start()
    def conditioning():
        for k in range(1, 2 * F):
            rc(gmod, gm.at[lax.rem(owner + 2 * F - k, 2 * F)], gs.at[k], gr.at[k], xn).wait_recv()
        rows = wada.shape[0]
        step = wada.shape[1] // 6
        total = jnp.zeros((2 * F, rows), f32)
        for i in range(F):
            for j in range(2):
                silu[2 * i + j : 2 * i + j + 1, :] = cond_all[i, j : j + 1, :]
        sl = silu[...]
        sl = (sl / (1.0 + jnp.exp(-sl))).T
        sl = jnp.where(x == 0, sl[0 : rows // 2], sl[rows // 2 : rows])
        for j in range(6):
            span = pl.ds(j * step, step)
            block = gm[:, j, :]
            ada[:, span] = jnp.dot(sl, block, precision=lax.Precision.HIGHEST, preferred_element_type=f32)
            bada[:, span] = jnp.sum(block, axis=0, keepdims=True)
            total += lax.dot_general(block.astype(bf16), wada[:, span], (((1,), (1,)), ((), ())), preferred_element_type=f32)
        for i in range(F):
            cpart[i, 0:2, 0:rows] = total[2 * i : 2 * i + 2, :]
        for k in range(1, F):
            rc(cpart.at[peer(k)[0]], gcond.at[f], ks.at[k], kr.at[k], peer(k)).start()
        gcond[f] = cpart[f]
    def finish():
        for k in range(1, F):
            rc(cpart.at[0], gcond.at[lax.rem(f + F - k, F)], ks.at[k], kr.at[k], xn).wait_recv()
            rc(cpart.at[peer(k)[0]], gcond.at[f], ks.at[k], kr.at[k], peer(k)).wait_send()
        for k in range(1, 2 * F):
            rc(gmod, gm.at[owner], gs.at[k], gr.at[k], other(k)).wait_send()
        for i, (a, b) in enumerate(pairs):
            keep(i, a, b).wait()
            swap(i, a, b).wait_send()
            rc(b.at[1 - x], b.at[1 - x], es.at[i], er.at[i], xn).wait_recv()
    def slot(o):
        zo = o // 8
        return (zo // 2, zo % 2, (o // 4) % 2, (o // 2) % 2, o % 2)
    def norm(v):
        v = v - jnp.mean(v, axis=-1, keepdims=True)
        inv = lax.rsqrt(jnp.mean(v * v, axis=-1, keepdims=True) + eps)
        return v * inv, inv
    def norm_grad(gv, nv, inv):
        return inv * (gv - jnp.mean(gv, axis=-1, keepdims=True) - nv * jnp.mean(gv * nv, axis=-1, keepdims=True))
    def tdot(p, q):
        return lax.dot_general(p, q, (((0,), (0,)), ((), ())), preferred_element_type=f32)
    def dott(p, q):
        return lax.dot_general(p, q, (((1,), (1,)), ((), ())), preferred_element_type=f32)
    def mod(i):
        return mods[i : i + 1, :]
    def fold(col0, right, span, first):
        step = 256 if span % 256 == 0 else 128
        def one(i, carry):
            off = first + i * step
            lo = jnp.dot(left[...], right[:, pl.ds(pl.multiple_of(off, 128), step)], preferred_element_type=f32)
            hi_at = right.shape[1] // 2 + off
            hi = jnp.dot(left[...], right[:, pl.ds(pl.multiple_of(hi_at, 128), step)], preferred_element_type=f32)
            to = pl.ds(pl.multiple_of(col0 + off, 128), step)
            for o in range(owners):
                both = jnp.concatenate([lo[o * half : o * half + half], hi[o * half : o * half + half]], axis=0)
                g[(*slot(o), slice(None), to)] = both.astype(bf16)
            return carry
        lax.fori_loop(0, span // step, one, 0)
    def owner_sums(total):
        wide = total.shape[1]
        per = wide // owners
        cols = lax.broadcasted_iota(jnp.int32, (owners, wide), 1)
        begin = lax.broadcasted_iota(jnp.int32, (owners, wide), 0) * per
        mine_ = (cols >= begin) & (cols < begin + per)
        spread = jnp.where(mine_, jnp.broadcast_to(total, (owners, wide)), 0.0).astype(bf16)
        line = lax.broadcasted_iota(jnp.int32, (1, wide), 1)
        pick = jnp.broadcast_to(line - line // per * per, (128, wide)) == lax.broadcasted_iota(jnp.int32, (128, wide), 0)
        return dott(spread, jnp.where(pick, 1.0, 0.0).astype(bf16))

    stages = [stage1, stage2, stage3] + [functools.partial(lambda k, h: hop(k, h), h=h) for h in range(1, Z - 1)] + [final]
    def advance(t):
        for i, st in enumerate(stages):
            if 0 <= t - i < n: st(t - i)
    def rowsum(v):
        return jnp.sum(v.astype(f32), axis=0, keepdims=True)

    def load(i):
        if i == 0:
            pair = (outs[3], w1)
        elif i == 1:
            pair = (outs[2], w2)
        elif i < 5:
            pair = (outs[0].at[:, pl.ds(d_model * (i - 2), d_model)], w1.at[pl.ds(d_model * (i - 2), d_model), :])
        else:
            pair = (outs[1], w1.at[pl.ds(3 * d_model, d_model), :])
        return pltpu.make_async_copy(*pair, wl.at[i])
    own_tokens = lat.shape[1]
    for k in range(1, F):
        to = peer(k)
        rc(cond.at[to[0]], cond_all.at[f], ges.at[0, k], ger.at[0, k], to).start()
        rc(bias, bias_all.at[f], ges.at[1, k], ger.at[1, k], to).start()
    def trade(i, a, b):
        return rc(a.at[1 - x], b.at[pl.ds(pl.multiple_of(x * own_tokens, 128), own_tokens), :], ges.at[2, i], ger.at[2, i], xn)
    def stay(i, a, b):
        return pltpu.make_async_copy(a.at[x], b.at[pl.ds(pl.multiple_of(x * own_tokens, 128), own_tokens), :], gloc.at[w + i])
    given = ((lat, lat_all), (cot, cot_all))
    for i, (a, b) in enumerate(given):
        trade(i, a, b).start()
        stay(i, a, b).start()
    def comm(ms, d):
        for m in ms:
            if 0 < d < Z: z_round(m, d)
            if 0 < d <= Z: xy_round(m, d - 1)
            if d > 1: last_round(m, d - 2)
    def assemble(which, lo, hi):
        row, size = layout[which]
        cols = lax.broadcasted_iota(jnp.int32, (1, hi - lo), 1) + lo
        block = cols // size
        place = jnp.broadcast_to(cols - block * size, (128, hi - lo)) - lax.broadcasted_iota(jnp.int32, (128, hi - lo), 0)
        total = None
        for i in range(-(-size // 128)):
            hot = jnp.where(place == i * 128, 1.0, 0.0).astype(bf16)
            term = jnp.dot(bias_all[:, row + i, :].astype(bf16), hot, preferred_element_type=f32)
            total = term if total is None else total + term
        mine_ = jnp.broadcast_to(block, (F, hi - lo)) == lax.broadcasted_iota(jnp.int32, (F, hi - lo), 0)
        return jnp.sum(jnp.where(mine_, total, 0.0), axis=0, keepdims=True)
    start_own(0)
    start_own(1)
    start_own(2)
    start_own(3)
    comm((0, 1), 1)
    cond_all[f] = cond[f]
    bias_all[f] = bias[...]
    for k in range(1, F):
        rc(cond.at[0], cond_all.at[lax.rem(f + F - k, F)], ges.at[0, k], ger.at[0, k], xn).wait_recv()
    picked = jnp.where(x == 0, cond_all[:, 0, :], cond_all[:, 1, :])[:, :rows]
    picked = (picked / (1.0 + jnp.exp(-picked))).astype(bf16)
    made = jnp.dot(picked, wada[...], preferred_element_type=f32)
    for i in range(F):
        part[i] = made[i : i + 1, :]
    for k in range(1, F):
        to = peer(k)
        rc(part.at[to[0]], parts.at[f], ps.at[k], pr.at[k], to).start()
    parts[f] = part[f]
    comm((2,), 1)
    comm((0, 1), 2)
    for k in range(1, F):
        rc(bias, bias_all.at[lax.rem(f + F - k, F)], ges.at[1, k], ger.at[1, k], xn).wait_recv()
        rc(part.at[0], parts.at[lax.rem(f + F - k, F)], ps.at[k], pr.at[k], xn).wait_recv()
    for i in range(6):
        span = slice(i * d_model, (i + 1) * d_model)
        mods[i : i + 1, :] = jnp.sum(parts[:, :, span], axis=0) + assemble(5, i * d_model, (i + 1) * d_model)
    comm((3,), 1)
    places = {}
    at = 0
    for which in (0, 1, 2, 3, 4):
        size = layout[which][1] * F
        places[which] = slice(at, at + size)
        for lo in range(0, size, d_model):
            vec[:, at + lo : at + lo + d_model] = assemble(which, lo, lo + d_model)
        at += size
    def bias_of(which):
        return vec[:, places[which]]
    comm((0, 1), 3)
    for i, (a, b) in enumerate(given):
        stay(i, a, b).wait()
        got = b.at[pl.ds(pl.multiple_of((1 - x) * own_tokens, 128), own_tokens), :]
        rc(got, got, ges.at[2, i], ger.at[2, i], xn).wait_recv()
    comm((2,), 2)
    comm((0, 1), 4)
    v, inv_one = norm(lat_all[...].astype(f32))
    norm_one[...] = v
    gt[:, 0:d_model] = (v * (1.0 + mod(1)) + mod(0)).astype(bf16)
    comm((3,), 2)
    comm((0, 1), 5)
    comm((2,), 3)
    for m in (0, 1): landed(m)
    for i in range(2, 6): load(i).start()
    comm((2,), 4)
    for i in range(2, 6): load(i).wait()
    for j in range(3):
        made = jnp.dot(gt[:, 0:d_model], w1[j * d_model : (j + 1) * d_model, :], preferred_element_type=f32)
        if j != 1:
            made = made + bias_of(0 if j == 0 else 1)
        proj[:, j * d_model : (j + 1) * d_model] = made.astype(bf16)
    scale = HD ** (-0.5)
    lanes = lax.broadcasted_iota(jnp.int32, (1, 2 * HD), 1)
    comm((3,), 3)
    def attend(i, carry):
        at = pl.multiple_of(i * 2 * HD, 128)
        qp = proj[:, pl.ds(at, 2 * HD)]
        kp = proj[:, pl.ds(pl.multiple_of(d_model + i * 2 * HD, 128), 2 * HD)]
        vp = proj[:, pl.ds(pl.multiple_of(2 * d_model + i * 2 * HD, 128), 2 * HD)]
        total = None
        for j in range(2):
            own = (lanes // HD) == j
            q_j, v_j = (jnp.where(own, m_, jnp.zeros_like(m_)) for m_ in (qp, vp))
            e = jnp.exp(dott(q_j, kp) * scale)
            soft = e * (1.0 / jnp.sum(e, axis=-1, keepdims=True))
            term = jnp.dot(soft.astype(bf16), v_j, preferred_element_type=f32)
            total = term if total is None else total + term
        mixed[:, pl.ds(at, 2 * HD)] = total.astype(bf16)
        return carry
    pairs_of = d_model // (2 * HD)
    lax.fori_loop(0, pairs_of // 2, attend, 0)
    comm((2,), 5)
    lax.fori_loop(pairs_of // 2, pairs_of, attend, 0)
    comm((3,), 4)
    attn_proj[...] = jnp.dot(mixed[...], w1[3 * d_model : 4 * d_model, :], preferred_element_type=f32) + bias_of(2)
    resid[...] = lat_all[...].astype(f32) + mod(2) * attn_proj[...]
    n2, inv_two = norm(resid[...])
    norm_two[...] = n2
    n2 = n2 * (1.0 + mod(4)) + mod(3)
    gt[:, 0:d_model] = n2.astype(bf16)
    left[...] = n2.T.astype(bf16)
    landed(2)
    load(1).start()
    load(1).wait()
    step = 512
    for i in range(ff // step):
        span = slice(i * step, (i + 1) * step)
        at = places[4].start + i * step
        u = jnp.dot(gt[:, 0:d_model], w2[:, span], preferred_element_type=f32) + vec[:, at : at + step]
        th = jnp.tanh(GELU * (u + 0.044715 * (u * u * u)))
        act[:, span] = (0.5 * u * (1.0 + th)).astype(bf16)
        upv[:, span] = 0.5 * (1.0 + th) + 0.5 * u * (1.0 - th * th) * (GELU * (1.0 + 3.0 * 0.044715 * (u * u)))
    comm((3,), 5)
    landed(3)
    load(0).start()
    load(0).wait()
    down = jnp.dot(act[...], w1[...], preferred_element_type=f32) + bias_of(3)
    outp[...] = (resid[...] + mod(5) * down).astype(bf16)
    hand_over(0)
    gmod[5:6, :] = rowsum(cot_all[...].astype(f32) * down)
    cpart[...] = jnp.zeros_like(cpart)

    cotf = cot_all[...].astype(f32)
    gdown = (cotf * mod(5)).astype(bf16)
    sums_down = owner_sums(rowsum(gdown))
    group = owners // 4
    wide = ff // 4
    for i in range(4):
        made = tdot(act[:, i * wide : (i + 1) * wide], gdown)
        for j in range(group):
            o = i * group + j
            for b in range(2):
                at = j * 2 * rows + b * rows
                g[(*slot(o), slice(None), slice(b * d_model, (b + 1) * d_model))] = made[at : at + rows].astype(bf16)
    stage0(0)
    stage0(1)
    step = 512
    for i in range(ff // step):
        span = slice(i * step, (i + 1) * step)
        gu[:, span] = (dott(gdown, w1[span, :]) * upv[:, span]).astype(bf16)
    for i in range(4): load(2 + i).start()
    advance(0)
    colbase = 2 * d_model
    fold(colbase, gu, ff // 4, 0)
    stage0(2)
    advance(1)
    fold(colbase, gu, ff // 4, ff // 4)
    stage0(3)
    sums_up = owner_sums(rowsum(gu[...]))
    gmlp = dott(gu[...], w2[...])
    gmod[4:5, :] = rowsum(gmlp * norm_two[...])
    gmod[3:4, :] = rowsum(gmlp)
    gres = cot_all[...].astype(f32) + norm_grad(gmlp * (1.0 + mod(4)), norm_two[...], inv_two)
    resid[...] = gres
    gmod[2:3, :] = rowsum(gres * attn_proj[...])
    gproj = (gres * mod(2)).astype(bf16)
    sums_out = owner_sums(rowsum(gproj))
    advance(2)
    left[...] = mixed[...].astype(f32).T.astype(bf16)
    gu[:, 0:d_model] = gproj
    colbase += ff // 2
    fold(colbase, gu.at[:, 0:d_model], d_model // 2, 0)
    stage0(4)
    for i in range(4): load(2 + i).wait()
    gmix = dott(gproj, w1[3 * d_model : 4 * d_model, :]).astype(bf16)
    gu[:, d_model : 2 * d_model] = gmix
    def heads(i, carry):
        at = pl.multiple_of(i * 2 * HD, 128)
        qp = proj[:, pl.ds(at, 2 * HD)]
        kp = proj[:, pl.ds(pl.multiple_of(d_model + i * 2 * HD, 128), 2 * HD)]
        vp = proj[:, pl.ds(pl.multiple_of(2 * d_model + i * 2 * HD, 128), 2 * HD)]
        gp = gu[:, pl.ds(pl.multiple_of(d_model + i * 2 * HD, 128), 2 * HD)]
        dq = dk = dv = None
        for j in range(2):
            own = (lanes // HD) == j
            q_j, k_j, g_j = (jnp.where(own, m, jnp.zeros_like(m)) for m in (qp, kp, gp))
            e = jnp.exp(dott(q_j, kp) * scale)
            soft = e * (1.0 / jnp.sum(e, axis=-1, keepdims=True))
            gs_ = dott(g_j, vp)
            delta = jnp.sum(soft * gs_, axis=-1, keepdims=True)
            ds_ = (soft * (gs_ - delta)).astype(bf16)
            a = jnp.dot(ds_, k_j, preferred_element_type=f32)
            b = tdot(ds_, q_j)
            c_ = tdot(soft.astype(bf16), g_j)
            dq, dk, dv = (a, b, c_) if dq is None else (dq + a, dk + b, dv + c_)
        gt[:, pl.ds(at, 2 * HD)] = (dq * scale).astype(bf16)
        gt[:, pl.ds(pl.multiple_of(d_model + i * 2 * HD, 128), 2 * HD)] = (dk * scale).astype(bf16)
        gt[:, pl.ds(pl.multiple_of(2 * d_model + i * 2 * HD, 128), 2 * HD)] = dv.astype(bf16)
        return carry
    lax.fori_loop(0, d_model // (2 * HD), heads, 0)
    advance(3)
    left[...] = (norm_one[...] * (1.0 + mod(1)) + mod(0)).T.astype(bf16)
    colbase += d_model // 2
    first = cuts[5][1]
    fold(colbase, gt, first, 0)
    stage0(5)
    advance(4)
    fold(colbase, gt, 3 * d_model // 2 - first, first)
    tail_at = pl.ds(colbase + 3 * d_model // 2, 128)
    sums = (
        owner_sums(rowsum(gt[:, 0:d_model])), owner_sums(rowsum(gt[:, 2 * d_model : 3 * d_model])),
        sums_out, sums_down, sums_up,
    )
    fill = jnp.zeros((rows - len(sums), 128), f32)
    for o in range(owners):
        g[(*slot(o), slice(None), tail_at)] = jnp.concatenate([m[o : o + 1] for m in sums] + [fill], axis=0).astype(bf16)
    stage0(6)
    advance(5)
    gain = None
    for j in range(3):
        share = dott(gt[:, j * d_model : (j + 1) * d_model], w1[j * d_model : (j + 1) * d_model, :])
        gain = share if gain is None else gain + share
    gmod[1:2, :] = rowsum(gain * norm_one[...])
    gmod[0:1, :] = rowsum(gain)
    gmod[6:8, :] = jnp.zeros((2, d_model), f32)
    resid[...] += norm_grad(gain * (1.0 + mod(1)), norm_one[...], inv_one)
    hand_over(1)
    for k in range(1, owners):
        rc(gmod, gm.at[owner], gs.at[k], gr.at[k], other(k)).start()
    gm[owner] = gmod[...]
    advance(6)
    advance(7)
    conditioning()
    for t in range(8, n + len(stages) - 1):
        advance(t)
    for k in range(n): drain(k)
    finish()
    for k in range(1, F):
        to = peer(k)
        rc(cond.at[to[0]], cond_all.at[f], ges.at[0, k], ger.at[0, k], to).wait_send()
        rc(bias, bias_all.at[f], ges.at[1, k], ger.at[1, k], to).wait_send()
        rc(part.at[to[0]], parts.at[f], ps.at[k], pr.at[k], to).wait_send()
    for i, (a, b) in enumerate(given):
        trade(i, a, b).wait_send()
    for ok, build in sends:
        if ok is None: build().wait_send()
        else: pl.when(ok)(lambda build=build: build().wait_send())


def block(shards, cond, lat, cot, wada, vectors, F):
    plans = [Plan(*s.shape) for s in shards]
    w = len(plans)
    d_model, ff = shards[3].shape[1], shards[2].shape[1]
    owners = 2 * F
    rows = wada.shape[0]
    Z = F // 4
    Zh = Z // 2
    q_half = 3 * d_model // 2
    first = 256 * -(-q_half // 512)
    cuts = []
    for size in (d_model, d_model, ff // 4, ff // 4, d_model // 2, first, q_half - first + 128):
        cuts.append((sum(c[1] for c in cuts), size))
    n = len(cuts)
    width = sum(c[1] for c in cuts)
    tokens = 2 * lat.shape[1]
    S = pltpu.SemaphoreType.DMA
    f32, bf16 = jnp.float32, jnp.bfloat16
    hbm, vm = pl.BlockSpec(memory_space=pl.ANY), pl.BlockSpec(memory_space=pltpu.VMEM)
    like = jax.ShapeDtypeStruct
    mods = 6 * d_model
    return pl.pallas_call(
        functools.partial(block_kernel, F, plans, cuts),
        out_shape=[like((s.shape[0] * F, s.shape[1]), bf16) for s in shards]
        + [
            like(lat.shape, bf16),
            like(lat.shape, f32),
            like((2 * rows, d_model), f32),
            like((rows // 2, ff), f32),
            like((rows // 2, d_model), f32),
            like((rows // 2, 3 * d_model), f32),
            like((8, 128), f32),
            like((rows // 2, mods), f32),
            like((1, mods), f32),
            like((F, 8, 128), f32),
        ],
        in_specs=[hbm] * w + [vm, hbm, hbm, vm] + [vm] * 6,
        out_specs=[hbm] * w + [hbm, hbm] + [vm] * 8,
        scratch_shapes=[
            pltpu.VMEM((F, 8, 128), f32),
            pltpu.VMEM((16, 128), f32),
            pltpu.VMEM((F, 16, 128), f32),
            pltpu.VMEM((F, 1, mods), f32),
            pltpu.VMEM((F, 1, mods), f32),
            pltpu.VMEM((8, d_model), f32),
            pltpu.VMEM((1, 4 * d_model + ff), f32),
            pltpu.VMEM((tokens, d_model), bf16),
            pltpu.VMEM((tokens, d_model), bf16),
            pltpu.VMEM((tokens, 3 * d_model), bf16),
            pltpu.VMEM((tokens, d_model), bf16),
            pltpu.VMEM((tokens, d_model), f32),
            pltpu.VMEM((tokens, ff), f32),
            pltpu.VMEM((tokens, ff), bf16),
            pltpu.VMEM((tokens, d_model), bf16),
            pltpu.VMEM((rows, width), f32),
            pltpu.VMEM((owners, 128), f32),
            pltpu.VMEM((Zh, 2, 2, 2, 2, rows, width), bf16),
            pltpu.VMEM((Zh, 2, 2, 2, rows, width), bf16),
            pltpu.VMEM((Zh, 2, 2, rows, width), bf16),
            pltpu.VMEM((Zh, 2, rows, width), bf16),
            pltpu.VMEM((Z, rows, width), bf16),
            pltpu.VMEM((Z, rows, width), bf16),
            pltpu.VMEM((owners, 8, d_model), f32),
            pltpu.VMEM((F, 8, 128), f32),
            pltpu.VMEM((ff, d_model), bf16),
            pltpu.VMEM((d_model, ff), bf16),
            pltpu.VMEM((tokens, ff), bf16),
            pltpu.VMEM((tokens, 3 * d_model), bf16),
            pltpu.VMEM((tokens, d_model), f32),
            pltpu.VMEM((tokens, d_model), f32),
            pltpu.VMEM((tokens, d_model), f32),
            pltpu.VMEM((8, d_model), f32),
            pltpu.VMEM((d_model, tokens), bf16),
            S((w, 4, Z)), S((2 * w, Z)), *[S((w, Z))] * 8, S((w, 6, Z)), S((w, 6, Z)), S((w + 2,)), S((3, F)), S((3, F)), S((F,)), S((F,)),
            S((n,)), S((n,)), S((n, 2)), S((n, 2)), S((n, 2)), S((n, 2)), S((n, 2, Z)), S((n, 2, Z)),
            S((owners,)), S((owners,)), S((F,)), S((F,)), S((2,)), S((2,)), S((2,)), S((6,)),
        ],
        compiler_params=pltpu.CompilerParams(
            collective_id=0, has_side_effects=True, vmem_limit_bytes=63 * 2**20
        ),
        name="block_forward_backward",
    )(*shards, cond, lat, cot, wada, *vectors)[w:]


def deliver(*arrays):
    count = len(arrays)

    def kernel(*refs):
        ins, outs, kept, sem = refs[:count], refs[count : 2 * count], refs[2 * count : -1], refs[-1]
        reads = [pltpu.make_async_copy(ins[i], kept[i], sem.at[0, i]) for i in range(count)]
        writes = [pltpu.make_async_copy(kept[i], outs[i], sem.at[1, i]) for i in range(count)]
        for copy in reads:
            copy.start()
        for i in range(count):
            reads[i].wait()
            writes[i].start()
        for copy in writes:
            copy.wait()

    hbm = pl.BlockSpec(memory_space=pl.ANY)
    return pl.pallas_call(
        kernel,
        out_shape=[jax.ShapeDtypeStruct(a.shape, a.dtype) for a in arrays],
        in_specs=[hbm] * count,
        out_specs=[hbm] * count,
        scratch_shapes=[pltpu.VMEM(a.shape, a.dtype) for a in arrays] + [pltpu.SemaphoreType.DMA((2, count))],
        compiler_params=pltpu.CompilerParams(vmem_limit_bytes=63 * 2**20),
        name="deliver",
    )(*arrays)


def body_fast(
    latents,
    condition,
    cotangent,
    w_ada,
    b_ada,
    w_qkv,
    b_query,
    b_value,
    w_out,
    b_out,
    w_up,
    b_up,
    w_down,
    b_down,
):
    f32 = jnp.float32
    F = lax.axis_size("fsdp")
    owners = F * lax.axis_size("sp")
    sp_index = lax.axis_index("sp")
    rows = w_qkv.shape[0]
    cond = jnp.pad(
        condition.astype(f32).reshape(2, F, rows).transpose(1, 0, 2), ((0, 0), (0, 6), (0, 128 - rows))
    )
    vectors = [part.reshape(1, -1) for part in (b_query, b_value, b_out, b_down, b_up, b_ada)]
    output, grad_latents, own_down, own_up, own_out, own_qkv, sums, own_ada, own_bada, grad_silu = block(
        (w_qkv, w_out, w_up, w_down), cond, latents, cotangent, w_ada, vectors, F
    )
    output, grad_latents, own_down, own_up, own_out, own_qkv, own_ada = deliver(
        output, grad_latents, own_down, own_up, own_out, own_qkv, own_ada
    )
    sizes = (rows, rows, rows, rows, b_up.shape[0])
    own_gb_query, own_gb_value, own_gb_out, own_gb_down, own_gb_up = (
        sums[i, : size // 2] for i, size in enumerate(sizes)
    )
    own_gb_ada = lax.dynamic_index_in_dim(
        own_bada.reshape(owners, -1), lax.axis_index("fsdp") * 2 + sp_index, 0, False
    )
    grad_silu = grad_silu[:, :2, :rows].transpose(1, 0, 2).reshape(2, -1)
    grad_condition = silu_back(condition.astype(f32), grad_silu)
    return (
        output,
        grad_latents,
        grad_condition,
        own_ada,
        own_gb_ada,
        own_qkv,
        own_gb_query,
        own_gb_value,
        own_out,
        own_gb_out,
        own_up,
        own_gb_up,
        own_down,
        own_gb_down,
    )


def choose(*args):
    latents, w_qkv, w_down = args[0], args[5], args[12]
    fits = (
        lax.axis_size("sp") == 2
        and lax.axis_size("fsdp") % 8 == 0
        and latents.shape[0] == 2
        and latents.shape[1] % 128 == 0
        and w_qkv.shape[0] % 16 == 0
        and w_qkv.shape[0] <= 128
        and w_down.shape[0] % 64 == 0
        and w_down.shape[0] == 4 * w_qkv.shape[0]
    )
    return (body_fast if fits else body_general)(*args)


def solution(mesh):
    in_specs = (
        P("fsdp", "sp", None),
        P("fsdp", None),
        P("fsdp", "sp", None),
        P("fsdp", None),
        P("fsdp"),
        P("fsdp", None),
        P("fsdp"),
        P("fsdp"),
        P("fsdp", None),
        P("fsdp"),
        P("fsdp", None),
        P("fsdp"),
        P("fsdp", None),
        P("fsdp"),
    )
    out_specs = (
        P("fsdp", "sp", None),
        P("fsdp", "sp", None),
        P("fsdp", None),
        P(("fsdp", "sp"), None),
        P(("fsdp", "sp")),
        P(("fsdp", "sp"), None),
        P(("fsdp", "sp")),
        P(("fsdp", "sp")),
        P(("fsdp", "sp"), None),
        P(("fsdp", "sp")),
        P(("fsdp", "sp"), None),
        P(("fsdp", "sp")),
        P(("fsdp", "sp"), None),
        P(("fsdp", "sp")),
    )
    return jax.shard_map(choose, mesh=mesh, in_specs=in_specs, out_specs=out_specs, check_vma=False)
```

```python
import functools

import jax
import jax.numpy as jnp
from jax import lax
from jax.experimental import pallas as pl
from jax.experimental.pallas import tpu as pltpu
from jax.sharding import PartitionSpec as P

D = 768
H = 12
HD = 64


eps = 1e-06


def normalize(values):
    centered = values - jnp.mean(values, axis=-1, keepdims=True)
    inverse = lax.rsqrt(jnp.mean(centered * centered, axis=-1, keepdims=True) + eps)
    return (centered * inverse, inverse)


def norm_back(grad_in, normed, inverse):
    return inverse * (
        grad_in
        - jnp.mean(grad_in, axis=-1, keepdims=True)
        - normed * jnp.mean(grad_in * normed, axis=-1, keepdims=True)
    )


def gelu_tanh(values):
    return jax.nn.gelu(values, approximate=True)


def silu_back(values, grad_out):
    return jax.vjp(jax.nn.silu, values)[1](grad_out)[0]


def gelu_back(values, grad_out):
    return jax.vjp(gelu_tanh, values)[1](grad_out)[0]


LANES = 2048


def body_general(
    latents,
    condition,
    cotangent,
    w_ada,
    b_ada,
    w_qkv,
    b_query,
    b_value,
    w_out,
    b_out,
    w_up,
    b_up,
    w_down,
    b_down,
):
    f32 = jnp.float32
    bf16 = jnp.bfloat16
    fsdp_count = lax.axis_size("fsdp")
    sp_count = lax.axis_size("sp")
    owners = fsdp_count * sp_count
    fsdp_index = lax.axis_index("fsdp")
    sp_index = lax.axis_index("sp")
    owner_index = fsdp_index * sp_count + sp_index
    pair_latents = latents.shape[0]
    own_latents = pair_latents // sp_count
    latent_total = pair_latents * fsdp_count
    tokens_all = latents.shape[1] * sp_count
    scale_factor = HD ** (-0.5)

    small = [condition.reshape(-1), b_ada, b_query, b_value, b_out, b_up, b_down]
    width = sum(part.size for part in small)
    padded = -(-width // LANES) * LANES
    small.append(jnp.zeros((padded - width,), bf16))
    small_all = lax.all_gather(
        jnp.concatenate(small).reshape(1, padded // 128, 128), "fsdp", axis=0, tiled=True
    ).reshape(fsdp_count, padded)
    pieces = []
    start = 0
    for part in small[:-1]:
        pieces.append(small_all[:, start : start + part.size].reshape(-1))
        start = start + part.size
    cond_all, ada_bias, query_bias, value_bias, out_bias, up_bias, down_bias = pieces
    cond_all = cond_all.reshape(latent_total, D).astype(f32)
    silu_all = jax.nn.silu(cond_all)

    inputs = lax.all_to_all(latents, "sp", split_axis=0, concat_axis=1, tiled=True).astype(f32)
    grad_out = lax.all_to_all(cotangent, "sp", split_axis=0, concat_axis=1, tiled=True).astype(f32)

    ada_rows = w_ada.shape[0]
    silu_mine = lax.dynamic_index_in_dim(
        silu_all.astype(bf16).reshape(fsdp_count, sp_count, own_latents, D), sp_index, 1, False
    )
    silu_mine = lax.dynamic_index_in_dim(
        silu_mine.reshape(fsdp_count * own_latents, fsdp_count, ada_rows), fsdp_index, 1, False
    )
    mod_part = jnp.dot(silu_mine, w_ada, preferred_element_type=f32)
    mod_part = lax.all_to_all(
        mod_part.reshape(fsdp_count, own_latents * 6 * D), "fsdp", split_axis=0, concat_axis=0, tiled=True
    )
    modulate = jnp.sum(mod_part, axis=0).reshape(own_latents, 6 * D) + ada_bias.astype(f32)
    mod_parts = modulate.reshape(own_latents, 6, 1, D)
    shift_one, scale_one, gate_one = (mod_parts[:, 0], mod_parts[:, 1], mod_parts[:, 2])
    shift_two, scale_two, gate_two = (mod_parts[:, 3], mod_parts[:, 4], mod_parts[:, 5])

    qkv_full = lax.all_gather(w_qkv, "fsdp", axis=0, tiled=True)
    out_full = lax.all_gather(w_out, "fsdp", axis=0, tiled=True)
    up_full = lax.all_gather(w_up, "fsdp", axis=0, tiled=True)
    down_full = lax.all_gather(w_down, "fsdp", axis=0, tiled=True)

    normed_one, inverse_one = normalize(inputs)
    attn_in = (normed_one * (1.0 + scale_one) + shift_one).astype(bf16)
    qkv_bias = jnp.concatenate([query_bias, jnp.zeros_like(query_bias), value_bias]).astype(f32)
    projected = (
        jnp.einsum("btd,de->bte", attn_in, qkv_full, preferred_element_type=f32) + qkv_bias
    ).astype(bf16)
    heads = projected.reshape(own_latents, tokens_all, 3, H, HD).transpose(2, 0, 3, 1, 4)
    queries, key_heads, value_heads = heads[0], heads[1], heads[2]
    scores = (
        jnp.einsum("bhqd,bhkd->bhqk", queries, key_heads, preferred_element_type=f32) * scale_factor
    )
    log_total = jnp.log(jnp.sum(jnp.exp(scores), axis=-1, keepdims=True))
    soft_float = jnp.exp(scores - log_total)
    soft_half = soft_float.astype(bf16)
    mixed = jnp.einsum("bhqk,bhkd->bhqd", soft_half, value_heads, preferred_element_type=f32).astype(
        bf16
    )
    mixed_tokens = mixed.transpose(0, 2, 1, 3).reshape(own_latents, tokens_all, D)
    attn_proj = jnp.einsum(
        "btd,de->bte", mixed_tokens, out_full, preferred_element_type=f32
    ) + out_bias.astype(f32)
    residual = inputs + gate_one * attn_proj
    normed_two, inverse_two = normalize(residual)
    mlp_in = (normed_two * (1.0 + scale_two) + shift_two).astype(bf16)
    up_value = jnp.einsum(
        "btd,df->btf", mlp_in, up_full, preferred_element_type=f32
    ) + up_bias.astype(f32)
    activated = gelu_tanh(up_value).astype(bf16)
    down_value = jnp.einsum(
        "btf,fd->btd", activated, down_full, preferred_element_type=f32
    ) + down_bias.astype(f32)
    output = (residual + gate_two * down_value).astype(bf16)
    output = lax.all_to_all(output, "sp", split_axis=1, concat_axis=0, tiled=True)

    grad_gate_two = jnp.sum(grad_out * down_value, axis=1)
    grad_down = (grad_out * gate_two).astype(bf16)
    gw_down = jnp.einsum("btf,btd->fd", activated, grad_down, preferred_element_type=f32)
    gb_down = jnp.sum(grad_down.astype(f32), axis=(0, 1))
    grad_act = jnp.einsum("btd,fd->btf", grad_down, down_full, preferred_element_type=f32)
    grad_up = gelu_back(up_value, grad_act).astype(bf16)
    gw_up = jnp.einsum("btd,btf->df", mlp_in, grad_up, preferred_element_type=f32)
    gb_up = jnp.sum(grad_up.astype(f32), axis=(0, 1))
    grad_mlp = jnp.einsum("btf,df->btd", grad_up, up_full, preferred_element_type=f32)
    grad_scale_two = jnp.sum(grad_mlp * normed_two, axis=1)
    grad_shift_two = jnp.sum(grad_mlp, axis=1)
    grad_resid = grad_out + norm_back(grad_mlp * (1.0 + scale_two), normed_two, inverse_two)
    grad_gate_one = jnp.sum(grad_resid * attn_proj, axis=1)
    grad_proj = (grad_resid * gate_one).astype(bf16)
    gw_out = jnp.einsum("btd,bte->de", mixed_tokens, grad_proj, preferred_element_type=f32)
    gb_out = jnp.sum(grad_proj.astype(f32), axis=(0, 1))
    grad_mixed = jnp.einsum("bte,de->btd", grad_proj, out_full, preferred_element_type=f32).astype(
        bf16
    )
    grad_heads = grad_mixed.reshape(own_latents, tokens_all, H, HD).transpose(0, 2, 1, 3)
    grad_soft = jnp.einsum("bhqd,bhkd->bhqk", grad_heads, value_heads, preferred_element_type=f32)
    delta_sum = jnp.sum(soft_float * grad_soft, axis=-1, keepdims=True)
    grad_scores = (soft_float * (grad_soft - delta_sum)).astype(bf16)
    grad_queries = (
        jnp.einsum("bhqk,bhkd->bhqd", grad_scores, key_heads, preferred_element_type=f32)
        * scale_factor
    ).astype(bf16)
    grad_keys = (
        jnp.einsum("bhqk,bhqd->bhkd", grad_scores, queries, preferred_element_type=f32)
        * scale_factor
    ).astype(bf16)
    grad_values = jnp.einsum(
        "bhqk,bhqd->bhkd", soft_half, grad_heads, preferred_element_type=f32
    ).astype(bf16)
    grad_tokens = (
        jnp.stack([grad_queries, grad_keys, grad_values], axis=0)
        .transpose(1, 3, 0, 2, 4)
        .reshape(own_latents, tokens_all, 3 * D)
    )
    gw_qkv = jnp.einsum("btd,bte->de", attn_in, grad_tokens, preferred_element_type=f32)
    grad_tok_float = grad_tokens.astype(f32)
    gb_query = jnp.sum(grad_tok_float[:, :, :D], axis=(0, 1))
    gb_value = jnp.sum(grad_tok_float[:, :, 2 * D :], axis=(0, 1))
    grad_attn_in = jnp.einsum("bte,de->btd", grad_tokens, qkv_full, preferred_element_type=f32)
    grad_scale_one = jnp.sum(grad_attn_in * normed_one, axis=1)
    grad_shift_one = jnp.sum(grad_attn_in, axis=1)
    grad_latents = grad_resid + norm_back(grad_attn_in * (1.0 + scale_one), normed_one, inverse_one)
    grad_latents = lax.all_to_all(grad_latents, "sp", split_axis=1, concat_axis=0, tiled=True)

    grad_mod = jnp.concatenate(
        [
            grad_shift_one,
            grad_scale_one,
            grad_gate_one,
            grad_shift_two,
            grad_scale_two,
            grad_gate_two,
        ],
        axis=1,
    )
    grad_mod = lax.all_to_all(
        jnp.broadcast_to(grad_mod[None], (owners, own_latents, 6 * D)),
        ("fsdp", "sp"),
        split_axis=0,
        concat_axis=0,
        tiled=True,
    ).reshape(latent_total, 6 * D)

    rows = D // owners
    biases = (gb_query, gb_value, gb_out, gb_up, gb_down)
    bias_rows = jnp.concatenate([part.reshape(owners, -1) for part in biases], axis=1)
    bias_width = bias_rows.shape[1]
    bias_lanes = -(-bias_width // (rows * 128)) * 128
    bias_rows = jnp.pad(bias_rows, ((0, 0), (0, rows * bias_lanes - bias_width)))
    stack = down_full.shape[0] // D
    gw_down = (
        gw_down.astype(bf16)
        .reshape(owners, stack, rows, D)
        .transpose(0, 2, 1, 3)
        .reshape(D, stack * D)
    )
    packed = jnp.concatenate(
        [
            gw_down,
            gw_up.astype(bf16),
            gw_qkv.astype(bf16),
            gw_out.astype(bf16),
            bias_rows.astype(bf16).reshape(D, bias_lanes),
        ],
        axis=1,
    )
    owned = lax.psum_scatter(packed, ("fsdp", "sp"), scatter_dimension=0, tiled=True).astype(f32)
    own_weights = []
    start = 0
    for width in (stack * D, up_full.shape[1], 3 * D, D, bias_lanes):
        own_weights.append(owned[:, start : start + width])
        start = start + width
    own_down, own_up, own_qkv, own_out, bias_sums = own_weights
    own_down = own_down.reshape(rows, stack, D).transpose(1, 0, 2).reshape(stack * rows, D)
    bias_sums = bias_sums.reshape(-1)
    own_bias = []
    start = 0
    for part in biases:
        width = part.size // owners
        own_bias.append(bias_sums[start : start + width])
        start = start + width
    own_gb_query, own_gb_value, own_gb_out, own_gb_up, own_gb_down = own_bias
    silu_rows = lax.dynamic_index_in_dim(
        silu_all.reshape(latent_total, owners, D // owners), owner_index, 1, False
    )
    own_ada = jnp.dot(silu_rows.T, grad_mod, precision=lax.Precision.HIGHEST)
    own_gb_ada = lax.dynamic_index_in_dim(
        jnp.sum(grad_mod, axis=0).reshape(owners, -1), owner_index, 0, False
    )
    grad_silu = jnp.dot(grad_mod.astype(bf16), w_ada.T, preferred_element_type=f32)
    grad_silu = lax.all_to_all(
        grad_silu.reshape(fsdp_count, pair_latents * ada_rows),
        "fsdp",
        split_axis=0,
        concat_axis=0,
        tiled=True,
    )
    grad_silu = (
        grad_silu.reshape(fsdp_count, pair_latents, ada_rows)
        .transpose(1, 0, 2)
        .reshape(pair_latents, D)
    )
    grad_condition = silu_back(condition.astype(f32), grad_silu)
    return (
        output,
        grad_latents,
        grad_condition,
        own_ada,
        own_gb_ada,
        own_qkv,
        own_gb_query,
        own_gb_value,
        own_out,
        own_gb_out,
        own_up,
        own_gb_up,
        own_down,
        own_gb_down,
    )


MESH = pl.DeviceIdType.MESH


class Plan:
    def __init__(self, rows, cols):
        self.rows, self.cols = rows, cols
        self.by_rows = rows % 64 == 0
        n = (rows // 32) if self.by_rows else (cols // 256)
        unit = 16 if self.by_rows else 128
        big = -(-2 * n // 3)
        self.half = n * unit
        self.big = big * unit
        self.unit = unit
    def at(self, ref, row, h=None, q=None):
        rows, cols, unit = self.rows, self.cols, self.unit
        if h is None:
            return ref.at[pl.ds(pl.multiple_of(row, 16), rows), :]
        start = h * self.half + (self.big if q == 1 else 0)
        size = self.half if q is None else (self.big if q == 0 else self.half - self.big)
        if self.by_rows:
            return ref.at[pl.ds(pl.multiple_of(row + start, 16), size), :]
        return ref.at[pl.ds(pl.multiple_of(row, 16), rows), pl.ds(pl.multiple_of(start, 128), size)]

GELU = 0.7978845608028654


def block_kernel(F, plans, cuts, *refs):
    n = len(cuts)
    w = len(plans)
    f32, bf16 = jnp.float32, jnp.bfloat16
    ins, (cond, lat, cot, wada), vectors = refs[:w], refs[w : w + 4], refs[w + 4 : w + 10]
    outs, refs = refs[w + 10 : 2 * w + 10], refs[2 * w + 10 :]
    (
        outp_own, glat_own, own_down, own_up, own_out, own_qkv, own_bias, ada, bada, gcond,
        cond_all, bias, bias_all, part, parts, mods, vec, lat_all, cot_all, proj, mixed, attn_proj, upv, act, outp,
        acc, silu, g, r0, r1, r2, up, dn, gm, cpart, w1, w2, gu, gt, norm_one, norm_two, resid, gmod, left, halves,
        zs, zr, xs, xr, ys, yr, xds, xdr, yds, ydr, ss, sr, gloc, ges, ger, ps, pr,
        s0, q0, s1, q1, s2, q2, s3, q3, gs, gr, ks, kr, es, er, loc, wl,
    ) = refs
    f = lax.axis_index("fsdp"); x = lax.axis_index("sp")
    c = f % 2; y = (f // 2) % 2; z = f // 4; Z = F // 4; Zh = Z // 2
    owners = 2 * F
    owner = f * 2 + x
    rows = plans[0].rows
    half = rows // 2
    d_model, ff = lat_all.shape[1], act.shape[1]
    def dev(x_, y_, z_, c_):
        return ((z_ * 2 + y_) * 2 + c_, x_)
    xn, yn, sib = dev(1 - x, y, z, c), dev(x, 1 - y, z, c), dev(x, y, z, 1 - c)
    zu, zd = dev(x, y, z + 1, c), dev(x, y, z - 1, c)
    def peer(k):
        return (lax.rem(f + k, F), x)
    def other(k):
        o = lax.rem(owner + k, owners)
        return (o // 2, o % 2)
    bar = pltpu.get_barrier_semaphore()
    for k in range(1, owners):
        pl.semaphore_signal(bar, inc=1, device_id=other(k), device_id_type=MESH)
    bias[...] = jnp.zeros_like(bias)
    layout = []
    row = 0
    for ref in vectors:
        size = ref.shape[1]
        layout.append((row, size))
        for at in range(0, size, 128):
            bias[row : row + 1, 0 : min(128, size - at)] = ref[:, at : min(at + 128, size)].astype(f32)
            row += 1
    pl.semaphore_wait(bar, owners - 1)

    sends = []
    def send(ok, build):
        if ok is None:
            build().start()
        else:
            pl.when(ok)(lambda: build().start())
        sends.append((ok, build))
    def rc(src, dst, s, r, d):
        return pltpu.make_async_remote_copy(src_ref=src, dst_ref=dst, send_sem=s, recv_sem=r, device_id=d, device_id_type=MESH)

    def base(m, y_, z_, c_=c):
        return ((z_ * 2 + y_) * 2 + c_) * plans[m].rows
    def piece(m, y_, z_, h=None, q=None, c_=None):
        return plans[m].at(outs[m], base(m, y_, z_, c if c_ is None else c_), h, q)
    def mine(m, h=None, q=None):
        return plans[m].at(ins[m], 0, h, q)
    def to_sib(m, ok, kind, y_, z_, h=None, q=None, own=False):
        send(ok, lambda: rc(mine(m, h, q) if own else piece(m, y_, z_, h, q), piece(m, y_, z_, h, q),
                              ss.at[m, kind, z_], sr.at[m, kind, z_], sib))
    def arrived(m, ok, sem_s, sem_r, *where, c_=None):
        def go():
            p = piece(m, *where, c_=c_)
            rc(p, p, sem_s, sem_r, xn).wait_recv()
        if ok is None: go()
        else: pl.when(ok)(go)

    def start_own(m):
        send(None, lambda: rc(mine(m, x), piece(m, y, z, x), ys.at[m, z], yr.at[m, z], yn))
        send(z + 1 < Z, lambda: rc(mine(m, x), piece(m, y, z, x), zs.at[m, 0, z], zr.at[m, z], zu))
        send(z > 0, lambda: rc(mine(m, x), piece(m, y, z, x), zs.at[m, 1, z], zr.at[m, z], zd))
        send(z + 1 < Z, lambda: rc(mine(m, 1 - x, 0), piece(m, y, z, 1 - x, 0), zs.at[m, 2, z], zr.at[w + m, z], zu))
        send(z > 0, lambda: rc(mine(m, 1 - x, 0), piece(m, y, z, 1 - x, 0), zs.at[m, 3, z], zr.at[w + m, z], zd))
        send(None, lambda: rc(mine(m, 1 - x, 1), piece(m, y, z, 1 - x, 1), yds.at[m, z], ydr.at[m, z], yn))
        to_sib(m, None, 0, y, z, own=True)
        pltpu.make_async_copy(mine(m), piece(m, y, z), gloc.at[m]).start()

    def z_round(m, d):
        for sign in (-1, 1):
            o = z + sign * d
            ok = (o >= 0) if sign < 0 else (o < Z)
            arrived(m, ok, zs.at[m, 0, o], zr.at[m, o], y, o, x)
            more = ok & ((z + 1 < Z) if sign < 0 else (z > 0))
            onward, way = (zu, 0) if sign < 0 else (zd, 1)
            send(more, lambda o=o, way=way, onward=onward: rc(piece(m, y, o, x), piece(m, y, o, x), zs.at[m, way, o], zr.at[m, o], onward))
            send(ok, lambda o=o: rc(piece(m, y, o, x, 1), piece(m, y, o, x, 1), xs.at[m, o], xr.at[m, o], xn))
            send(ok, lambda o=o: rc(piece(m, y, o, x), piece(m, y, o, x), ys.at[m, o], yr.at[m, o], yn))
            to_sib(m, ok, 0, y, o, x)
            arrived(m, ok, zs.at[m, 2, o], zr.at[w + m, o], y, o, 1 - x, 0)
            send(more, lambda o=o, way=way, onward=onward: rc(piece(m, y, o, 1 - x, 0), piece(m, y, o, 1 - x, 0), zs.at[m, 2 + way, o], zr.at[w + m, o], onward))
            to_sib(m, ok, 5, y, o, 1 - x, 0)

    def xy_round(m, d):
        for sign in ((-1, 1) if d else (0,)):
            o = z + sign * d
            ok = None if d == 0 else ((o >= 0) if sign < 0 else (o < Z))
            arrived(m, ok, ys.at[m, o], yr.at[m, o], 1 - y, o, x)
            send(ok, lambda o=o: rc(piece(m, 1 - y, o, x, 0), piece(m, 1 - y, o, x, 0), xds.at[m, o], xdr.at[m, o], xn))
            to_sib(m, ok, 2, 1 - y, o, x)
            if d:
                arrived(m, ok, xs.at[m, o], xr.at[m, o], y, o, 1 - x, 1)
                send(ok, lambda o=o: rc(piece(m, y, o, 1 - x, 1), piece(m, y, o, 1 - x, 1), yds.at[m, o], ydr.at[m, o], yn))
                to_sib(m, ok, 1, y, o, 1 - x, 1)

    def last_round(m, d):
        for sign in ((-1, 1) if d else (0,)):
            o = z + sign * d
            ok = None if d == 0 else ((o >= 0) if sign < 0 else (o < Z))
            arrived(m, ok, xds.at[m, o], xdr.at[m, o], 1 - y, o, 1 - x, 0)
            to_sib(m, ok, 3, 1 - y, o, 1 - x, 0)
            arrived(m, ok, yds.at[m, o], ydr.at[m, o], 1 - y, o, 1 - x, 1)
            to_sib(m, ok, 4, 1 - y, o, 1 - x, 1)

    def landed(m):
        pltpu.make_async_copy(mine(m), piece(m, y, z), gloc.at[m]).wait()
        b = 1 - c
        arrived(m, None, ss.at[m, 0, z], sr.at[m, 0, z], y, z, c_=b)
        for d in range(Z):
            for sign in ((-1, 1) if d else (0,)):
                o = z + sign * d
                ok = None if d == 0 else ((o >= 0) if sign < 0 else (o < Z))
                if d:
                    arrived(m, ok, ss.at[m, 0, o], sr.at[m, 0, o], y, o, x, c_=b)
                    arrived(m, ok, ss.at[m, 1, o], sr.at[m, 1, o], y, o, 1 - x, 1, c_=b)
                    arrived(m, ok, ss.at[m, 5, o], sr.at[m, 5, o], y, o, 1 - x, 0, c_=b)
                arrived(m, ok, ss.at[m, 2, o], sr.at[m, 2, o], 1 - y, o, x, c_=b)
                arrived(m, ok, ss.at[m, 3, o], sr.at[m, 3, o], 1 - y, o, 1 - x, 0, c_=b)
                arrived(m, ok, ss.at[m, 4, o], sr.at[m, 4, o], 1 - y, o, 1 - x, 1, c_=b)

    def col(k):
        return pl.ds(*cuts[k])
    def c0(k):
        return rc(g.at[:, :, :, 1 - c, :, :, col(k)], r0.at[:, :, :, :, :, col(k)], s0.at[k], q0.at[k], sib)
    def c1(k, p):
        if p == 0:
            return rc(r0.at[:, 0, :, 1 - x, :, col(k)], r1.at[:, 0, :, :, col(k)], s1.at[k, 0], q1.at[k, 0], xn)
        return rc(r0.at[:, 1, 1 - y, :, :, col(k)], r1.at[:, 1, :, :, col(k)], s1.at[k, 1], q1.at[k, 1], yn)
    def c2(k, p):
        if p == 0:
            return rc(r1.at[:, 0, 1 - y, :, col(k)], r2.at[:, 0, :, col(k)], s2.at[k, 0], q2.at[k, 0], yn)
        return rc(r1.at[:, 1, 1 - x, :, col(k)], r2.at[:, 1, :, col(k)], s2.at[k, 1], q2.at[k, 1], xn)
    def c3(k, o, way, edge):
        buf = dn if way else up
        src = r2.at[o // 2, o % 2, :, col(k)] if edge else buf.at[o, :, col(k)]
        return rc(src, buf.at[o, :, col(k)], s3.at[k, way, o], q3.at[k, way, o], zd if way else zu)

    def stage0(k):
        c0(k).start()
    def stage1(k):
        c0(k).wait_recv()
        for p in (0, 1):
            for zh in range(Zh):
                for j in range(2):
                    at = (zh, 0, j, 1 - x) if p == 0 else (zh, 1, 1 - y, j)
                    own = g[at[0], at[1], at[2], c, at[3], :, col(k)].astype(f32)
                    r0[(*at, slice(None), col(k))] = (r0[(*at, slice(None), col(k))].astype(f32) + own).astype(bf16)
            c1(k, p).start()
    def pair(k, at):
        return g[at[0], at[1], at[2], c, at[3], :, col(k)].astype(f32) + r0[(*at, slice(None), col(k))].astype(f32)
    def stage2(k):
        for p in (0, 1):
            c1(k, p).wait_recv()
            j = (1 - y) if p == 0 else (1 - x)
            for zh in range(Zh):
                at = (zh, 0, j, x) if p == 0 else (zh, 1, y, j)
                r1[zh, p, j, :, col(k)] = (r1[zh, p, j, :, col(k)].astype(f32) + pair(k, at)).astype(bf16)
            c2(k, p).start()
    def stage3(k):
        for p in (0, 1):
            c2(k, p).wait_recv()
            j = y if p == 0 else x
            for zh in range(Zh):
                mine = r1[zh, p, j, :, col(k)].astype(f32) + pair(k, (zh, p, y, x))
                r2[zh, p, :, col(k)] = (r2[zh, p, :, col(k)].astype(f32) + mine).astype(bf16)
        @pl.when(z == 0)
        def _():
            for o in reversed(range(1, Z)): c3(k, o, 0, True).start()
        @pl.when(z == Z - 1)
        def _():
            for o in range(Z - 1): c3(k, o, 1, True).start()
    def hop(k, h):
        def go(way):
            for o in (reversed(range(h + 1, Z)) if way == 0 else range(Z - 1 - h)):
                buf = dn if way else up
                c3(k, o, way, False).wait_recv()
                buf[o, :, col(k)] = (buf[o, :, col(k)].astype(f32) + r2[o // 2, o % 2, :, col(k)].astype(f32)).astype(bf16)
                c3(k, o, way, False).start()
        pl.when(z == h)(lambda: go(0))
        pl.when(z == Z - 1 - h)(lambda: go(1))
    def final(k):
        acc[:, col(k)] = r2[z // 2, z % 2, :, col(k)].astype(f32)
        @pl.when(z > 0)
        def _():
            c3(k, z, 0, False).wait_recv()
            acc[:, col(k)] += up[z, :, col(k)].astype(f32)
        @pl.when(z < Z - 1)
        def _():
            c3(k, z, 1, False).wait_recv()
            acc[:, col(k)] += dn[z, :, col(k)].astype(f32)
        at, size = cuts[k]
        if k < 2:
            own_down[k * rows : (k + 1) * rows, :] = acc[:, at : at + size]
            return
        ref, begin = ((own_up, 2), (own_up, 2), (own_out, 4), (own_qkv, 5), (own_qkv, 5))[k - 2]
        off = at - cuts[begin][0]
        if k == 6:
            size -= 128
            own_bias[...] = acc[0:8, at + size : at + size + 128]
        wide = ref.shape[1] // 2
        ref[:, off : off + size] = acc[0 : rows // 2, at : at + size]
        ref[:, wide + off : wide + off + size] = acc[rows // 2 : rows, at : at + size]
    def drain(k):
        c0(k).wait_send()
        for p in (0, 1):
            c1(k, p).wait_send(); c2(k, p).wait_send()
        for o in range(Z):
            pl.when(o > z)(lambda o=o: c3(k, o, 0, False).wait_send())
            pl.when(o < z)(lambda o=o: c3(k, o, 1, False).wait_send())

    tokens = outp_own.shape[1]
    def swap(i, a, b):
        return rc(a.at[pl.ds(pl.multiple_of((1 - x) * tokens, 128), tokens), :], b.at[x], es.at[i], er.at[i], xn)
    def keep(i, a, b):
        return pltpu.make_async_copy(a.at[pl.ds(pl.multiple_of(x * tokens, 128), tokens), :], b.at[x], loc.at[i])
    pairs = ((outp, outp_own), (resid, glat_own))
    away = pl.ds(pl.multiple_of((1 - x) * tokens, 128), tokens)
    def swap_grad():
        return rc(halves.at[0], halves.at[1], es.at[1], er.at[1], xn)
    def hand_over(i):
        if i == 1:
            halves[0] = resid[away, :].astype(bf16)
            swap_grad().start()
            keep(1, *pairs[1]).start()
            return
        swap(i, *pairs[i]).start()
        keep(i, *pairs[i]).start()
    def conditioning():
        for k in range(1, 2 * F):
            rc(gmod, gm.at[lax.rem(owner + 2 * F - k, 2 * F)], gs.at[k], gr.at[k], xn).wait_recv()
        rows = wada.shape[0]
        step = wada.shape[1] // 6
        total = jnp.zeros((2 * F, rows), f32)
        for i in range(F):
            for j in range(2):
                silu[2 * i + j : 2 * i + j + 1, :] = cond_all[i, j : j + 1, :]
        sl = silu[...]
        sl = (sl / (1.0 + jnp.exp(-sl))).T
        sl = jnp.where(x == 0, sl[0 : rows // 2], sl[rows // 2 : rows])
        for j in range(6):
            span = pl.ds(j * step, step)
            block = gm[:, j, :]
            ada[:, span] = jnp.dot(sl, block, precision=lax.Precision.HIGHEST, preferred_element_type=f32)
            bada[:, span] = jnp.sum(block, axis=0, keepdims=True)
            total += lax.dot_general(block.astype(bf16), wada[:, span], (((1,), (1,)), ((), ())), preferred_element_type=f32)
        for i in range(F):
            cpart[i, 0:2, 0:rows] = total[2 * i : 2 * i + 2, :]
        for k in range(1, F):
            rc(cpart.at[peer(k)[0]], gcond.at[f], ks.at[k], kr.at[k], peer(k)).start()
        gcond[f] = cpart[f]
    def finish():
        for k in range(1, F):
            rc(cpart.at[0], gcond.at[lax.rem(f + F - k, F)], ks.at[k], kr.at[k], xn).wait_recv()
            rc(cpart.at[peer(k)[0]], gcond.at[f], ks.at[k], kr.at[k], peer(k)).wait_send()
        for k in range(1, 2 * F):
            rc(gmod, gm.at[owner], gs.at[k], gr.at[k], other(k)).wait_send()
        keep(1, *pairs[1]).wait()
        swap_grad().wait()
        resid[away, :] = halves[1].astype(f32)
        rest = pltpu.make_async_copy(resid.at[away, :], glat_own.at[1 - x], loc.at[1])
        rest.start()
        rest.wait()
        for i, (a, b) in enumerate(pairs[:1]):
            keep(i, a, b).wait()
            swap(i, a, b).wait_send()
            rc(b.at[1 - x], b.at[1 - x], es.at[i], er.at[i], xn).wait_recv()
    def slot(o):
        zo = o // 8
        return (zo // 2, zo % 2, (o // 4) % 2, (o // 2) % 2, o % 2)
    def norm(v):
        v = v - jnp.mean(v, axis=-1, keepdims=True)
        inv = lax.rsqrt(jnp.mean(v * v, axis=-1, keepdims=True) + eps)
        return v * inv, inv
    def norm_grad(gv, nv, inv):
        return inv * (gv - jnp.mean(gv, axis=-1, keepdims=True) - nv * jnp.mean(gv * nv, axis=-1, keepdims=True))
    def tdot(p, q):
        return lax.dot_general(p, q, (((0,), (0,)), ((), ())), preferred_element_type=f32)
    def dott(p, q):
        return lax.dot_general(p, q, (((1,), (1,)), ((), ())), preferred_element_type=f32)
    def mod(i):
        return mods[i : i + 1, :]
    def fold(col0, right, span, first):
        step = 256 if span % 256 == 0 else 128
        def one(i, carry):
            off = first + i * step
            lo = jnp.dot(left[...], right[:, pl.ds(pl.multiple_of(off, 128), step)], preferred_element_type=f32)
            hi_at = right.shape[1] // 2 + off
            hi = jnp.dot(left[...], right[:, pl.ds(pl.multiple_of(hi_at, 128), step)], preferred_element_type=f32)
            to = pl.ds(pl.multiple_of(col0 + off, 128), step)
            for o in range(owners):
                both = jnp.concatenate([lo[o * half : o * half + half], hi[o * half : o * half + half]], axis=0)
                g[(*slot(o), slice(None), to)] = both.astype(bf16)
            return carry
        lax.fori_loop(0, span // step, one, 0)
    def owner_sums(total):
        wide = total.shape[1]
        per = wide // owners
        cols = lax.broadcasted_iota(jnp.int32, (owners, wide), 1)
        begin = lax.broadcasted_iota(jnp.int32, (owners, wide), 0) * per
        mine_ = (cols >= begin) & (cols < begin + per)
        spread = jnp.where(mine_, jnp.broadcast_to(total, (owners, wide)), 0.0).astype(bf16)
        line = lax.broadcasted_iota(jnp.int32, (1, wide), 1)
        pick = jnp.broadcast_to(line - line // per * per, (128, wide)) == lax.broadcasted_iota(jnp.int32, (128, wide), 0)
        return dott(spread, jnp.where(pick, 1.0, 0.0).astype(bf16))

    stages = [stage1, stage2, stage3] + [functools.partial(lambda k, h: hop(k, h), h=h) for h in range(1, Z - 1)] + [final]
    def advance(t):
        for i, st in enumerate(stages):
            if 0 <= t - i < n: st(t - i)
    def rowsum(v):
        return jnp.sum(v.astype(f32), axis=0, keepdims=True)

    def load(i):
        if i == 0:
            pair = (outs[3], w1)
        elif i == 1:
            pair = (outs[2], w2)
        elif i < 5:
            pair = (outs[0].at[:, pl.ds(d_model * (i - 2), d_model)], w1.at[pl.ds(d_model * (i - 2), d_model), :])
        else:
            pair = (outs[1], w1.at[pl.ds(3 * d_model, d_model), :])
        return pltpu.make_async_copy(*pair, wl.at[i])
    own_tokens = lat.shape[1]
    for k in range(1, F):
        to = peer(k)
        rc(cond.at[to[0]], cond_all.at[f], ges.at[0, k], ger.at[0, k], to).start()
        rc(bias, bias_all.at[f], ges.at[1, k], ger.at[1, k], to).start()
    def trade(i, a, b):
        return rc(a.at[1 - x], b.at[pl.ds(pl.multiple_of(x * own_tokens, 128), own_tokens), :], ges.at[2, i], ger.at[2, i], xn)
    def stay(i, a, b):
        return pltpu.make_async_copy(a.at[x], b.at[pl.ds(pl.multiple_of(x * own_tokens, 128), own_tokens), :], gloc.at[w + i])
    given = ((lat, lat_all), (cot, cot_all))
    for i, (a, b) in enumerate(given):
        trade(i, a, b).start()
        stay(i, a, b).start()
    def comm(ms, d):
        for m in ms:
            if 0 < d < Z: z_round(m, d)
            if 0 < d <= Z: xy_round(m, d - 1)
            if d > 1: last_round(m, d - 2)
    def assemble(which, lo, hi):
        row, size = layout[which]
        cols = lax.broadcasted_iota(jnp.int32, (1, hi - lo), 1) + lo
        block = cols // size
        place = jnp.broadcast_to(cols - block * size, (128, hi - lo)) - lax.broadcasted_iota(jnp.int32, (128, hi - lo), 0)
        total = None
        for i in range(-(-size // 128)):
            hot = jnp.where(place == i * 128, 1.0, 0.0).astype(bf16)
            term = jnp.dot(bias_all[:, row + i, :].astype(bf16), hot, preferred_element_type=f32)
            total = term if total is None else total + term
        mine_ = jnp.broadcast_to(block, (F, hi - lo)) == lax.broadcasted_iota(jnp.int32, (F, hi - lo), 0)
        return jnp.sum(jnp.where(mine_, total, 0.0), axis=0, keepdims=True)
    start_own(0)
    start_own(1)
    start_own(2)
    start_own(3)
    comm((0, 1), 1)
    cond_all[f] = cond[f]
    bias_all[f] = bias[...]
    for k in range(1, F):
        rc(cond.at[0], cond_all.at[lax.rem(f + F - k, F)], ges.at[0, k], ger.at[0, k], xn).wait_recv()
    picked = jnp.where(x == 0, cond_all[:, 0, :], cond_all[:, 1, :])[:, :rows]
    picked = (picked / (1.0 + jnp.exp(-picked))).astype(bf16)
    made = jnp.dot(picked, wada[...], preferred_element_type=f32)
    for i in range(F):
        part[i] = made[i : i + 1, :]
    for k in range(1, F):
        to = peer(k)
        rc(part.at[to[0]], parts.at[f], ps.at[k], pr.at[k], to).start()
    parts[f] = part[f]
    comm((2,), 1)
    comm((0, 1), 2)
    for k in range(1, F):
        rc(bias, bias_all.at[lax.rem(f + F - k, F)], ges.at[1, k], ger.at[1, k], xn).wait_recv()
        rc(part.at[0], parts.at[lax.rem(f + F - k, F)], ps.at[k], pr.at[k], xn).wait_recv()
    for i in range(6):
        span = slice(i * d_model, (i + 1) * d_model)
        mods[i : i + 1, :] = jnp.sum(parts[:, :, span], axis=0) + assemble(5, i * d_model, (i + 1) * d_model)
    comm((3,), 1)
    places = {}
    at = 0
    for which in (0, 1, 2, 3, 4):
        size = layout[which][1] * F
        places[which] = slice(at, at + size)
        for lo in range(0, size, d_model):
            vec[:, at + lo : at + lo + d_model] = assemble(which, lo, lo + d_model)
        at += size
    def bias_of(which):
        return vec[:, places[which]]
    comm((0, 1), 3)
    for i, (a, b) in enumerate(given):
        stay(i, a, b).wait()
        got = b.at[pl.ds(pl.multiple_of((1 - x) * own_tokens, 128), own_tokens), :]
        rc(got, got, ges.at[2, i], ger.at[2, i], xn).wait_recv()
    comm((2,), 2)
    comm((0, 1), 4)
    v, inv_one = norm(lat_all[...].astype(f32))
    norm_one[...] = v
    gt[:, 0:d_model] = (v * (1.0 + mod(1)) + mod(0)).astype(bf16)
    comm((3,), 2)
    comm((0, 1), 5)
    comm((2,), 3)
    for m in (0, 1): landed(m)
    for i in range(2, 6): load(i).start()
    comm((2,), 4)
    for i in range(2, 6): load(i).wait()
    for j in range(3):
        made = jnp.dot(gt[:, 0:d_model], w1[j * d_model : (j + 1) * d_model, :], preferred_element_type=f32)
        if j != 1:
            made = made + bias_of(0 if j == 0 else 1)
        proj[:, j * d_model : (j + 1) * d_model] = made.astype(bf16)
    scale = HD ** (-0.5)
    lanes = lax.broadcasted_iota(jnp.int32, (1, 2 * HD), 1)
    comm((3,), 3)
    def attend(i, carry):
        at = pl.multiple_of(i * 2 * HD, 128)
        qp = proj[:, pl.ds(at, 2 * HD)]
        kp = proj[:, pl.ds(pl.multiple_of(d_model + i * 2 * HD, 128), 2 * HD)]
        vp = proj[:, pl.ds(pl.multiple_of(2 * d_model + i * 2 * HD, 128), 2 * HD)]
        total = None
        for j in range(2):
            own = (lanes // HD) == j
            q_j, v_j = (jnp.where(own, m_, jnp.zeros_like(m_)) for m_ in (qp, vp))
            e = jnp.exp(dott(q_j, kp) * scale)
            soft = e * (1.0 / jnp.sum(e, axis=-1, keepdims=True))
            term = jnp.dot(soft.astype(bf16), v_j, preferred_element_type=f32)
            total = term if total is None else total + term
        mixed[:, pl.ds(at, 2 * HD)] = total.astype(bf16)
        return carry
    pairs_of = d_model // (2 * HD)
    lax.fori_loop(0, pairs_of // 2, attend, 0)
    comm((2,), 5)
    lax.fori_loop(pairs_of // 2, pairs_of, attend, 0)
    comm((3,), 4)
    attn_proj[...] = jnp.dot(mixed[...], w1[3 * d_model : 4 * d_model, :], preferred_element_type=f32) + bias_of(2)
    resid[...] = lat_all[...].astype(f32) + mod(2) * attn_proj[...]
    n2, inv_two = norm(resid[...])
    norm_two[...] = n2
    n2 = n2 * (1.0 + mod(4)) + mod(3)
    gt[:, 0:d_model] = n2.astype(bf16)
    left[...] = n2.T.astype(bf16)
    landed(2)
    load(1).start()
    load(1).wait()
    step = 512
    for i in range(ff // step):
        span = slice(i * step, (i + 1) * step)
        at = places[4].start + i * step
        u = jnp.dot(gt[:, 0:d_model], w2[:, span], preferred_element_type=f32) + vec[:, at : at + step]
        th = jnp.tanh(GELU * (u + 0.044715 * (u * u * u)))
        act[:, span] = (0.5 * u * (1.0 + th)).astype(bf16)
        upv[:, span] = 0.5 * (1.0 + th) + 0.5 * u * (1.0 - th * th) * (GELU * (1.0 + 3.0 * 0.044715 * (u * u)))
    comm((3,), 5)
    landed(3)
    load(0).start()
    load(0).wait()
    down = jnp.dot(act[...], w1[...], preferred_element_type=f32) + bias_of(3)
    outp[...] = (resid[...] + mod(5) * down).astype(bf16)
    hand_over(0)
    gmod[5:6, :] = rowsum(cot_all[...].astype(f32) * down)
    cpart[...] = jnp.zeros_like(cpart)

    cotf = cot_all[...].astype(f32)
    gdown = (cotf * mod(5)).astype(bf16)
    sums_down = owner_sums(rowsum(gdown))
    group = owners // 4
    wide = ff // 4
    for i in range(4):
        made = tdot(act[:, i * wide : (i + 1) * wide], gdown)
        for j in range(group):
            o = i * group + j
            for b in range(2):
                at = j * 2 * rows + b * rows
                g[(*slot(o), slice(None), slice(b * d_model, (b + 1) * d_model))] = made[at : at + rows].astype(bf16)
    stage0(0)
    stage0(1)
    step = 512
    for i in range(ff // step):
        span = slice(i * step, (i + 1) * step)
        gu[:, span] = (dott(gdown, w1[span, :]) * upv[:, span]).astype(bf16)
    for i in range(4): load(2 + i).start()
    advance(0)
    colbase = 2 * d_model
    fold(colbase, gu, ff // 4, 0)
    stage0(2)
    advance(1)
    fold(colbase, gu, ff // 4, ff // 4)
    stage0(3)
    sums_up = owner_sums(rowsum(gu[...]))
    gmlp = dott(gu[...], w2[...])
    gmod[4:5, :] = rowsum(gmlp * norm_two[...])
    gmod[3:4, :] = rowsum(gmlp)
    gres = cot_all[...].astype(f32) + norm_grad(gmlp * (1.0 + mod(4)), norm_two[...], inv_two)
    resid[...] = gres
    gmod[2:3, :] = rowsum(gres * attn_proj[...])
    gproj = (gres * mod(2)).astype(bf16)
    sums_out = owner_sums(rowsum(gproj))
    advance(2)
    left[...] = mixed[...].astype(f32).T.astype(bf16)
    gu[:, 0:d_model] = gproj
    colbase += ff // 2
    fold(colbase, gu.at[:, 0:d_model], d_model // 2, 0)
    stage0(4)
    for i in range(4): load(2 + i).wait()
    gmix = dott(gproj, w1[3 * d_model : 4 * d_model, :]).astype(bf16)
    gu[:, d_model : 2 * d_model] = gmix
    def heads(i, carry):
        at = pl.multiple_of(i * 2 * HD, 128)
        qp = proj[:, pl.ds(at, 2 * HD)]
        kp = proj[:, pl.ds(pl.multiple_of(d_model + i * 2 * HD, 128), 2 * HD)]
        vp = proj[:, pl.ds(pl.multiple_of(2 * d_model + i * 2 * HD, 128), 2 * HD)]
        gp = gu[:, pl.ds(pl.multiple_of(d_model + i * 2 * HD, 128), 2 * HD)]
        dq = dk = dv = None
        for j in range(2):
            own = (lanes // HD) == j
            q_j, k_j, g_j = (jnp.where(own, m, jnp.zeros_like(m)) for m in (qp, kp, gp))
            e = jnp.exp(dott(q_j, kp) * scale)
            soft = e * (1.0 / jnp.sum(e, axis=-1, keepdims=True))
            gs_ = dott(g_j, vp)
            delta = jnp.sum(soft * gs_, axis=-1, keepdims=True)
            ds_ = (soft * (gs_ - delta)).astype(bf16)
            a = jnp.dot(ds_, k_j, preferred_element_type=f32)
            b = tdot(ds_, q_j)
            c_ = tdot(soft.astype(bf16), g_j)
            dq, dk, dv = (a, b, c_) if dq is None else (dq + a, dk + b, dv + c_)
        gt[:, pl.ds(at, 2 * HD)] = (dq * scale).astype(bf16)
        gt[:, pl.ds(pl.multiple_of(d_model + i * 2 * HD, 128), 2 * HD)] = (dk * scale).astype(bf16)
        gt[:, pl.ds(pl.multiple_of(2 * d_model + i * 2 * HD, 128), 2 * HD)] = dv.astype(bf16)
        return carry
    lax.fori_loop(0, d_model // (2 * HD), heads, 0)
    advance(3)
    left[...] = (norm_one[...] * (1.0 + mod(1)) + mod(0)).T.astype(bf16)
    colbase += d_model // 2
    first = cuts[5][1]
    fold(colbase, gt, first, 0)
    stage0(5)
    advance(4)
    fold(colbase, gt, 3 * d_model // 2 - first, first)
    tail_at = pl.ds(colbase + 3 * d_model // 2, 128)
    sums = (
        owner_sums(rowsum(gt[:, 0:d_model])), owner_sums(rowsum(gt[:, 2 * d_model : 3 * d_model])),
        sums_out, sums_down, sums_up,
    )
    fill = jnp.zeros((rows - len(sums), 128), f32)
    for o in range(owners):
        g[(*slot(o), slice(None), tail_at)] = jnp.concatenate([m[o : o + 1] for m in sums] + [fill], axis=0).astype(bf16)
    stage0(6)
    advance(5)
    gain = None
    for j in range(3):
        share = dott(gt[:, j * d_model : (j + 1) * d_model], w1[j * d_model : (j + 1) * d_model, :])
        gain = share if gain is None else gain + share
    gmod[1:2, :] = rowsum(gain * norm_one[...])
    gmod[0:1, :] = rowsum(gain)
    gmod[6:8, :] = jnp.zeros((2, d_model), f32)
    resid[...] += norm_grad(gain * (1.0 + mod(1)), norm_one[...], inv_one)
    hand_over(1)
    for k in range(1, owners):
        rc(gmod, gm.at[owner], gs.at[k], gr.at[k], other(k)).start()
    gm[owner] = gmod[...]
    advance(6)
    advance(7)
    conditioning()
    for t in range(8, n + len(stages) - 1):
        advance(t)
    for k in range(n): drain(k)
    finish()
    for k in range(1, F):
        to = peer(k)
        rc(cond.at[to[0]], cond_all.at[f], ges.at[0, k], ger.at[0, k], to).wait_send()
        rc(bias, bias_all.at[f], ges.at[1, k], ger.at[1, k], to).wait_send()
        rc(part.at[to[0]], parts.at[f], ps.at[k], pr.at[k], to).wait_send()
    for i, (a, b) in enumerate(given):
        trade(i, a, b).wait_send()
    for ok, build in sends:
        if ok is None: build().wait_send()
        else: pl.when(ok)(lambda build=build: build().wait_send())


def block(shards, cond, lat, cot, wada, vectors, F):
    plans = [Plan(*s.shape) for s in shards]
    w = len(plans)
    d_model, ff = shards[3].shape[1], shards[2].shape[1]
    owners = 2 * F
    rows = wada.shape[0]
    Z = F // 4
    Zh = Z // 2
    q_half = 3 * d_model // 2
    first = 256 * -(-q_half // 512)
    cuts = []
    for size in (d_model, d_model, ff // 4, ff // 4, d_model // 2, first, q_half - first + 128):
        cuts.append((sum(c[1] for c in cuts), size))
    n = len(cuts)
    width = sum(c[1] for c in cuts)
    tokens = 2 * lat.shape[1]
    S = pltpu.SemaphoreType.DMA
    f32, bf16 = jnp.float32, jnp.bfloat16
    hbm, vm = pl.BlockSpec(memory_space=pl.ANY), pl.BlockSpec(memory_space=pltpu.VMEM)
    like = jax.ShapeDtypeStruct
    mods = 6 * d_model
    return pl.pallas_call(
        functools.partial(block_kernel, F, plans, cuts),
        out_shape=[like((s.shape[0] * F, s.shape[1]), bf16) for s in shards]
        + [
            like(lat.shape, bf16),
            like(lat.shape, f32),
            like((2 * rows, d_model), f32),
            like((rows // 2, ff), f32),
            like((rows // 2, d_model), f32),
            like((rows // 2, 3 * d_model), f32),
            like((8, 128), f32),
            like((rows // 2, mods), f32),
            like((1, mods), f32),
            like((F, 8, 128), f32),
        ],
        in_specs=[hbm] * w + [vm, hbm, hbm, vm] + [vm] * 6,
        out_specs=[hbm] * w + [hbm, hbm] + [vm] * 8,
        scratch_shapes=[
            pltpu.VMEM((F, 8, 128), f32),
            pltpu.VMEM((16, 128), f32),
            pltpu.VMEM((F, 16, 128), f32),
            pltpu.VMEM((F, 1, mods), f32),
            pltpu.VMEM((F, 1, mods), f32),
            pltpu.VMEM((8, d_model), f32),
            pltpu.VMEM((1, 4 * d_model + ff), f32),
            pltpu.VMEM((tokens, d_model), bf16),
            pltpu.VMEM((tokens, d_model), bf16),
            pltpu.VMEM((tokens, 3 * d_model), bf16),
            pltpu.VMEM((tokens, d_model), bf16),
            pltpu.VMEM((tokens, d_model), f32),
            pltpu.VMEM((tokens, ff), f32),
            pltpu.VMEM((tokens, ff), bf16),
            pltpu.VMEM((tokens, d_model), bf16),
            pltpu.VMEM((rows, width), f32),
            pltpu.VMEM((owners, 128), f32),
            pltpu.VMEM((Zh, 2, 2, 2, 2, rows, width), bf16),
            pltpu.VMEM((Zh, 2, 2, 2, rows, width), bf16),
            pltpu.VMEM((Zh, 2, 2, rows, width), bf16),
            pltpu.VMEM((Zh, 2, rows, width), bf16),
            pltpu.VMEM((Z, rows, width), bf16),
            pltpu.VMEM((Z, rows, width), bf16),
            pltpu.VMEM((owners, 8, d_model), f32),
            pltpu.VMEM((F, 8, 128), f32),
            pltpu.VMEM((ff, d_model), bf16),
            pltpu.VMEM((d_model, ff), bf16),
            pltpu.VMEM((tokens, ff), bf16),
            pltpu.VMEM((tokens, 3 * d_model), bf16),
            pltpu.VMEM((tokens, d_model), f32),
            pltpu.VMEM((tokens, d_model), f32),
            pltpu.VMEM((tokens, d_model), f32),
            pltpu.VMEM((8, d_model), f32),
            pltpu.VMEM((d_model, tokens), bf16),
            pltpu.VMEM((2, tokens // 2, d_model), bf16),
            S((w, 4, Z)), S((2 * w, Z)), *[S((w, Z))] * 8, S((w, 6, Z)), S((w, 6, Z)), S((w + 2,)), S((3, F)), S((3, F)), S((F,)), S((F,)),
            S((n,)), S((n,)), S((n, 2)), S((n, 2)), S((n, 2)), S((n, 2)), S((n, 2, Z)), S((n, 2, Z)),
            S((owners,)), S((owners,)), S((F,)), S((F,)), S((2,)), S((2,)), S((2,)), S((6,)),
        ],
        compiler_params=pltpu.CompilerParams(
            collective_id=0, has_side_effects=True, vmem_limit_bytes=63 * 2**20
        ),
        name="block_forward_backward",
    )(*shards, cond, lat, cot, wada, *vectors)[w:]


def deliver(*arrays):
    count = len(arrays)

    def kernel(*refs):
        ins, outs, kept, sem = refs[:count], refs[count : 2 * count], refs[2 * count : -1], refs[-1]
        reads = [pltpu.make_async_copy(ins[i], kept[i], sem.at[0, i]) for i in range(count)]
        writes = [pltpu.make_async_copy(kept[i], outs[i], sem.at[1, i]) for i in range(count)]
        for copy in reads:
            copy.start()
        for i in range(count):
            reads[i].wait()
            writes[i].start()
        for copy in writes:
            copy.wait()

    hbm = pl.BlockSpec(memory_space=pl.ANY)
    return pl.pallas_call(
        kernel,
        out_shape=[jax.ShapeDtypeStruct(a.shape, a.dtype) for a in arrays],
        in_specs=[hbm] * count,
        out_specs=[hbm] * count,
        scratch_shapes=[pltpu.VMEM(a.shape, a.dtype) for a in arrays] + [pltpu.SemaphoreType.DMA((2, count))],
        compiler_params=pltpu.CompilerParams(vmem_limit_bytes=63 * 2**20),
        name="deliver",
    )(*arrays)


def body_fast(
    latents,
    condition,
    cotangent,
    w_ada,
    b_ada,
    w_qkv,
    b_query,
    b_value,
    w_out,
    b_out,
    w_up,
    b_up,
    w_down,
    b_down,
):
    f32 = jnp.float32
    F = lax.axis_size("fsdp")
    owners = F * lax.axis_size("sp")
    sp_index = lax.axis_index("sp")
    rows = w_qkv.shape[0]
    cond = jnp.pad(
        condition.astype(f32).reshape(2, F, rows).transpose(1, 0, 2), ((0, 0), (0, 6), (0, 128 - rows))
    )
    vectors = [part.reshape(1, -1) for part in (b_query, b_value, b_out, b_down, b_up, b_ada)]
    output, grad_latents, own_down, own_up, own_out, own_qkv, sums, own_ada, own_bada, grad_silu = block(
        (w_qkv, w_out, w_up, w_down), cond, latents, cotangent, w_ada, vectors, F
    )
    output, grad_latents, own_down, own_up, own_out, own_qkv, own_ada = deliver(
        output, grad_latents, own_down, own_up, own_out, own_qkv, own_ada
    )
    sizes = (rows, rows, rows, rows, b_up.shape[0])
    own_gb_query, own_gb_value, own_gb_out, own_gb_down, own_gb_up = (
        sums[i, : size // 2] for i, size in enumerate(sizes)
    )
    own_gb_ada = lax.dynamic_index_in_dim(
        own_bada.reshape(owners, -1), lax.axis_index("fsdp") * 2 + sp_index, 0, False
    )
    grad_silu = grad_silu[:, :2, :rows].transpose(1, 0, 2).reshape(2, -1)
    grad_condition = silu_back(condition.astype(f32), grad_silu)
    return (
        output,
        grad_latents,
        grad_condition,
        own_ada,
        own_gb_ada,
        own_qkv,
        own_gb_query,
        own_gb_value,
        own_out,
        own_gb_out,
        own_up,
        own_gb_up,
        own_down,
        own_gb_down,
    )


def choose(*args):
    latents, w_qkv, w_down = args[0], args[5], args[12]
    fits = (
        lax.axis_size("sp") == 2
        and lax.axis_size("fsdp") % 8 == 0
        and latents.shape[0] == 2
        and latents.shape[1] % 128 == 0
        and w_qkv.shape[0] % 16 == 0
        and w_qkv.shape[0] <= 128
        and w_down.shape[0] % 64 == 0
        and w_down.shape[0] == 4 * w_qkv.shape[0]
    )
    return (body_fast if fits else body_general)(*args)


def solution(mesh):
    in_specs = (
        P("fsdp", "sp", None),
        P("fsdp", None),
        P("fsdp", "sp", None),
        P("fsdp", None),
        P("fsdp"),
        P("fsdp", None),
        P("fsdp"),
        P("fsdp"),
        P("fsdp", None),
        P("fsdp"),
        P("fsdp", None),
        P("fsdp"),
        P("fsdp", None),
        P("fsdp"),
    )
    out_specs = (
        P("fsdp", "sp", None),
        P("fsdp", "sp", None),
        P("fsdp", None),
        P(("fsdp", "sp"), None),
        P(("fsdp", "sp")),
        P(("fsdp", "sp"), None),
        P(("fsdp", "sp")),
        P(("fsdp", "sp")),
        P(("fsdp", "sp"), None),
        P(("fsdp", "sp")),
        P(("fsdp", "sp"), None),
        P(("fsdp", "sp")),
        P(("fsdp", "sp"), None),
        P(("fsdp", "sp")),
    )
    return jax.shard_map(choose, mesh=mesh, in_specs=in_specs, out_specs=out_specs, check_vma=False)
```
